32 devices in a mesh: lon: 8 (over y, x, core), lat: 2 (over z_hi), depth: 2 (over z_lo).
Axes of the slice: x: 2, y: 2, z: 4 (z_hi: 2, z_lo: 2; z = z_hi * 2 + z_lo), core: 2. Of those that a mesh axis runs over, the one named last changes fastest.
Arguments:
- adj_temp: float32 [96, 16, 1024], P('depth', 'lat', 'lon'), may hold values from -6 to 6
- adj_salt: float32 [96, 16, 1024], P('depth', 'lat', 'lon'), may hold values from -6 to 6
- adj_zonal: float32 [96, 16, 1024], P('depth', 'lat', 'lon'), may hold values from -6 to 6
- adj_merid: float32 [96, 16, 1024], P('depth', 'lat', 'lon'), may hold values from -6 to 6
- east_speed: float32 [96, 16, 1024], P('depth', 'lat', 'lon'), may hold values from -4 to 4
- north_speed: float32 [96, 16, 1024], P('depth', 'lat', 'lon'), may hold values from -4 to 4
- branch_flags: int32 [2, 96, 16, 1024], P(None, 'depth', 'lat', 'lon'), may hold values from 0 to 8
- sea_mask: int32 [96, 16, 1024], P('depth', 'lat', 'lon'), may hold values 0 or 1
- block_inverse: float32 [16, 96, 48], P('lat', 'depth'), may hold values from -1 to 1, as said below
- coupling: float32 [16], P('lat'), may hold values from 0.3 to 0.9
Outputs:
- grad_temp: float32 [96, 16, 1024], P('depth', 'lat', 'lon')
- grad_salt: float32 [96, 16, 1024], P('depth', 'lat', 'lon')
- grad_zonal: float32 [96, 16, 1024], P('depth', 'lat', 'lon')
- grad_merid: float32 [96, 16, 1024], P('depth', 'lat', 'lon')
The draws below stay inside these ranges and needn't reach their ends.
Inputs may be any that keep to these rules, and one draw needn't show every extreme that they name: `branch_flags`: a flag is 3 times the branch of the north face plus the branch of the east face. `sea_mask`: 1 marks a sea cell. `block_inverse`: the diagonal entries of every 48 x 48 block lie between 0.4 and 1, the other entries between -0.5 / 48 and 0.5 / 48.
All inputs are finite; a program needn't handle non-finite values. No bound on the sum of `sea_mask` on one device may be relied on, other than what follows from the above.
Results may differ from the reference program's by a relative error of at most 0.00016.
Values sent between devices are 32-bit elements; how exact they have to be, the bound alone decides.
No kernel may reach another device: no remote copies, remote signals or barrier semaphores. Data moves between devices by JAX's collectives and lax.ppermute only.
A program may use at most 64 MiB of HBM per device.

```python
import math
import jax
import jax.numpy as jnp
from jax import lax

LEV_DEV = 48
STEPS = 2
NX = 1024
NY = 16
LEVELS = 96


def draw_block_inverse(key, part):
    key_diag, key_off = jax.random.split(jax.random.fold_in(key, 7))
    rows_pos = jnp.arange(LEVELS)[:, None] % LEV_DEV
    cols_pos = jnp.arange(LEV_DEV)[None, :]
    on_diag = (rows_pos == cols_pos)[None]
    diagonal = jax.random.uniform(key_diag, (NY, LEVELS, LEV_DEV), jnp.float32, 0.5, 0.9)
    others = jnp.clip(jax.random.normal(key_off, (NY, LEVELS, LEV_DEV), jnp.float32), -1.6, 1.6) * (0.3 / LEV_DEV)
    return jnp.where(on_diag, diagonal, others)


def place_ends(result, stream_key, smallest, top_value):
    longest = result.shape.index(max(result.shape))
    spots = []
    for shift in (0, 1):
        where = [jax.random.randint(jax.random.fold_in(stream_key, axis), (), 0, length) for axis, length in enumerate(result.shape)]
        where[longest] = (where[longest] + shift) % result.shape[longest]
        spots.append(tuple(where))
    return result.at[spots[0]].set(smallest).at[spots[1]].set(top_value)


def levels(own_key, extent, shards, low, top_value):
    level = 1.0
    for axis_at, parts in shards:
        steps = jax.random.uniform(jax.random.fold_in(jax.random.fold_in(own_key, 6), axis_at), (parts,), jnp.float32, low / len(shards), top_value / len(shards))
        level = level * jnp.repeat(jnp.exp(steps), extent[axis_at] // parts).reshape((-1,) + (1,) * (len(extent) - 1 - axis_at))
    return level


def centred(own_key, shape, scale, bound, cuts=(), held_as=jnp.bfloat16):
    level = levels(own_key, shape, cuts, -0.22, 0.18) if cuts else 1.0
    result = jax.random.normal(own_key, shape, jnp.float32) * scale * level
    return jnp.minimum(jnp.maximum(result, -bound), bound).astype(held_as)


def setup_inputs(seed: int = 0) -> dict:
    keys = jax.random.split(jax.random.key(seed), 11)
    return {
        "adj_temp": centred(keys[0], (LEVELS, NY, NX), 1.0, 6.0, ((0, 2), (1, 2), (2, 8)), jnp.float32),
        "adj_salt": centred(keys[1], (LEVELS, NY, NX), 1.0, 6.0, ((0, 2), (1, 2), (2, 8)), jnp.float32),
        "adj_zonal": centred(keys[2], (LEVELS, NY, NX), 1.0, 6.0, ((0, 2), (1, 2), (2, 8)), jnp.float32),
        "adj_merid": centred(keys[3], (LEVELS, NY, NX), 1.0, 6.0, ((0, 2), (1, 2), (2, 8)), jnp.float32),
        "east_speed": centred(keys[4], (LEVELS, NY, NX), 1.0, 4.0, ((0, 2), (1, 2), (2, 8)), jnp.float32),
        "north_speed": centred(keys[5], (LEVELS, NY, NX), 0.7, 4.0, ((0, 2), (1, 2), (2, 8)), jnp.float32),
        "branch_flags": place_ends(jax.random.randint(keys[6], (STEPS, LEVELS, NY, NX), 0, 9), jax.random.fold_in(keys[6], 1), 0, 8).astype(jnp.int32),
        "sea_mask": place_ends((jax.random.randint(keys[7], (LEVELS, NY, NX), 0, 6) < 5).astype(jnp.int32), jax.random.fold_in(keys[7], 1), 0, 1),
        "block_inverse": draw_block_inverse(jax.random.fold_in(keys[10], 71), 0),
        "coupling": jnp.clip(jnp.exp(math.log(0.9) - 1.0986122 * jax.random.uniform(keys[9], (NY,), jnp.float32) ** levels(keys[9], (NY,), ((0, 2),), -0.2, 0.2)), 0.3, 0.9),
    }


advect_scale = 0.25
diffusion = 0.5
gravity = 0.1
pressure_scale = 1.0
viscosity = 0.1
haline = 0.8

def eastward(field):
    return jnp.roll(field, -1, axis=2)

def westward(field):
    return jnp.roll(field, 1, axis=2)

def northward(field):
    return jnp.concatenate([field[:, 1:, :], jnp.zeros_like(field[:, :1, :])], axis=1)

def southward(field):
    return jnp.concatenate([jnp.zeros_like(field[:, :1, :]), field[:, :-1, :]], axis=1)

def laplace(field):
    return eastward(field) + westward(field) + northward(field) + southward(field) - 4.0 * field

def column_solve(field, block_inverse, coupling):
    upper_block = block_inverse[:, :LEV_DEV, :]
    lower_block = block_inverse[:, LEV_DEV:, :]
    highest = lax.Precision.HIGHEST
    upper_part = jnp.einsum('yjk,kyx->jyx', upper_block, field[:LEV_DEV], precision=highest)
    lower_part = jnp.einsum('yjk,kyx->jyx', lower_block, field[LEV_DEV:], precision=highest)
    upper_corner = upper_block[:, LEV_DEV - 1, LEV_DEV - 1]
    lower_corner = lower_block[:, 0, 0]
    divisor = (1.0 - coupling * coupling * upper_corner * lower_corner)[:, None]
    first = upper_part[LEV_DEV - 1]
    second = lower_part[0]
    upper_value = (first + (coupling * upper_corner)[:, None] * second) / divisor
    lower_value = (second + (coupling * lower_corner)[:, None] * first) / divisor
    upper_part = upper_part + (coupling[:, None] * upper_block[:, :, LEV_DEV - 1]).T[:, :, None] * lower_value[None]
    lower_part = lower_part + (coupling[:, None] * lower_block[:, :, 0]).T[:, :, None] * upper_value[None]
    return jnp.concatenate([upper_part, lower_part], axis=0)

def forward_step(state, flags_now, east_speed, north_speed, sea, block_inverse, coupling):
    zonal_branch = (flags_now % 3).astype(jnp.float32) * 0.5
    merid_branch = (flags_now // 3).astype(jnp.float32) * 0.5
    east_open = sea * eastward(sea)
    north_open = sea * northward(sea)
    east_self = east_open * (east_speed * (1.0 - zonal_branch) + diffusion)
    east_next = east_open * (east_speed * zonal_branch - diffusion)
    north_self = north_open * (north_speed * (1.0 - merid_branch) + diffusion)
    north_next = north_open * (north_speed * merid_branch - diffusion)

    def tracer(field):
        flux_east = east_self * field + east_next * eastward(field)
        flux_north = north_self * field + north_next * northward(field)
        return sea * (field - advect_scale * (flux_east - westward(flux_east) + flux_north - southward(flux_north)))
    temp, salt, zonal, merid = state
    pressure = gravity * jnp.cumsum(temp - haline * salt, axis=0)
    coriolis = (0.2 + 0.6 * (jnp.arange(NY).astype(jnp.float32) + 0.5) / NY)[None, :, None]
    zonal_star = sea * (zonal + coriolis * merid - 0.5 * pressure_scale * (eastward(pressure) - westward(pressure)) + viscosity * laplace(zonal))
    merid_star = sea * (merid - coriolis * zonal - 0.5 * pressure_scale * (northward(pressure) - southward(pressure)) + viscosity * laplace(merid))
    return (column_solve(tracer(temp), block_inverse, coupling), column_solve(tracer(salt), block_inverse, coupling), column_solve(zonal_star, block_inverse, coupling), column_solve(merid_star, block_inverse, coupling))

def reference(adj_temp, adj_salt, adj_zonal, adj_merid, east_speed, north_speed, branch_flags, sea_mask, block_inverse, coupling):
    sea = sea_mask.astype(jnp.float32)
    state = (adj_temp, adj_salt, adj_zonal, adj_merid)
    zeros = (jnp.zeros_like(adj_temp), jnp.zeros_like(adj_temp), jnp.zeros_like(adj_temp), jnp.zeros_like(adj_temp))
    for step_index in reversed(range(STEPS)):
        flags_now = branch_flags[step_index]

        def advance(temp, salt, zonal, merid):
            return forward_step((temp, salt, zonal, merid), flags_now, east_speed, north_speed, sea, block_inverse, coupling)
        outputs, pullback = jax.vjp(advance, *zeros)
        state = pullback(state)
    return (state[0], state[1], state[2], state[3])
```

```python
import functools

import jax
import jax.numpy as jnp
from jax import lax
from jax.experimental import pallas as pl
from jax.experimental.pallas import tpu as pltpu
from jax.sharding import PartitionSpec as P

STEPS = 2

advect_scale = 0.25
diffusion = 0.5
gravity = 0.1
pressure_scale = 1.0
viscosity = 0.1
haline = 0.8

BLOCK = 8
f32 = jnp.float32
bf16 = jnp.bfloat16
CORNER_LANE = 16


def split(value):
    high = value.astype(bf16)
    return high, (value - high.astype(f32)).astype(bf16)


def dot(a, b, contract=((1,), (0,))):
    return lax.dot_general(a, b, (contract, ((), ())), preferred_element_type=f32)


def dot3(a, b):
    return dot(a[0], b[0]) + (dot(a[0], b[1]) + dot(a[1], b[0]))


def iota(shape, dim):
    return lax.broadcasted_iota(jnp.int32, shape, dim)


def branches(flags):
    one = jnp.where(flags >= 3, 1, 0) + jnp.where(flags >= 6, 1, 0)
    zonal = (flags - 3 * one).astype(f32) * 0.5
    return zonal, one.astype(f32) * 0.5


def lane_of(value, lane):
    return jnp.broadcast_to(value[:, lane : lane + 1], value.shape)


def level(ref, k, rows):
    return ref[pl.ds(pl.multiple_of(k * rows, rows), rows), :]


def take_row(ref, row, levels, rows):
    if isinstance(row, int):
        return ref[pl.ds(row, levels, stride=rows), :]
    low = ref[pl.ds(0, levels, stride=rows), :]
    high = ref[pl.ds(rows - 1, levels, stride=rows), :]
    return jnp.where(row == 0, low, high)


def row_choices(pair, rows, lat):
    return [jnp.where(lat == 0, rows - 1, 0)] if pair else [0, rows - 1]


def pack_kernel(dims, ids, t, s, u, v, sea, east, north, flags, inverse, to_east, to_west, nn_late, *lat_msgs):
    levels, rows, cols, half, pair = dims
    lane = iota((rows, cols), 1)
    fields = (t, s, u, v)

    def some(b, carry):
        accs = list(carry)
        for i in range(BLOCK):
            k = b * BLOCK + i
            here = [level(x, k, rows) for x in fields]
            wet = level(sea, k, rows).astype(f32)
            speed = level(east, k, rows)
            nexts = []
            for step in (1, 0):
                zonal, _ = branches(level(flags.at[step], k, rows))
                nexts.append(wet * (speed * zonal - diffusion))
            low, high = lane == k, lane == k + half
            last = here + [wet] + nexts
            for j, value in enumerate(last):
                place = k + (j % 2) * half
                accs[j // 2] = jnp.where(
                    high if j % 2 else low, pltpu.roll(value, (place + 1) % cols, 1), accs[j // 2]
                )
            for j, value in enumerate(here + [wet]):
                place = k + (j % 2) * half
                accs[4 + j // 2] = jnp.where(
                    high if j % 2 else low, pltpu.roll(value, place % cols, 1), accs[4 + j // 2]
                )
        return tuple(accs)

    zero = jnp.zeros((rows, cols), f32)
    accs = lax.fori_loop(0, levels // BLOCK, some, (zero,) * 7)
    for j in range(4):
        to_east[j] = accs[j]
    for j in range(3):
        to_west[j] = accs[4 + j]
    for which, row in enumerate(row_choices(pair, rows, ids[0])):
        msg = lat_msgs[which]
        for j, x in enumerate(fields):
            msg[j] = take_row(x, row, levels, rows)
        wet = take_row(sea, row, levels, rows).astype(f32)
        speed = take_row(north, row, levels, rows)
        msg[4] = wet
        for step in (1, 0):
            _, merid = branches(take_row(flags.at[step], row, levels, rows))
            value = wet * (speed * merid - diffusion)
            if step:
                msg[5] = value
            elif pair or row:
                nn_late[...] = value
        msg[6] = jnp.zeros((levels, cols), f32)
        if pair:
            block = jnp.where(row == 0, inverse[0], inverse[rows - 1])
        else:
            block = inverse[row]
        msg[6, :, pl.ds(0, levels)] = block


def project_kernel(dims, setup, ids, t, s, u, v, sea, *rest):
    levels, rows, cols, half, pair = dims
    if setup:
        inverse, coup, proj, planes, *rest = rest
        lat_out, (spike, w_high, w_low, p_high, p_low, spike_packed, cells, wide) = rest[:-8], rest[-8:]
        n = levels * rows
        for y in range(rows):
            cells[pl.ds(y, levels, stride=rows), :] = inverse[y]
        pieces = split(cells[...])
        pick = (iota((n, levels), 0) // rows == iota((n, levels), 1)).astype(bf16)
        same = (iota((n, n), 0) % rows) == (iota((n, n), 1) % rows)
        for piece, out in zip(pieces, (w_high, w_low)):
            full = dot(pick, piece, ((1,), (1,)))
            out[...] = jnp.where(same, full, 0.0).astype(bf16)
        wide[...] = jnp.zeros_like(wide)
        for y in range(rows):
            wide[y, pl.ds(0, levels), pl.ds(0, levels)] = inverse[y]
            wide[y, pl.ds(half, levels), pl.ds(half, levels)] = inverse[y]
        high, low = split(wide[...].reshape(rows * cols, cols))
        p_high[...] = high
        p_low[...] = low
        spike_packed[...] = jnp.zeros_like(spike_packed)
        for y in range(rows):
            line = inverse[y, pl.ds(ids[2], 1), :]
            spike_packed[pl.ds(y, 1), pl.ds(0, levels)] = line
            spike_packed[pl.ds(y, 1), pl.ds(half, levels)] = line
    else:
        coup, spike, w_high, w_low, proj, planes, *lat_out = rest
    w = (w_high[...], w_low[...])
    for f, x in enumerate((t, s, u, v)):
        proj[f] = dot3(w, split(x[...]))
    if setup:
        n = levels * rows
        pick = (iota((n, cols), 0) // rows == ids[2]).astype(bf16)
        spike[...] = dot(w[0], pick) + dot(w[1], pick)
    edge = pl.ds(pl.multiple_of(ids[2] * rows, rows), rows)
    for f in range(4):
        planes[f] = proj[f, edge, :]
    sums = [jnp.zeros((rows, cols), f32)] * 3
    for k in range(levels):
        here = pl.ds(k * rows, rows)
        wet = sea[here, :].astype(f32)
        sums = [
            sums[0] + wet * proj[2, here, :],
            sums[1] + wet * proj[3, here, :],
            sums[2] + wet * spike[here, :],
        ]
    for j in range(3):
        planes[4 + j] = sums[j]
    corner = spike[edge, :]
    lane_row = iota((rows, cols), 0)
    coupled = jnp.zeros((rows, cols), f32)
    for y in range(rows):
        coupled = jnp.where(lane_row == y, coup[y], coupled)
    lines = [proj[f, edge, :] for f in range(4)] + [sums[1], sums[2], corner, coupled]
    for which, row in enumerate(row_choices(pair, rows, ids[0])):
        for j, value in enumerate(lines):
            if pair:
                line = jnp.where(row == 0, value[0:1], value[rows - 1 : rows])
            else:
                line = value[row : row + 1]
            lat_out[which][pl.ds(j, 1), :] = line


def side_kernel(dims, ids, west, east, west_sea, east_sea, planes, spike, spike_packed, p_high, p_low, msg, proj):
    levels, rows, cols, half, pair = dims
    lane = iota((rows, cols), 1)
    row = iota((rows, cols), 0)
    packed = (west[0], west[1], east[0], east[1])
    chunks = []
    for y in range(rows):
        chunks.append(jnp.concatenate([jnp.where(row == y, x, 0.0) for x in packed], axis=0))
    lhs = jnp.concatenate(chunks, axis=1)
    out = dot3(split(lhs), (p_high[...], p_low[...]))
    for j in range(4):
        proj[j] = out[j * rows : (j + 1) * rows]
    for j in range(7):
        msg[j] = planes[j]
    edge = ids[2]
    misc = jnp.zeros((rows, cols), f32)
    spk = spike_packed[...]
    for side, wet in enumerate((west_sea, east_sea)):
        wet = jnp.where(lane < half, wet[2], 0.0)
        for p in range(2):
            value = out[(2 * side + p) * rows : (2 * side + p + 1) * rows]
            for i in range(2):
                column = jnp.sum(jnp.where(lane == edge + i * half, value, 0.0), axis=1, keepdims=True)
                misc = jnp.where(lane == side * 8 + 2 * p + i, column, misc)
            if p == 1:
                column = jnp.sum(wet * value, axis=1, keepdims=True)
                misc = jnp.where(lane == side * 8 + 4, column, misc)
        column = jnp.sum(wet * spk, axis=1, keepdims=True)
        misc = jnp.where(lane == side * 8 + 5, column, misc)
    corner = level(spike, edge, rows)
    msg[7] = jnp.where(lane == CORNER_LANE, corner, misc)


def stencil_kernel(dims, step, final, ids, coup, proj, spike, spike_packed, mine, theirs, side_proj,
                   west_const, east_const, sea, east, north, flags, *rest):
    levels, rows, cols, half, pair = dims
    count = 1 if pair else 2
    row_new, row_const, row_late, row_far = (rest[i * count : (i + 1) * count] for i in range(4))
    rest = rest[4 * count :]
    if final:
        outs, rest = rest[:4], rest[4:]
    else:
        late_out, rest = rest[0], rest[1:]
        outs, (to_east, to_west), rest = rest[:4], rest[4:6], rest[6:]
        lat_msgs, rest = rest[:count], rest[count:]
    north_w, south_w, north_sea, south_next, line, sides = rest
    lat, depth, edge, parts = ids[0], ids[1], ids[2], ids[3]
    lane = iota((rows, cols), 1)
    row = iota((rows, cols), 0)
    has_north = jnp.where(lat < parts - 1, 1.0, 0.0)
    has_south = jnp.where(lat > 0, 1.0, 0.0)

    row_sums = []
    for h in range(count):
        block = split(row_const[h][6][:, :levels])
        eye = (iota((levels, levels), 0) == iota((levels, levels), 1)).astype(bf16)
        turned = tuple(dot(eye, piece, ((1,), (1,))).astype(bf16) for piece in block)
        pick = (iota((levels, cols), 0) == edge).astype(bf16)
        thin = dot(turned[0], pick) + dot(turned[1], pick)
        line[4] = thin
        for f in range(4):
            line[f] = dot3(turned, split(row_new[h][f]))
        at_edge = pl.ds(edge, 1)
        far = row_far[h]
        c = far[7:8, :]
        other_corner = far[6:7, :]
        own_corner = line[4, at_edge, :]
        scaled = c / (1.0 - c * c * own_corner * other_corner)
        wet = row_const[h][4]
        if pair:
            masks = ((north_w, has_north), (south_w, has_south))
        else:
            masks = ((north_w, has_north),) if h == 0 else ((south_w, has_south),)
        for f in range(4):
            carried = scaled * (far[f : f + 1, :] + c * other_corner * line[f, at_edge, :])
            value = wet * (line[f] + thin * carried)
            for target, mask in masks:
                target[f] = value * mask
        if pair or h == 0:
            north_sea[...] = wet * has_north
        if pair or h == 1:
            late = row_const[h][5] if step else row_late[h][4]
            south_next[...] = late * has_south
        theirs_v = scaled * (line[3, at_edge, :] + c * own_corner * far[3:4, :])
        row_sums.append(far[4:5, :] + far[5:6, :] * theirs_v)
    row_sum_north, row_sum_south = row_sums[0], row_sums[-1]

    c = jnp.zeros((rows, cols), f32)
    for y in range(rows):
        c = jnp.where(row == y, coup[y], c)
    own_corner = lane_of(mine[7], CORNER_LANE)
    other_corner = lane_of(theirs[7], CORNER_LANE)
    scaled = c / (1.0 - c * c * own_corner * other_corner)
    co, cm = c * other_corner, c * own_corner
    carried = [scaled * (theirs[f] + co * mine[f]) for f in range(4)]
    misc = theirs[7]
    carried_side = scaled * (misc + co * mine[7])
    theirs_side = scaled * (mine[7] + cm * misc)

    spk = spike_packed[...]
    for side, const in enumerate((west_const, east_const)):
        wet = jnp.where(lane < half, const[2], pltpu.roll(const[2], half, 1))
        for p in range(2):
            joined = jnp.where(
                lane < half,
                lane_of(carried_side, side * 8 + 2 * p),
                lane_of(carried_side, side * 8 + 2 * p + 1),
            )
            sides[2 * side + p] = wet * (side_proj[2 * side + p] + spk * joined)

    sum_u = theirs[4] + theirs[6] * (scaled * (mine[2] + cm * theirs[2]))
    sum_v = theirs[5] + theirs[6] * (scaled * (mine[3] + cm * theirs[3]))
    side_u = [lane_of(misc, q * 8 + 4) + lane_of(misc, q * 8 + 5) * lane_of(theirs_side, q * 8 + 2) for q in (0, 1)]

    def shifted(value, west_in, east_in, south_in, north_in):
        return (
            jnp.where(lane == 0, west_in, pltpu.roll(value, 1, 1)),
            jnp.where(lane == cols - 1, east_in, pltpu.roll(value, cols - 1, 1)),
            jnp.where(row == 0, south_in, pltpu.roll(value, 1, 0)),
            jnp.where(row == rows - 1, north_in, pltpu.roll(value, rows - 1, 0)),
        )

    west_u = jnp.where(lane == 0, side_u[0], pltpu.roll(sum_u, 1, 1))
    east_u = jnp.where(lane == cols - 1, side_u[1], pltpu.roll(sum_u, cols - 1, 1))
    south_v = jnp.where(row == 0, row_sum_south * has_south, pltpu.roll(sum_v, 1, 0))
    north_v = jnp.where(row == rows - 1, row_sum_north * has_north, pltpu.roll(sum_v, rows - 1, 0))
    upper = jnp.where(depth == 0, 1.0, 0.0)
    deeper = (-0.5 * pressure_scale) * (west_u - east_u + south_v - north_v) * upper

    north_index = (lat * rows + row).astype(f32)
    coriolis = 0.2 + 0.6 * (north_index + 0.5) / (rows * parts).astype(f32)

    west_sides = (sides[0], sides[1])
    east_sides = (sides[2], sides[3])
    sea_east_side = east_const[2]
    next_west_side = west_const[2] if step else west_const[3]
    next_shift = half if step else 0

    def some(b, carry):
        below, *accs = carry
        for i in range(BLOCK):
            k = levels - 1 - (b * BLOCK + i)
            wet = level(sea, k, rows).astype(f32)
            speed_e, speed_n = level(east, k, rows), level(north, k, rows)
            zonal_b, merid_b = branches(level(flags.at[step], k, rows))
            east_self = wet * (speed_e * (1.0 - zonal_b) + diffusion)
            east_next = wet * (speed_e * zonal_b - diffusion)
            north_self = wet * (speed_n * (1.0 - merid_b) + diffusion)
            north_next = wet * (speed_n * merid_b - diffusion)
            one = pl.ds(k, 1)
            sea_east = jnp.where(
                lane == cols - 1, pltpu.roll(sea_east_side, cols - 1 - k, 1), pltpu.roll(wet, cols - 1, 1)
            )
            next_west = jnp.where(
                lane == 0, pltpu.roll(next_west_side, (cols - next_shift) - k, 1), pltpu.roll(east_next, 1, 1)
            )
            sea_north = jnp.where(row == rows - 1, north_sea[one, :], pltpu.roll(wet, rows - 1, 0))
            next_south = jnp.where(row == 0, south_next[one, :], pltpu.roll(north_next, 1, 0))
            east_own = advect_scale * east_self * sea_east
            west_own = advect_scale * next_west * wet
            north_own = advect_scale * north_self * sea_north
            south_own = advect_scale * next_south * wet
            spk_k = level(spike, k, rows)
            solved, around = [], []
            for f in range(4):
                w = wet * (level(proj.at[f], k, rows) + spk_k * carried[f])
                shift = (f % 2) * half
                solved.append(w)
                around.append(
                    shifted(
                        w,
                        pltpu.roll(west_sides[f // 2], (cols - shift) - k, 1),
                        pltpu.roll(east_sides[f // 2], (cols - 1 - shift) - k, 1),
                        south_w[f, one, :],
                        north_w[f, one, :],
                    )
                )
            pressure = (-0.5 * pressure_scale) * (
                around[2][0] - around[2][1] + around[3][2] - around[3][3]
            )
            below = below + pressure
            buoyancy = gravity * below
            new = []
            for f in range(2):
                w, (ww, we, ws, wn) = solved[f], around[f]
                q = w + (
                    (east_own * (we - w) + west_own * (w - ww)) + (north_own * (wn - w) + south_own * (w - ws))
                )
                new.append(q + buoyancy if f == 0 else q - haline * buoyancy)
            for f in (2, 3):
                w, (ww, we, ws, wn) = solved[f], around[f]
                turn = -solved[3] if f == 2 else solved[2]
                new.append(w + coriolis * turn + viscosity * ((we + ww) + (wn + ws) - 4.0 * w))
            here = pl.ds(pl.multiple_of(k * rows, rows), rows)
            for f in range(4):
                outs[f][here, :] = new[f]
            if not final:
                for f in range(4):
                    place = k + (f % 2) * half
                    there = lane == place
                    accs[f // 2] = jnp.where(there, pltpu.roll(new[f], (place + 1) % cols, 1), accs[f // 2])
                    accs[2 + f // 2] = jnp.where(there, pltpu.roll(new[f], place % cols, 1), accs[2 + f // 2])
        return (below, *accs)

    zero = jnp.zeros((rows, cols), f32)
    extra = () if final else (zero,) * 4
    _, *accs = lax.fori_loop(0, levels // BLOCK, some, (deeper, *extra))
    if not final:
        for p in range(2):
            to_east[p] = accs[p]
            to_west[p] = accs[2 + p]
        for which, at in enumerate(row_choices(pair, rows, lat)):
            for f in range(4):
                lat_msgs[which][f] = take_row(outs[f], at, levels, rows)
            lat_msgs[which][4] = late_out[...]


def call(kernel, outs, args, smem=(0,), scratch=(), name=None):
    specs = [
        pl.BlockSpec(memory_space=pltpu.SMEM if i in smem else pltpu.VMEM) for i in range(len(args))
    ]
    return pl.pallas_call(
        kernel,
        out_shape=[jax.ShapeDtypeStruct(shape, kind) for shape, kind in outs],
        in_specs=specs,
        out_specs=[pl.BlockSpec(memory_space=pltpu.VMEM)] * len(outs),
        scratch_shapes=list(scratch),
        name=name,
    )(*args)


def on_device(
    adj_temp,
    adj_salt,
    adj_zonal,
    adj_merid,
    east_speed,
    north_speed,
    branch_flags,
    sea_mask,
    block_inverse,
    coupling,
):
    levels, rows, cols = adj_temp.shape
    half = cols // 2
    lons, lats, depths = (lax.axis_size(a) for a in ("lon", "lat", "depth"))
    pair = lats == 2
    dims = (levels, rows, cols, half, pair)
    count = 1 if pair else 2
    n = levels * rows
    lat, depth = lax.axis_index("lat"), lax.axis_index("depth")
    ids = jnp.stack([lat, depth, (levels - 1) * (1 - depth), jnp.int32(lats)]).astype(jnp.int32)
    flat = lambda x: x.reshape(x.shape[:-3] + (n, cols))
    sea, east, north, flags = flat(sea_mask), flat(east_speed), flat(north_speed), flat(branch_flags)
    state = [flat(x) for x in (adj_temp, adj_salt, adj_zonal, adj_merid)]
    plane = (rows, cols)
    grid = (levels, cols)

    ring = [(i, (i + 1) % lons) for i in range(lons)]
    back = [(b, a) for a, b in ring]
    up = [(i, i + 1) for i in range(lats - 1)]
    down = [(b, a) for a, b in up]

    def to_lat(msgs, flip):
        routes = [up + down] if pair else [down, up]
        if not flip:
            return [lax.ppermute(m, "lat", r) for m, r in zip(msgs, routes)]
        both = [
            [(a * depths + d, b * depths + (depths - 1 - d)) for a, b in r for d in range(depths)] for r in routes
        ]
        return [lax.ppermute(m, ("lat", "depth"), r) for m, r in zip(msgs, both)]

    def to_depth(msg):
        return lax.ppermute(msg, "depth", [(d, depths - 1 - d) for d in range(depths)])

    to_east, to_west, late, *lat_msgs = call(
        functools.partial(pack_kernel, dims),
        [((4,) + plane, f32), ((3,) + plane, f32), (grid, f32)] + [((7,) + grid, f32)] * count,
        (ids, *state, sea, east, north, flags, block_inverse),
        name="pack",
    )
    row_const = to_lat(lat_msgs, False)
    west_const = lax.ppermute(to_east, "lon", ring)
    east_const = lax.ppermute(to_west, "lon", back)
    row_new, west, east_in = row_const, west_const, east_const

    for step in reversed(range(STEPS)):
        first = step == STEPS - 1
        outs = [((4, n, cols), f32), ((7,) + plane, f32)] + [(plane, f32)] * count
        if first:
            outs += [((n, cols), f32)] + [((n, n), bf16)] * 2 + [((rows * cols, cols), bf16)] * 2 + [(plane, f32)]
            args = (ids, *state, sea, block_inverse, coupling)
            smem = (0, 7)
            scratch = (pltpu.VMEM((n, levels), f32), pltpu.VMEM((rows, cols, cols), f32))
        else:
            args = (ids, *state, sea, coupling, spike, w_high, w_low)
            smem = (0, 6)
            scratch = ()
        proj, planes, *more = call(
            functools.partial(project_kernel, dims, first), outs, args, smem, scratch, name="project"
        )
        far_msgs = more[:count]
        if first:
            spike, w_high, w_low, p_high, p_low, spike_packed = more[count:]
        row_far = to_lat(far_msgs, True)
        mine, side_proj = call(
            functools.partial(side_kernel, dims),
            [((8,) + plane, f32), ((4,) + plane, f32)],
            (ids, west, east_in, west_const, east_const, planes, spike, spike_packed, p_high, p_low),
            name="sides",
        )
        theirs = to_depth(mine)
        final = step == 0
        state_shape = [((n, cols), f32)] * 4
        if final:
            outs, extra = state_shape, ()
        else:
            outs = state_shape + [((2,) + plane, f32)] * 2 + [((5,) + grid, f32)] * count
            extra = (late,)
        result = call(
            functools.partial(stencil_kernel, dims, step, final),
            outs,
            (
                ids, coupling, proj, spike, spike_packed, mine, theirs, side_proj, west_const, east_const,
                sea, east, north, flags, *row_new, *row_const, *row_new, *row_far, *extra,
            ),
            (0, 1),
            (
                pltpu.VMEM((4,) + grid, f32),
                pltpu.VMEM((4,) + grid, f32),
                pltpu.VMEM(grid, f32),
                pltpu.VMEM(grid, f32),
                pltpu.VMEM((5,) + grid, f32),
                pltpu.VMEM((4,) + plane, f32),
            ),
            name="stencil",
        )
        state = result[:4]
        if not final:
            row_new = to_lat(result[6:], False)
            west = lax.ppermute(result[4], "lon", ring)
            east_in = lax.ppermute(result[5], "lon", back)
    return tuple(x.reshape(levels, rows, cols) for x in state)


def solution(mesh):
    in_specs = (
        P("depth", "lat", "lon"),
        P("depth", "lat", "lon"),
        P("depth", "lat", "lon"),
        P("depth", "lat", "lon"),
        P("depth", "lat", "lon"),
        P("depth", "lat", "lon"),
        P(None, "depth", "lat", "lon"),
        P("depth", "lat", "lon"),
        P("lat", "depth", None),
        P("lat"),
    )
    out_specs = (
        P("depth", "lat", "lon"),
        P("depth", "lat", "lon"),
        P("depth", "lat", "lon"),
        P("depth", "lat", "lon"),
    )
    return jax.shard_map(
        on_device, mesh=mesh, in_specs=in_specs, out_specs=out_specs, check_vma=False
    )
```

```python
import functools

import jax
import jax.numpy as jnp
from jax import lax
from jax.experimental import pallas as pl
from jax.experimental.pallas import tpu as pltpu
from jax.sharding import PartitionSpec as P

STEPS = 2

advect_scale = 0.25
diffusion = 0.5
gravity = 0.1
pressure_scale = 1.0
viscosity = 0.1
haline = 0.8

BLOCK = 8
VMEM_BYTES = 12 * 1024 * 1024
f32 = jnp.float32
bf16 = jnp.bfloat16
CORNER_LANE = 16


def split(value):
    high = value.astype(bf16)
    return high, (value - high.astype(f32)).astype(bf16)


def dot(a, b, contract=((1,), (0,))):
    return lax.dot_general(a, b, (contract, ((), ())), preferred_element_type=f32)


def dot3(a, b):
    return dot(a[0], b[0]) + (dot(a[0], b[1]) + dot(a[1], b[0]))


def iota(shape, dim):
    return lax.broadcasted_iota(jnp.int32, shape, dim)


def branches(flags):
    one = jnp.where(flags >= 3, 1, 0) + jnp.where(flags >= 6, 1, 0)
    zonal = (flags - 3 * one).astype(f32) * 0.5
    return zonal, one.astype(f32) * 0.5


def lane_of(value, lane):
    return jnp.broadcast_to(value[:, lane : lane + 1], value.shape)


def level(ref, k, rows):
    return ref[pl.ds(pl.multiple_of(k * rows, rows), rows), :]


def take_row(ref, row, levels, rows):
    if isinstance(row, int):
        return ref[pl.ds(row, levels, stride=rows), :]
    low = ref[pl.ds(0, levels, stride=rows), :]
    high = ref[pl.ds(rows - 1, levels, stride=rows), :]
    return jnp.where(row == 0, low, high)


def row_choices(pair, rows, lat):
    return [jnp.where(lat == 0, rows - 1, 0)] if pair else [0, rows - 1]


def pack_kernel(dims, ids, t, s, u, v, sea, east, north, flags, inverse, to_east, to_west, nn_late, *lat_msgs):
    levels, rows, cols, half, pair = dims
    lane = iota((rows, cols), 1)
    fields = (t, s, u, v)

    def some(b, carry):
        accs = list(carry)
        for i in range(BLOCK):
            k = b * BLOCK + i
            here = [level(x, k, rows) for x in fields]
            wet = level(sea, k, rows).astype(f32)
            speed = level(east, k, rows)
            nexts = []
            for step in (1, 0):
                zonal, _ = branches(level(flags.at[step], k, rows))
                nexts.append(wet * (speed * zonal - diffusion))
            low, high = lane == k, lane == k + half
            last = here + [wet] + nexts
            for j, value in enumerate(last):
                place = k + (j % 2) * half
                accs[j // 2] = jnp.where(
                    high if j % 2 else low, pltpu.roll(value, (place + 1) % cols, 1), accs[j // 2]
                )
            for j, value in enumerate(here + [wet]):
                place = k + (j % 2) * half
                accs[4 + j // 2] = jnp.where(
                    high if j % 2 else low, pltpu.roll(value, place % cols, 1), accs[4 + j // 2]
                )
        return tuple(accs)

    zero = jnp.zeros((rows, cols), f32)
    accs = lax.fori_loop(0, levels // BLOCK, some, (zero,) * 7)
    for j in range(4):
        to_east[j] = accs[j]
    for j in range(3):
        to_west[j] = accs[4 + j]
    for which, row in enumerate(row_choices(pair, rows, ids[0])):
        msg = lat_msgs[which]
        for j, x in enumerate(fields):
            msg[j] = take_row(x, row, levels, rows)
        wet = take_row(sea, row, levels, rows).astype(f32)
        speed = take_row(north, row, levels, rows)
        msg[4] = wet
        for step in (1, 0):
            _, merid = branches(take_row(flags.at[step], row, levels, rows))
            value = wet * (speed * merid - diffusion)
            if step:
                msg[5] = value
            elif pair or row:
                nn_late[...] = value
        msg[6] = jnp.zeros((levels, cols), f32)
        if pair:
            block = jnp.where(row == 0, inverse[0], inverse[rows - 1])
        else:
            block = inverse[row]
        msg[6, :, pl.ds(0, levels)] = block


def project_kernel(dims, setup, ids, t, s, u, v, sea, *rest):
    levels, rows, cols, half, pair = dims
    if setup:
        inverse, coup, proj, planes, *rest = rest
        lat_out, (spike, w_high, w_low, p_high, p_low, spike_packed, cells, wide) = rest[:-8], rest[-8:]
        n = levels * rows
        for y in range(rows):
            cells[pl.ds(y, levels, stride=rows), :] = inverse[y]
        pieces = split(cells[...])
        pick = (iota((n, levels), 0) // rows == iota((n, levels), 1)).astype(bf16)
        same = (iota((n, n), 0) % rows) == (iota((n, n), 1) % rows)
        for piece, out in zip(pieces, (w_high, w_low)):
            full = dot(pick, piece, ((1,), (1,)))
            out[...] = jnp.where(same, full, 0.0).astype(bf16)
        wide[...] = jnp.zeros_like(wide)
        for y in range(rows):
            wide[y, pl.ds(0, levels), pl.ds(0, levels)] = inverse[y]
            wide[y, pl.ds(half, levels), pl.ds(half, levels)] = inverse[y]
        high, low = split(wide[...].reshape(rows * cols, cols))
        p_high[...] = high
        p_low[...] = low
        spike_packed[...] = jnp.zeros_like(spike_packed)
        for y in range(rows):
            line = inverse[y, pl.ds(ids[2], 1), :]
            spike_packed[pl.ds(y, 1), pl.ds(0, levels)] = line
            spike_packed[pl.ds(y, 1), pl.ds(half, levels)] = line
    else:
        coup, spike, w_high, w_low, proj, planes, *lat_out = rest
    w = (w_high[...], w_low[...])
    for f, x in enumerate((t, s, u, v)):
        proj[f] = dot3(w, split(x[...]))
    if setup:
        n = levels * rows
        pick = (iota((n, cols), 0) // rows == ids[2]).astype(bf16)
        spike[...] = dot(w[0], pick) + dot(w[1], pick)
    edge = pl.ds(pl.multiple_of(ids[2] * rows, rows), rows)
    for f in range(4):
        planes[f] = proj[f, edge, :]
    sums = [jnp.zeros((rows, cols), f32)] * 3
    for k in range(levels):
        here = pl.ds(k * rows, rows)
        wet = sea[here, :].astype(f32)
        sums = [
            sums[0] + wet * proj[2, here, :],
            sums[1] + wet * proj[3, here, :],
            sums[2] + wet * spike[here, :],
        ]
    for j in range(3):
        planes[4 + j] = sums[j]
    corner = spike[edge, :]
    lane_row = iota((rows, cols), 0)
    coupled = jnp.zeros((rows, cols), f32)
    for y in range(rows):
        coupled = jnp.where(lane_row == y, coup[y], coupled)
    lines = [proj[f, edge, :] for f in range(4)] + [sums[1], sums[2], corner, coupled]
    for which, row in enumerate(row_choices(pair, rows, ids[0])):
        for j, value in enumerate(lines):
            if pair:
                line = jnp.where(row == 0, value[0:1], value[rows - 1 : rows])
            else:
                line = value[row : row + 1]
            lat_out[which][pl.ds(j, 1), :] = line


def side_kernel(dims, ids, west, east, west_sea, east_sea, planes, spike, spike_packed, p_high, p_low, msg, proj):
    levels, rows, cols, half, pair = dims
    lane = iota((rows, cols), 1)
    row = iota((rows, cols), 0)
    packed = (west[0], west[1], east[0], east[1])
    chunks = []
    for y in range(rows):
        chunks.append(jnp.concatenate([jnp.where(row == y, x, 0.0) for x in packed], axis=0))
    lhs = jnp.concatenate(chunks, axis=1)
    out = dot3(split(lhs), (p_high[...], p_low[...]))
    for j in range(4):
        proj[j] = out[j * rows : (j + 1) * rows]
    for j in range(7):
        msg[j] = planes[j]
    edge = ids[2]
    misc = jnp.zeros((rows, cols), f32)
    spk = spike_packed[...]
    for side, wet in enumerate((west_sea, east_sea)):
        wet = jnp.where(lane < half, wet[2], 0.0)
        for p in range(2):
            value = out[(2 * side + p) * rows : (2 * side + p + 1) * rows]
            for i in range(2):
                column = jnp.sum(jnp.where(lane == edge + i * half, value, 0.0), axis=1, keepdims=True)
                misc = jnp.where(lane == side * 8 + 2 * p + i, column, misc)
            if p == 1:
                column = jnp.sum(wet * value, axis=1, keepdims=True)
                misc = jnp.where(lane == side * 8 + 4, column, misc)
        column = jnp.sum(wet * spk, axis=1, keepdims=True)
        misc = jnp.where(lane == side * 8 + 5, column, misc)
    corner = level(spike, edge, rows)
    msg[7] = jnp.where(lane == CORNER_LANE, corner, misc)


def stencil_kernel(dims, step, final, ids, coup, proj, spike, spike_packed, mine, theirs, side_proj,
                   west_const, east_const, sea, east, north, flags, *rest):
    levels, rows, cols, half, pair = dims
    count = 1 if pair else 2
    row_new, row_const, row_late, row_far = (rest[i * count : (i + 1) * count] for i in range(4))
    rest = rest[4 * count :]
    if final:
        outs, rest = rest[:4], rest[4:]
    else:
        late_out, rest = rest[0], rest[1:]
        outs, (to_east, to_west), rest = rest[:4], rest[4:6], rest[6:]
        lat_msgs, rest = rest[:count], rest[count:]
    north_w, south_w, north_sea, south_next, line, sides = rest
    lat, depth, edge, parts = ids[0], ids[1], ids[2], ids[3]
    lane = iota((rows, cols), 1)
    row = iota((rows, cols), 0)
    has_north = jnp.where(lat < parts - 1, 1.0, 0.0)
    has_south = jnp.where(lat > 0, 1.0, 0.0)

    row_sums = []
    for h in range(count):
        block = split(row_const[h][6][:, :levels])
        eye = (iota((levels, levels), 0) == iota((levels, levels), 1)).astype(bf16)
        turned = tuple(dot(eye, piece, ((1,), (1,))).astype(bf16) for piece in block)
        pick = (iota((levels, cols), 0) == edge).astype(bf16)
        thin = dot(turned[0], pick) + dot(turned[1], pick)
        line[4] = thin
        for f in range(4):
            line[f] = dot3(turned, split(row_new[h][f]))
        at_edge = pl.ds(edge, 1)
        far = row_far[h]
        c = far[7:8, :]
        other_corner = far[6:7, :]
        own_corner = line[4, at_edge, :]
        scaled = c / (1.0 - c * c * own_corner * other_corner)
        wet = row_const[h][4]
        if pair:
            masks = ((north_w, has_north), (south_w, has_south))
        else:
            masks = ((north_w, has_north),) if h == 0 else ((south_w, has_south),)
        for f in range(4):
            carried = scaled * (far[f : f + 1, :] + c * other_corner * line[f, at_edge, :])
            value = wet * (line[f] + thin * carried)
            for target, mask in masks:
                target[f] = value * mask
        if pair or h == 0:
            north_sea[...] = wet * has_north
        if pair or h == 1:
            late = row_const[h][5] if step else row_late[h][4]
            south_next[...] = late * has_south
        theirs_v = scaled * (line[3, at_edge, :] + c * own_corner * far[3:4, :])
        row_sums.append(far[4:5, :] + far[5:6, :] * theirs_v)
    row_sum_north, row_sum_south = row_sums[0], row_sums[-1]

    c = jnp.zeros((rows, cols), f32)
    for y in range(rows):
        c = jnp.where(row == y, coup[y], c)
    own_corner = lane_of(mine[7], CORNER_LANE)
    other_corner = lane_of(theirs[7], CORNER_LANE)
    scaled = c / (1.0 - c * c * own_corner * other_corner)
    co, cm = c * other_corner, c * own_corner
    carried = [scaled * (theirs[f] + co * mine[f]) for f in range(4)]
    misc = theirs[7]
    carried_side = scaled * (misc + co * mine[7])
    theirs_side = scaled * (mine[7] + cm * misc)

    spk = spike_packed[...]
    for side, const in enumerate((west_const, east_const)):
        wet = jnp.where(lane < half, const[2], pltpu.roll(const[2], half, 1))
        for p in range(2):
            joined = jnp.where(
                lane < half,
                lane_of(carried_side, side * 8 + 2 * p),
                lane_of(carried_side, side * 8 + 2 * p + 1),
            )
            sides[2 * side + p] = wet * (side_proj[2 * side + p] + spk * joined)

    sum_u = theirs[4] + theirs[6] * (scaled * (mine[2] + cm * theirs[2]))
    sum_v = theirs[5] + theirs[6] * (scaled * (mine[3] + cm * theirs[3]))
    side_u = [lane_of(misc, q * 8 + 4) + lane_of(misc, q * 8 + 5) * lane_of(theirs_side, q * 8 + 2) for q in (0, 1)]

    def shifted(value, west_in, east_in, south_in, north_in):
        return (
            jnp.where(lane == 0, west_in, pltpu.roll(value, 1, 1)),
            jnp.where(lane == cols - 1, east_in, pltpu.roll(value, cols - 1, 1)),
            jnp.where(row == 0, south_in, pltpu.roll(value, 1, 0)),
            jnp.where(row == rows - 1, north_in, pltpu.roll(value, rows - 1, 0)),
        )

    west_u = jnp.where(lane == 0, side_u[0], pltpu.roll(sum_u, 1, 1))
    east_u = jnp.where(lane == cols - 1, side_u[1], pltpu.roll(sum_u, cols - 1, 1))
    south_v = jnp.where(row == 0, row_sum_south * has_south, pltpu.roll(sum_v, 1, 0))
    north_v = jnp.where(row == rows - 1, row_sum_north * has_north, pltpu.roll(sum_v, rows - 1, 0))
    upper = jnp.where(depth == 0, 1.0, 0.0)
    deeper = (-0.5 * pressure_scale) * (west_u - east_u + south_v - north_v) * upper

    north_index = (lat * rows + row).astype(f32)
    coriolis = 0.2 + 0.6 * (north_index + 0.5) / (rows * parts).astype(f32)

    west_sides = (sides[0], sides[1])
    east_sides = (sides[2], sides[3])
    sea_east_side = east_const[2]
    next_west_side = west_const[2] if step else west_const[3]
    next_shift = half if step else 0

    def some(b, carry):
        below, *accs = carry
        for i in range(BLOCK):
            k = levels - 1 - (b * BLOCK + i)
            wet = level(sea, k, rows).astype(f32)
            speed_e, speed_n = level(east, k, rows), level(north, k, rows)
            zonal_b, merid_b = branches(level(flags.at[step], k, rows))
            east_self = wet * (speed_e * (1.0 - zonal_b) + diffusion)
            east_next = wet * (speed_e * zonal_b - diffusion)
            north_self = wet * (speed_n * (1.0 - merid_b) + diffusion)
            north_next = wet * (speed_n * merid_b - diffusion)
            one = pl.ds(k, 1)
            sea_east = jnp.where(
                lane == cols - 1, pltpu.roll(sea_east_side, cols - 1 - k, 1), pltpu.roll(wet, cols - 1, 1)
            )
            next_west = jnp.where(
                lane == 0, pltpu.roll(next_west_side, (cols - next_shift) - k, 1), pltpu.roll(east_next, 1, 1)
            )
            sea_north = jnp.where(row == rows - 1, north_sea[one, :], pltpu.roll(wet, rows - 1, 0))
            next_south = jnp.where(row == 0, south_next[one, :], pltpu.roll(north_next, 1, 0))
            east_own = advect_scale * east_self * sea_east
            west_own = advect_scale * next_west * wet
            north_own = advect_scale * north_self * sea_north
            south_own = advect_scale * next_south * wet
            spk_k = level(spike, k, rows)
            solved, around = [], []
            for f in range(4):
                w = wet * (level(proj.at[f], k, rows) + spk_k * carried[f])
                shift = (f % 2) * half
                solved.append(w)
                around.append(
                    shifted(
                        w,
                        pltpu.roll(west_sides[f // 2], (cols - shift) - k, 1),
                        pltpu.roll(east_sides[f // 2], (cols - 1 - shift) - k, 1),
                        south_w[f, one, :],
                        north_w[f, one, :],
                    )
                )
            pressure = (-0.5 * pressure_scale) * (
                around[2][0] - around[2][1] + around[3][2] - around[3][3]
            )
            below = below + pressure
            buoyancy = gravity * below
            new = []
            for f in range(2):
                w, (ww, we, ws, wn) = solved[f], around[f]
                q = w + (
                    (east_own * (we - w) + west_own * (w - ww)) + (north_own * (wn - w) + south_own * (w - ws))
                )
                new.append(q + buoyancy if f == 0 else q - haline * buoyancy)
            for f in (2, 3):
                w, (ww, we, ws, wn) = solved[f], around[f]
                turn = -solved[3] if f == 2 else solved[2]
                new.append(w + coriolis * turn + viscosity * ((we + ww) + (wn + ws) - 4.0 * w))
            here = pl.ds(pl.multiple_of(k * rows, rows), rows)
            for f in range(4):
                outs[f][here, :] = new[f]
            if not final:
                for f in range(4):
                    place = k + (f % 2) * half
                    there = lane == place
                    accs[f // 2] = jnp.where(there, pltpu.roll(new[f], (place + 1) % cols, 1), accs[f // 2])
                    accs[2 + f // 2] = jnp.where(there, pltpu.roll(new[f], place % cols, 1), accs[2 + f // 2])
        return (below, *accs)

    zero = jnp.zeros((rows, cols), f32)
    extra = () if final else (zero,) * 4
    _, *accs = lax.fori_loop(0, levels // BLOCK, some, (deeper, *extra))
    if not final:
        for p in range(2):
            to_east[p] = accs[p]
            to_west[p] = accs[2 + p]
        for which, at in enumerate(row_choices(pair, rows, lat)):
            for f in range(4):
                lat_msgs[which][f] = take_row(outs[f], at, levels, rows)
            lat_msgs[which][4] = late_out[...]


def call(kernel, outs, args, smem=(0,), scratch=(), name=None):
    specs = [
        pl.BlockSpec(memory_space=pltpu.SMEM if i in smem else pltpu.VMEM) for i in range(len(args))
    ]
    return pl.pallas_call(
        kernel,
        out_shape=[jax.ShapeDtypeStruct(shape, kind) for shape, kind in outs],
        in_specs=specs,
        out_specs=[pl.BlockSpec(memory_space=pltpu.VMEM)] * len(outs),
        scratch_shapes=list(scratch),
        compiler_params=pltpu.CompilerParams(vmem_limit_bytes=VMEM_BYTES),
        name=name,
    )(*args)


def on_device(
    adj_temp,
    adj_salt,
    adj_zonal,
    adj_merid,
    east_speed,
    north_speed,
    branch_flags,
    sea_mask,
    block_inverse,
    coupling,
):
    levels, rows, cols = adj_temp.shape
    half = cols // 2
    lons, lats, depths = (lax.axis_size(a) for a in ("lon", "lat", "depth"))
    pair = lats == 2
    dims = (levels, rows, cols, half, pair)
    count = 1 if pair else 2
    n = levels * rows
    lat, depth = lax.axis_index("lat"), lax.axis_index("depth")
    ids = jnp.stack([lat, depth, (levels - 1) * (1 - depth), jnp.int32(lats)]).astype(jnp.int32)
    flat = lambda x: x.reshape(x.shape[:-3] + (n, cols))
    sea, east, north, flags = flat(sea_mask), flat(east_speed), flat(north_speed), flat(branch_flags)
    state = [flat(x) for x in (adj_temp, adj_salt, adj_zonal, adj_merid)]
    plane = (rows, cols)
    grid = (levels, cols)

    ring = [(i, (i + 1) % lons) for i in range(lons)]
    back = [(b, a) for a, b in ring]
    up = [(i, i + 1) for i in range(lats - 1)]
    down = [(b, a) for a, b in up]

    def to_lat(msgs, flip):
        routes = [up + down] if pair else [down, up]
        if not flip:
            return [lax.ppermute(m, "lat", r) for m, r in zip(msgs, routes)]
        both = [
            [(a * depths + d, b * depths + (depths - 1 - d)) for a, b in r for d in range(depths)] for r in routes
        ]
        return [lax.ppermute(m, ("lat", "depth"), r) for m, r in zip(msgs, both)]

    def to_depth(msg):
        return lax.ppermute(msg, "depth", [(d, depths - 1 - d) for d in range(depths)])

    to_east, to_west, late, *lat_msgs = call(
        functools.partial(pack_kernel, dims),
        [((4,) + plane, f32), ((3,) + plane, f32), (grid, f32)] + [((7,) + grid, f32)] * count,
        (ids, *state, sea, east, north, flags, block_inverse),
        name="pack",
    )
    row_const = to_lat(lat_msgs, False)
    west_const = lax.ppermute(to_east, "lon", ring)
    east_const = lax.ppermute(to_west, "lon", back)
    row_new, west, east_in = row_const, west_const, east_const

    for step in reversed(range(STEPS)):
        first = step == STEPS - 1
        outs = [((4, n, cols), f32), ((7,) + plane, f32)] + [(plane, f32)] * count
        if first:
            outs += [((n, cols), f32)] + [((n, n), bf16)] * 2 + [((rows * cols, cols), bf16)] * 2 + [(plane, f32)]
            args = (ids, *state, sea, block_inverse, coupling)
            smem = (0, 7)
            scratch = (pltpu.VMEM((n, levels), f32), pltpu.VMEM((rows, cols, cols), f32))
        else:
            args = (ids, *state, sea, coupling, spike, w_high, w_low)
            smem = (0, 6)
            scratch = ()
        proj, planes, *more = call(
            functools.partial(project_kernel, dims, first), outs, args, smem, scratch, name="project"
        )
        far_msgs = more[:count]
        if first:
            spike, w_high, w_low, p_high, p_low, spike_packed = more[count:]
        row_far = to_lat(far_msgs, True)
        mine, side_proj = call(
            functools.partial(side_kernel, dims),
            [((8,) + plane, f32), ((4,) + plane, f32)],
            (ids, west, east_in, west_const, east_const, planes, spike, spike_packed, p_high, p_low),
            name="sides",
        )
        theirs = to_depth(mine)
        final = step == 0
        state_shape = [((n, cols), f32)] * 4
        if final:
            outs, extra = state_shape, ()
        else:
            outs = state_shape + [((2,) + plane, f32)] * 2 + [((5,) + grid, f32)] * count
            extra = (late,)
        result = call(
            functools.partial(stencil_kernel, dims, step, final),
            outs,
            (
                ids, coupling, proj, spike, spike_packed, mine, theirs, side_proj, west_const, east_const,
                sea, east, north, flags, *row_new, *row_const, *row_new, *row_far, *extra,
            ),
            (0, 1),
            (
                pltpu.VMEM((4,) + grid, f32),
                pltpu.VMEM((4,) + grid, f32),
                pltpu.VMEM(grid, f32),
                pltpu.VMEM(grid, f32),
                pltpu.VMEM((5,) + grid, f32),
                pltpu.VMEM((4,) + plane, f32),
            ),
            name="stencil",
        )
        state = result[:4]
        if not final:
            row_new = to_lat(result[6:], False)
            west = lax.ppermute(result[4], "lon", ring)
            east_in = lax.ppermute(result[5], "lon", back)
    return tuple(x.reshape(levels, rows, cols) for x in state)


def solution(mesh):
    in_specs = (
        P("depth", "lat", "lon"),
        P("depth", "lat", "lon"),
        P("depth", "lat", "lon"),
        P("depth", "lat", "lon"),
        P("depth", "lat", "lon"),
        P("depth", "lat", "lon"),
        P(None, "depth", "lat", "lon"),
        P("depth", "lat", "lon"),
        P("lat", "depth", None),
        P("lat"),
    )
    out_specs = (
        P("depth", "lat", "lon"),
        P("depth", "lat", "lon"),
        P("depth", "lat", "lon"),
        P("depth", "lat", "lon"),
    )
    return jax.shard_map(
        on_device, mesh=mesh, in_specs=in_specs, out_specs=out_specs, check_vma=False
    )
```

```python
import functools

import jax
import jax.numpy as jnp
from jax import lax
from jax.experimental import pallas as pl
from jax.experimental.pallas import tpu as pltpu
from jax.sharding import PartitionSpec as P

STEPS = 2

advect_scale = 0.25
diffusion = 0.5
gravity = 0.1
pressure_scale = 1.0
viscosity = 0.1
haline = 0.8

BLOCK = 48
VMEM_BYTES = 12 * 1024 * 1024
f32 = jnp.float32
bf16 = jnp.bfloat16
CORNER_LANE = 16


def split(value):
    high = value.astype(bf16)
    return high, (value - high.astype(f32)).astype(bf16)


def dot(a, b, contract=((1,), (0,))):
    return lax.dot_general(a, b, (contract, ((), ())), preferred_element_type=f32)


def dot3(a, b):
    return dot(a[0], b[0]) + (dot(a[0], b[1]) + dot(a[1], b[0]))


def iota(shape, dim):
    return lax.broadcasted_iota(jnp.int32, shape, dim)


def branches(flags):
    one = jnp.where(flags >= 3, 1, 0) + jnp.where(flags >= 6, 1, 0)
    zonal = (flags - 3 * one).astype(f32) * 0.5
    return zonal, one.astype(f32) * 0.5


def lane_of(value, lane):
    return jnp.broadcast_to(value[:, lane : lane + 1], value.shape)


def level_at(k, rows):
    return pl.ds(k * rows if isinstance(k, int) else pl.multiple_of(k * rows, rows), rows)


def level(ref, k, rows):
    return ref[level_at(k, rows), :]


def turn(value, shift):
    return pltpu.roll(value, shift % value.shape[1], 1)


def each_level(levels, body, carry):
    block = min(BLOCK, levels)

    def some(b, carry):
        for i in range(block):
            carry = body(b * block + i, carry)
        return carry

    if block == levels:
        return some(0, carry)
    return lax.fori_loop(0, levels // block, some, carry)


def take_row(ref, row, levels, rows):
    if isinstance(row, int):
        return ref[pl.ds(row, levels, stride=rows), :]
    low = ref[pl.ds(0, levels, stride=rows), :]
    high = ref[pl.ds(rows - 1, levels, stride=rows), :]
    return jnp.where(row == 0, low, high)


def row_choices(pair, rows, lat):
    return [jnp.where(lat == 0, rows - 1, 0)] if pair else [0, rows - 1]


def pack_kernel(dims, ids, *refs):
    levels, rows, cols, half, pair = dims
    sources, (to_east, to_west, nn_late), rest = refs[:9], refs[9:12], refs[12:]
    count = 1 if pair else 2
    lat_msgs, copies, sems = rest[:count], rest[count : count + 9], rest[-1]
    moves = [pltpu.make_async_copy(a, b, sems.at[i]) for i, (a, b) in enumerate(zip(sources, copies))]
    for move in moves:
        move.start()
    t, s, u, v, sea, east, north, flags, inverse = copies
    lane = iota((rows, cols), 1)
    fields = (t, s, u, v)
    for move in moves:
        move.wait()

    def one(k, accs):
        accs = list(accs)
        here = [level(x, k, rows) for x in (*fields, sea, east, flags.at[1], flags.at[0])]
        at = lane == k, lane == k + half
        for j, value in enumerate(here):
            accs[j // 2 if j < 4 else j - 2] = jnp.where(
                at[j % 2 if j < 4 else 0],
                turn(value, k + (j % 2 if j < 4 else 0) * half + 1),
                accs[j // 2 if j < 4 else j - 2],
            )
        for j, value in enumerate(here[:5]):
            accs[6 + j // 2] = jnp.where(at[j % 2], turn(value, k + (j % 2) * half), accs[6 + j // 2])
        return tuple(accs)

    zero, none = jnp.zeros((rows, cols), f32), jnp.zeros((rows, cols), jnp.int32)
    accs = each_level(levels, one, (zero, zero, none, zero, none, none, zero, zero, none))
    wet, speed = accs[2].astype(f32), accs[3]
    nexts = [wet * (speed * branches(flag)[0] - diffusion) for flag in accs[4:6]]
    to_east[0], to_east[1] = accs[0], accs[1]
    to_east[2] = jnp.where(lane < half, wet, turn(nexts[0], half))
    to_east[3] = nexts[1]
    to_west[0], to_west[1] = accs[6], accs[7]
    to_west[2] = accs[8].astype(f32)
    for which, row in enumerate(row_choices(pair, rows, ids[0])):
        msg = lat_msgs[which]
        for j, x in enumerate(fields):
            msg[j] = take_row(x, row, levels, rows)
        wet = take_row(sea, row, levels, rows).astype(f32)
        speed = take_row(north, row, levels, rows)
        msg[4] = wet
        for step in (1, 0):
            _, merid = branches(take_row(flags.at[step], row, levels, rows))
            value = wet * (speed * merid - diffusion)
            if step:
                msg[5] = value
            elif pair or row:
                nn_late[...] = value
        msg[6] = jnp.zeros((levels, cols), f32)
        if pair:
            block = jnp.where(row == 0, inverse[0], inverse[rows - 1])
        else:
            block = inverse[row]
        msg[6, :, pl.ds(0, levels)] = block


def coef_kernel(dims, sea, east, north, flags, west_const, east_const, out):
    levels, rows, cols, half, pair = dims
    lane, row = iota((rows, cols), 1), iota((rows, cols), 0)
    sea_side = east_const[2]
    sides = (west_const[3], west_const[2])

    def one(k, carry):
        wet = level(sea, k, rows).astype(f32)
        part = advect_scale * wet
        speed_e, speed_n = level(east, k, rows), level(north, k, rows)
        sea_east = jnp.where(lane == cols - 1, turn(sea_side, cols - 1 - k), turn(wet, cols - 1))
        sea_north = jnp.where(row == rows - 1, 1.0, pltpu.roll(wet, rows - 1, 0))
        here = level_at(k, rows)
        for step in (1, 0):
            zonal, merid = branches(level(flags.at[step], k, rows))
            speed_z, speed_m = speed_e * zonal, speed_n * merid
            out[step, 0, here, :] = part * (speed_e - speed_z + diffusion) * sea_east
            next_west = jnp.where(
                lane == 0, turn(sides[step], 2 * cols - step * half - k), turn(wet * (speed_z - diffusion), 1)
            )
            out[step, 1, here, :] = part * next_west
            out[step, 2, here, :] = part * (speed_n - speed_m + diffusion) * sea_north
            next_south = jnp.where(row == 0, 1.0, pltpu.roll(wet * (speed_m - diffusion), 1, 0))
            out[step, 3, here, :] = part * next_south
        return carry

    each_level(levels, one, ())


def project_kernel(dims, setup, ids, t, s, u, v, sea, *rest):
    levels, rows, cols, half, pair = dims
    if setup:
        inverse, coup, proj, planes, *rest = rest
        lat_out, (spike, w_high, w_low, p_high, p_low, spike_packed, corner, b_plane, cells, wide) = rest[:-10], rest[-10:]
        n = levels * rows
        for y in range(rows):
            cells[pl.ds(y, levels, stride=rows), :] = inverse[y]
        pieces = split(cells[...])
        pick = (iota((n, levels), 0) // rows == iota((n, levels), 1)).astype(bf16)
        same = (iota((n, n), 0) % rows) == (iota((n, n), 1) % rows)
        for piece, out in zip(pieces, (w_high, w_low)):
            full = dot(pick, piece, ((1,), (1,)))
            out[...] = jnp.where(same, full, 0.0).astype(bf16)
        wide[...] = jnp.zeros_like(wide)
        for y in range(rows):
            wide[y, pl.ds(0, levels), pl.ds(0, levels)] = inverse[y]
            wide[y, pl.ds(half, levels), pl.ds(half, levels)] = inverse[y]
        high, low = split(wide[...].reshape(rows * cols, cols))
        p_high[...] = high
        p_low[...] = low
        spike_packed[...] = jnp.zeros_like(spike_packed)
        for y in range(rows):
            line = inverse[y, pl.ds(ids[2], 1), :]
            spike_packed[pl.ds(y, 1), pl.ds(0, levels)] = line
            spike_packed[pl.ds(y, 1), pl.ds(half, levels)] = line
    else:
        coup, corner, b_plane, w_high, w_low, proj, planes, *lat_out = rest
    w = (w_high[...], w_low[...])
    for f, (x, y) in enumerate(((t, s), (u, v))):
        both = dot3(w, split(jnp.concatenate([x[...], y[...]], axis=1)))
        proj[2 * f] = both[:, :cols]
        proj[2 * f + 1] = both[:, cols:]
    edge = pl.ds(pl.multiple_of(ids[2] * rows, rows), rows)
    zero = jnp.zeros((rows, cols), f32)
    if setup:
        n = levels * rows
        pick = (iota((n, cols), 0) // rows == ids[2]).astype(bf16)
        spike[...] = dot(w[0], pick) + dot(w[1], pick)
        corner[...] = spike[edge, :]
    for f in range(4):
        planes[f] = proj[f, edge, :]

    def one(k, sums):
        here = level_at(k, rows)
        wet = sea[here, :].astype(f32)
        values = [wet * proj[f, here, :] for f in range(4)]
        for f in range(4):
            proj[f, here, :] = values[f]
        sums = [sums[0] + values[2], sums[1] + values[3], *sums[2:]]
        if setup:
            value = wet * spike[here, :]
            spike[here, :] = value
            sums[2] = sums[2] + value
        return tuple(sums)

    sums = each_level(levels, one, (zero,) * (3 if setup else 2))
    if setup:
        b_plane[...] = sums[2]
    sums = [sums[0], sums[1], b_plane[...]]
    for j in range(3):
        planes[4 + j] = sums[j]
    lane_row = iota((rows, cols), 0)
    coupled = jnp.zeros((rows, cols), f32)
    for y in range(rows):
        coupled = jnp.where(lane_row == y, coup[y], coupled)
    lines = [planes[f] for f in range(4)] + [sums[1], sums[2], corner[...], coupled]
    for which, row in enumerate(row_choices(pair, rows, ids[0])):
        for j, value in enumerate(lines):
            if pair:
                line = jnp.where(row == 0, value[0:1], value[rows - 1 : rows])
            else:
                line = value[row : row + 1]
            lat_out[which][pl.ds(j, 1), :] = line


def side_kernel(dims, ids, west, east, west_sea, east_sea, planes, corner, spike_packed, p_high, p_low, msg, proj):
    levels, rows, cols, half, pair = dims
    lane = iota((rows, cols), 1)
    row = iota((rows, cols), 0)
    packed = (west[0], west[1], east[0], east[1])
    chunks = []
    for y in range(rows):
        chunks.append(jnp.concatenate([jnp.where(row == y, x, 0.0) for x in packed], axis=0))
    lhs = jnp.concatenate(chunks, axis=1)
    out = dot3(split(lhs), (p_high[...], p_low[...]))
    for j in range(4):
        proj[j] = out[j * rows : (j + 1) * rows]
    for j in range(7):
        msg[j] = planes[j]
    edge = ids[2]
    misc = jnp.zeros((rows, cols), f32)
    spk = spike_packed[...]
    for side, wet in enumerate((west_sea, east_sea)):
        wet = jnp.where(lane < half, wet[2], 0.0)
        for p in range(2):
            value = out[(2 * side + p) * rows : (2 * side + p + 1) * rows]
            for i in range(2):
                column = jnp.sum(jnp.where(lane == edge + i * half, value, 0.0), axis=1, keepdims=True)
                misc = jnp.where(lane == side * 8 + 2 * p + i, column, misc)
            if p == 1:
                column = jnp.sum(wet * value, axis=1, keepdims=True)
                misc = jnp.where(lane == side * 8 + 4, column, misc)
        column = jnp.sum(wet * spk, axis=1, keepdims=True)
        misc = jnp.where(lane == side * 8 + 5, column, misc)
    msg[7] = jnp.where(lane == CORNER_LANE, corner[...], misc)


def stencil_kernel(dims, step, final, ids, coup, proj, spike, spike_packed, mine, theirs, side_proj,
                   west_const, east_const, coef, *rest):
    levels, rows, cols, half, pair = dims
    count = 1 if pair else 2
    row_new, row_const, row_late, row_far = (rest[i * count : (i + 1) * count] for i in range(4))
    rest = rest[4 * count :]
    if final:
        outs, rest = rest[:4], rest[4:]
    else:
        late_out, rest = rest[0], rest[1:]
        outs, (to_east, to_west), rest = rest[:4], rest[4:6], rest[6:]
        lat_msgs, rest = rest[:count], rest[count:]
    north_w, south_w, north_sea, south_next, line, sides = rest
    lat, depth, edge, parts = ids[0], ids[1], ids[2], ids[3]
    lane = iota((rows, cols), 1)
    row = iota((rows, cols), 0)
    has_north = jnp.where(lat < parts - 1, 1.0, 0.0)
    has_south = jnp.where(lat > 0, 1.0, 0.0)

    row_sums = []
    for h in range(count):
        block = split(row_const[h][6][:, :levels])
        eye = (iota((levels, levels), 0) == iota((levels, levels), 1)).astype(bf16)
        turned = tuple(dot(eye, piece, ((1,), (1,))).astype(bf16) for piece in block)
        pick = (iota((levels, cols), 0) == edge).astype(bf16)
        thin = dot(turned[0], pick) + dot(turned[1], pick)
        line[4] = thin
        for f in range(4):
            line[f] = dot3(turned, split(row_new[h][f]))
        at_edge = pl.ds(edge, 1)
        far = row_far[h]
        c = far[7:8, :]
        other_corner = far[6:7, :]
        own_corner = line[4, at_edge, :]
        scaled = c / (1.0 - c * c * own_corner * other_corner)
        wet = row_const[h][4]
        if pair:
            masks = ((north_w, has_north), (south_w, has_south))
        else:
            masks = ((north_w, has_north),) if h == 0 else ((south_w, has_south),)
        for f in range(4):
            carried = scaled * (far[f : f + 1, :] + c * other_corner * line[f, at_edge, :])
            value = wet * (line[f] + thin * carried)
            for target, mask in masks:
                target[f] = value * mask
        if pair or h == 0:
            north_sea[...] = wet * has_north
        if pair or h == 1:
            late = row_const[h][5] if step else row_late[h][4]
            south_next[...] = late * has_south
        theirs_v = scaled * (line[3, at_edge, :] + c * own_corner * far[3:4, :])
        row_sums.append(far[4:5, :] + far[5:6, :] * theirs_v)
    row_sum_north, row_sum_south = row_sums[0], row_sums[-1]

    c = jnp.zeros((rows, cols), f32)
    for y in range(rows):
        c = jnp.where(row == y, coup[y], c)
    own_corner = lane_of(mine[7], CORNER_LANE)
    other_corner = lane_of(theirs[7], CORNER_LANE)
    scaled = c / (1.0 - c * c * own_corner * other_corner)
    co, cm = c * other_corner, c * own_corner
    carried = [scaled * (theirs[f] + co * mine[f]) for f in range(4)]
    misc = theirs[7]
    carried_side = scaled * (misc + co * mine[7])
    theirs_side = scaled * (mine[7] + cm * misc)

    spk = spike_packed[...]
    for side, const in enumerate((west_const, east_const)):
        wet = jnp.where(lane < half, const[2], pltpu.roll(const[2], half, 1))
        for p in range(2):
            joined = jnp.where(
                lane < half,
                lane_of(carried_side, side * 8 + 2 * p),
                lane_of(carried_side, side * 8 + 2 * p + 1),
            )
            sides[2 * side + p] = wet * (side_proj[2 * side + p] + spk * joined)

    sum_u = theirs[4] + theirs[6] * (scaled * (mine[2] + cm * theirs[2]))
    sum_v = theirs[5] + theirs[6] * (scaled * (mine[3] + cm * theirs[3]))
    side_u = [lane_of(misc, q * 8 + 4) + lane_of(misc, q * 8 + 5) * lane_of(theirs_side, q * 8 + 2) for q in (0, 1)]

    def shifted(value, west_in, east_in, south_in, north_in):
        return (
            jnp.where(lane == 0, west_in, pltpu.roll(value, 1, 1)),
            jnp.where(lane == cols - 1, east_in, pltpu.roll(value, cols - 1, 1)),
            jnp.where(row == 0, south_in, pltpu.roll(value, 1, 0)),
            jnp.where(row == rows - 1, north_in, pltpu.roll(value, rows - 1, 0)),
        )

    west_u = jnp.where(lane == 0, side_u[0], pltpu.roll(sum_u, 1, 1))
    east_u = jnp.where(lane == cols - 1, side_u[1], pltpu.roll(sum_u, cols - 1, 1))
    south_v = jnp.where(row == 0, row_sum_south * has_south, pltpu.roll(sum_v, 1, 0))
    north_v = jnp.where(row == rows - 1, row_sum_north * has_north, pltpu.roll(sum_v, rows - 1, 0))
    upper = jnp.where(depth == 0, 1.0, 0.0)
    deeper = (west_u - east_u + south_v - north_v) * upper

    north_index = (lat * rows + row).astype(f32)
    coriolis = 0.2 + 0.6 * (north_index + 0.5) / (rows * parts).astype(f32)

    west_sides = (sides[0], sides[1])
    east_sides = (sides[2], sides[3])
    push = -0.5 * pressure_scale * gravity
    top, bottom = row == rows - 1, row == 0

    def one(j, carry):
        below, *accs = carry
        k = levels - 1 - j
        here = level_at(k, rows)
        one = pl.ds(k, 1)
        east_own, west_own = coef[step, 0, here, :], coef[step, 1, here, :]
        north_own = coef[step, 2, here, :] * jnp.where(top, north_sea[one, :], 1.0)
        south_own = coef[step, 3, here, :] * jnp.where(bottom, south_next[one, :], 1.0)
        spk_k = spike[here, :]
        solved, around = [], []
        for f in range(4):
            w = proj[f, here, :] + spk_k * carried[f]
            shift = (f % 2) * half
            solved.append(w)
            around.append(
                shifted(
                    w,
                    turn(west_sides[f // 2], 2 * cols - shift - k),
                    turn(east_sides[f // 2], 2 * cols - 1 - shift - k),
                    south_w[f, one, :],
                    north_w[f, one, :],
                )
            )
        below = below + ((around[2][0] - around[2][1]) + (around[3][2] - around[3][3]))
        buoyancy = push * below
        new = []
        for f in range(2):
            w, (ww, we, ws, wn) = solved[f], around[f]
            q = w + ((east_own * (we - w) + west_own * (w - ww)) + (north_own * (wn - w) + south_own * (w - ws)))
            new.append(q + buoyancy if f == 0 else q - haline * buoyancy)
        for f in (2, 3):
            w, (ww, we, ws, wn) = solved[f], around[f]
            spin = coriolis * solved[5 - f]
            centre = (1.0 - 4.0 * viscosity) * w
            centre = centre - spin if f == 2 else centre + spin
            new.append(centre + viscosity * ((we + ww) + (wn + ws)))
        for f in range(4):
            outs[f][here, :] = new[f]
        if not final:
            for f in range(4):
                place = k + (f % 2) * half
                there = lane == place
                accs[f // 2] = jnp.where(there, turn(new[f], place + 1), accs[f // 2])
                accs[2 + f // 2] = jnp.where(there, turn(new[f], place), accs[2 + f // 2])
        return (below, *accs)

    zero = jnp.zeros((rows, cols), f32)
    extra = () if final else (zero,) * 4
    _, *accs = each_level(levels, one, (deeper, *extra))
    if not final:
        for p in range(2):
            to_east[p] = accs[p]
            to_west[p] = accs[2 + p]
        for which, at in enumerate(row_choices(pair, rows, lat)):
            for f in range(4):
                lat_msgs[which][f] = take_row(outs[f], at, levels, rows)
            lat_msgs[which][4] = late_out[...]


def call(kernel, outs, args, smem=(0,), scratch=(), name=None, hbm=()):
    places = [pltpu.SMEM if i in smem else pltpu.HBM if i in hbm else pltpu.VMEM for i in range(len(args))]
    specs = [pl.BlockSpec(memory_space=place) for place in places]
    return pl.pallas_call(
        kernel,
        out_shape=[jax.ShapeDtypeStruct(shape, kind) for shape, kind in outs],
        in_specs=specs,
        out_specs=[pl.BlockSpec(memory_space=pltpu.VMEM)] * len(outs),
        scratch_shapes=list(scratch),
        compiler_params=pltpu.CompilerParams(vmem_limit_bytes=VMEM_BYTES),
        name=name,
    )(*args)


def on_device(
    adj_temp,
    adj_salt,
    adj_zonal,
    adj_merid,
    east_speed,
    north_speed,
    branch_flags,
    sea_mask,
    block_inverse,
    coupling,
):
    levels, rows, cols = adj_temp.shape
    half = cols // 2
    lons, lats, depths = (lax.axis_size(a) for a in ("lon", "lat", "depth"))
    pair = lats == 2
    dims = (levels, rows, cols, half, pair)
    count = 1 if pair else 2
    n = levels * rows
    lat, depth = lax.axis_index("lat"), lax.axis_index("depth")
    ids = jnp.stack([lat, depth, (levels - 1) * (1 - depth), jnp.int32(lats)]).astype(jnp.int32)
    flat = lambda x: x.reshape(x.shape[:-3] + (n, cols))
    sea, east, north, flags = flat(sea_mask), flat(east_speed), flat(north_speed), flat(branch_flags)
    state = [flat(x) for x in (adj_temp, adj_salt, adj_zonal, adj_merid)]
    plane = (rows, cols)
    grid = (levels, cols)

    ring = [(i, (i + 1) % lons) for i in range(lons)]
    back = [(b, a) for a, b in ring]
    up = [(i, i + 1) for i in range(lats - 1)]
    down = [(b, a) for a, b in up]

    def to_lat(msgs, flip):
        routes = [up + down] if pair else [down, up]
        if not flip:
            return [lax.ppermute(m, "lat", r) for m, r in zip(msgs, routes)]
        both = [
            [(a * depths + d, b * depths + (depths - 1 - d)) for a, b in r for d in range(depths)] for r in routes
        ]
        return [lax.ppermute(m, ("lat", "depth"), r) for m, r in zip(msgs, both)]

    def to_depth(msg):
        return lax.ppermute(msg, "depth", [(d, depths - 1 - d) for d in range(depths)])

    sources = (*state, sea, east, north, flags, block_inverse)
    to_east, to_west, late, *rest = call(
        functools.partial(pack_kernel, dims),
        [((4,) + plane, f32), ((3,) + plane, f32), (grid, f32)]
        + [((7,) + grid, f32)] * count
        + [(x.shape, x.dtype) for x in sources],
        (ids, *sources),
        scratch=(pltpu.SemaphoreType.DMA((9,)),),
        name="pack",
        hbm=range(1, 10),
    )
    lat_msgs, rest = rest[:count], rest[count:]
    state, (sea, east, north, flags, block_inverse) = rest[:4], rest[4:]
    row_const = to_lat(lat_msgs, False)
    west_const = lax.ppermute(to_east, "lon", ring)
    east_const = lax.ppermute(to_west, "lon", back)
    row_new, west, east_in = row_const, west_const, east_const

    for step in reversed(range(STEPS)):
        first = step == STEPS - 1
        outs = [((4, n, cols), f32), ((7,) + plane, f32)] + [(plane, f32)] * count
        if first:
            outs += [((n, cols), f32)] + [((n, n), bf16)] * 2 + [((rows * cols, cols), bf16)] * 2 + [(plane, f32)] * 3
            args = (ids, *state, sea, block_inverse, coupling)
            smem = (0, 7)
            scratch = (pltpu.VMEM((n, levels), f32), pltpu.VMEM((rows, cols, cols), f32))
        else:
            args = (ids, *state, sea, coupling, corner, b_plane, w_high, w_low)
            smem = (0, 6)
            scratch = ()
        proj, planes, *more = call(
            functools.partial(project_kernel, dims, first), outs, args, smem, scratch, name="project"
        )
        far_msgs = more[:count]
        if first:
            spike, w_high, w_low, p_high, p_low, spike_packed, corner, b_plane = more[count:]
        row_far = to_lat(far_msgs, True)
        mine, side_proj = call(
            functools.partial(side_kernel, dims),
            [((8,) + plane, f32), ((4,) + plane, f32)],
            (ids, west, east_in, west_const, east_const, planes, corner, spike_packed, p_high, p_low),
            name="sides",
        )
        theirs = to_depth(mine)
        if first:
            (coef,) = call(
                functools.partial(coef_kernel, dims),
                [((STEPS, 4, n, cols), f32)],
                (sea, east, north, flags, west_const, east_const),
                (),
                name="coef",
            )
        final = step == 0
        state_shape = [((n, cols), f32)] * 4
        if final:
            outs, extra = state_shape, ()
        else:
            outs = state_shape + [((2,) + plane, f32)] * 2 + [((5,) + grid, f32)] * count
            extra = (late,)
        result = call(
            functools.partial(stencil_kernel, dims, step, final),
            outs,
            (
                ids, coupling, proj, spike, spike_packed, mine, theirs, side_proj, west_const, east_const,
                coef, *row_new, *row_const, *row_new, *row_far, *extra,
            ),
            (0, 1),
            (
                pltpu.VMEM((4,) + grid, f32),
                pltpu.VMEM((4,) + grid, f32),
                pltpu.VMEM(grid, f32),
                pltpu.VMEM(grid, f32),
                pltpu.VMEM((5,) + grid, f32),
                pltpu.VMEM((4,) + plane, f32),
            ),
            name="stencil",
        )
        state = result[:4]
        if not final:
            row_new = to_lat(result[6:], False)
            west = lax.ppermute(result[4], "lon", ring)
            east_in = lax.ppermute(result[5], "lon", back)
    return tuple(x.reshape(levels, rows, cols) for x in state)


def solution(mesh):
    in_specs = (
        P("depth", "lat", "lon"),
        P("depth", "lat", "lon"),
        P("depth", "lat", "lon"),
        P("depth", "lat", "lon"),
        P("depth", "lat", "lon"),
        P("depth", "lat", "lon"),
        P(None, "depth", "lat", "lon"),
        P("depth", "lat", "lon"),
        P("lat", "depth", None),
        P("lat"),
    )
    out_specs = (
        P("depth", "lat", "lon"),
        P("depth", "lat", "lon"),
        P("depth", "lat", "lon"),
        P("depth", "lat", "lon"),
    )
    return jax.shard_map(
        on_device, mesh=mesh, in_specs=in_specs, out_specs=out_specs, check_vma=False
    )
```

```python
import functools

import jax
import jax.numpy as jnp
from jax import lax
from jax.experimental import pallas as pl
from jax.experimental.pallas import tpu as pltpu
from jax.sharding import PartitionSpec as P

STEPS = 2

advect_scale = 0.25
diffusion = 0.5
gravity = 0.1
pressure_scale = 1.0
viscosity = 0.1
haline = 0.8

BLOCK = 48
VMEM_BYTES = 12 * 1024 * 1024
f32 = jnp.float32
bf16 = jnp.bfloat16
CORNER_LANE = 16


def split(value):
    high = value.astype(bf16)
    return high, (value - high.astype(f32)).astype(bf16)


def dot(a, b, contract=((1,), (0,))):
    return lax.dot_general(a, b, (contract, ((), ())), preferred_element_type=f32)


def dot3(a, b):
    return dot(a[0], b[0]) + (dot(a[0], b[1]) + dot(a[1], b[0]))


def iota(shape, dim):
    return lax.broadcasted_iota(jnp.int32, shape, dim)


def branches(flags):
    one = jnp.where(flags >= 3, 1, 0) + jnp.where(flags >= 6, 1, 0)
    zonal = (flags - 3 * one).astype(f32) * 0.5
    return zonal, one.astype(f32) * 0.5


def lane_of(value, lane):
    return jnp.broadcast_to(value[:, lane : lane + 1], value.shape)


def level_at(k, rows):
    return pl.ds(k * rows if isinstance(k, int) else pl.multiple_of(k * rows, rows), rows)


def level(ref, k, rows):
    return ref[level_at(k, rows), :]


def turn(value, shift):
    return pltpu.roll(value, shift % value.shape[1], 1)


def each_level(levels, body, carry):
    block = min(BLOCK, levels)

    def some(b, carry):
        for i in range(block):
            carry = body(b * block + i, carry)
        return carry

    if block == levels:
        return some(0, carry)
    return lax.fori_loop(0, levels // block, some, carry)


def take_row(ref, row, levels, rows):
    if isinstance(row, int):
        return ref[pl.ds(row, levels, stride=rows), :]
    low = ref[pl.ds(0, levels, stride=rows), :]
    high = ref[pl.ds(rows - 1, levels, stride=rows), :]
    return jnp.where(row == 0, low, high)


def row_choices(pair, rows, lat):
    return [jnp.where(lat == 0, rows - 1, 0)] if pair else [0, rows - 1]


def pack_kernel(dims, ids, *refs):
    levels, rows, cols, half, pair = dims
    sources, (to_east, to_west, nn_late), rest = refs[:9], refs[9:12], refs[12:]
    count = 1 if pair else 2
    lat_msgs, copies, sems = rest[:count], rest[count : count + 9], rest[-1]
    moves = [pltpu.make_async_copy(a, b, sems.at[i]) for i, (a, b) in enumerate(zip(sources, copies))]
    for move in moves:
        move.start()
    t, s, u, v, sea, east, north, flags, inverse = copies
    lane = iota((rows, cols), 1)
    fields = (t, s, u, v)
    for move in moves:
        move.wait()

    def one(k, accs):
        accs = list(accs)
        here = [level(x, k, rows) for x in (*fields, sea, east, flags.at[1], flags.at[0])]
        at = lane == k, lane == k + half
        for j, value in enumerate(here):
            accs[j // 2 if j < 4 else j - 2] = jnp.where(
                at[j % 2 if j < 4 else 0],
                turn(value, k + (j % 2 if j < 4 else 0) * half + 1),
                accs[j // 2 if j < 4 else j - 2],
            )
        for j, value in enumerate(here[:5]):
            accs[6 + j // 2] = jnp.where(at[j % 2], turn(value, k + (j % 2) * half), accs[6 + j // 2])
        return tuple(accs)

    zero, none = jnp.zeros((rows, cols), f32), jnp.zeros((rows, cols), jnp.int32)
    accs = each_level(levels, one, (zero, zero, none, zero, none, none, zero, zero, none))
    wet, speed = accs[2].astype(f32), accs[3]
    nexts = [wet * (speed * branches(flag)[0] - diffusion) for flag in accs[4:6]]
    to_east[0], to_east[1] = accs[0], accs[1]
    to_east[2] = jnp.where(lane < half, wet, turn(nexts[0], half))
    to_east[3] = nexts[1]
    to_west[0], to_west[1] = accs[6], accs[7]
    to_west[2] = accs[8].astype(f32)
    for which, row in enumerate(row_choices(pair, rows, ids[0])):
        msg = lat_msgs[which]
        for j, x in enumerate(fields):
            msg[j] = take_row(x, row, levels, rows)
        wet = take_row(sea, row, levels, rows).astype(f32)
        speed = take_row(north, row, levels, rows)
        msg[4] = wet
        for step in (1, 0):
            _, merid = branches(take_row(flags.at[step], row, levels, rows))
            value = wet * (speed * merid - diffusion)
            if step:
                msg[5] = value
            elif pair or row:
                nn_late[...] = value
        msg[6] = jnp.zeros((levels, cols), f32)
        if pair:
            block = jnp.where(row == 0, inverse[0], inverse[rows - 1])
        else:
            block = inverse[row]
        msg[6, :, pl.ds(0, levels)] = block


def coef_kernel(dims, sea, east, north, flags, west_const, east_const, out):
    levels, rows, cols, half, pair = dims
    lane, row = iota((rows, cols), 1), iota((rows, cols), 0)
    sea_side = east_const[2]
    sides = (west_const[3], west_const[2])

    def one(k, carry):
        wet = level(sea, k, rows).astype(f32)
        part = advect_scale * wet
        speed_e, speed_n = level(east, k, rows), level(north, k, rows)
        sea_east = jnp.where(lane == cols - 1, turn(sea_side, cols - 1 - k), turn(wet, cols - 1))
        sea_north = jnp.where(row == rows - 1, 1.0, pltpu.roll(wet, rows - 1, 0))
        here = level_at(k, rows)
        for step in (1, 0):
            zonal, merid = branches(level(flags.at[step], k, rows))
            speed_z, speed_m = speed_e * zonal, speed_n * merid
            out[step, 0, here, :] = part * (speed_e - speed_z + diffusion) * sea_east
            next_west = jnp.where(
                lane == 0, turn(sides[step], 2 * cols - step * half - k), turn(wet * (speed_z - diffusion), 1)
            )
            out[step, 1, here, :] = part * next_west
            out[step, 2, here, :] = part * (speed_n - speed_m + diffusion) * sea_north
            next_south = jnp.where(row == 0, 1.0, pltpu.roll(wet * (speed_m - diffusion), 1, 0))
            out[step, 3, here, :] = part * next_south
        return carry

    each_level(levels, one, ())


def project_kernel(dims, setup, ids, t, s, u, v, sea, *rest):
    levels, rows, cols, half, pair = dims
    if setup:
        inverse, coup, proj, planes, *rest = rest
        lat_out, (spike, w_high, w_low, p_high, p_low, spike_packed, corner, b_plane, cells, wide) = rest[:-10], rest[-10:]
        n = levels * rows
        for y in range(rows):
            cells[pl.ds(y, levels, stride=rows), :] = inverse[y]
        pieces = split(cells[...])
        pick = (iota((n, levels), 0) // rows == iota((n, levels), 1)).astype(bf16)
        same = (iota((n, n), 0) % rows) == (iota((n, n), 1) % rows)
        for piece, out in zip(pieces, (w_high, w_low)):
            full = dot(pick, piece, ((1,), (1,)))
            out[...] = jnp.where(same, full, 0.0).astype(bf16)
        wide[...] = jnp.zeros_like(wide)
        for y in range(rows):
            wide[y, pl.ds(0, levels), pl.ds(0, levels)] = inverse[y]
            wide[y, pl.ds(half, levels), pl.ds(half, levels)] = inverse[y]
        high, low = split(wide[...].reshape(rows * cols, cols))
        p_high[...] = high
        p_low[...] = low
        spike_packed[...] = jnp.zeros_like(spike_packed)
        for y in range(rows):
            line = inverse[y, pl.ds(ids[2], 1), :]
            spike_packed[pl.ds(y, 1), pl.ds(0, levels)] = line
            spike_packed[pl.ds(y, 1), pl.ds(half, levels)] = line
    else:
        coup, corner, b_plane, w_high, w_low, proj, planes, *lat_out = rest
    w = (w_high[...], w_low[...])
    for f, (x, y) in enumerate(((t, s), (u, v))):
        both = dot3(w, split(jnp.concatenate([x[...], y[...]], axis=1)))
        proj[2 * f] = both[:, :cols]
        proj[2 * f + 1] = both[:, cols:]
    edge = pl.ds(pl.multiple_of(ids[2] * rows, rows), rows)
    zero = jnp.zeros((rows, cols), f32)
    if setup:
        n = levels * rows
        pick = (iota((n, cols), 0) // rows == ids[2]).astype(bf16)
        spike[...] = dot(w[0], pick) + dot(w[1], pick)
        corner[...] = spike[edge, :]
    for f in range(4):
        planes[f] = proj[f, edge, :]

    def one(k, sums):
        here = level_at(k, rows)
        wet = sea[here, :].astype(f32)
        values = [wet * proj[f, here, :] for f in range(4)]
        for f in range(4):
            proj[f, here, :] = values[f]
        sums = [sums[0] + values[2], sums[1] + values[3], *sums[2:]]
        if setup:
            value = wet * spike[here, :]
            spike[here, :] = value
            sums[2] = sums[2] + value
        return tuple(sums)

    sums = each_level(levels, one, (zero,) * (3 if setup else 2))
    if setup:
        b_plane[...] = sums[2]
    sums = [sums[0], sums[1], b_plane[...]]
    for j in range(3):
        planes[4 + j] = sums[j]
    lane_row = iota((rows, cols), 0)
    coupled = jnp.zeros((rows, cols), f32)
    for y in range(rows):
        coupled = jnp.where(lane_row == y, coup[y], coupled)
    lines = [planes[f] for f in range(4)] + [sums[1], sums[2], corner[...], coupled]
    for which, row in enumerate(row_choices(pair, rows, ids[0])):
        for j, value in enumerate(lines):
            if pair:
                line = jnp.where(row == 0, value[0:1], value[rows - 1 : rows])
            else:
                line = value[row : row + 1]
            lat_out[which][pl.ds(j, 1), :] = line


def side_kernel(dims, ids, west, east, west_sea, east_sea, planes, corner, spike_packed, p_high, p_low, msg, proj):
    levels, rows, cols, half, pair = dims
    lane = iota((rows, cols), 1)
    row = iota((rows, cols), 0)
    packed = (west[0], west[1], east[0], east[1])
    chunks = []
    for y in range(rows):
        chunks.append(jnp.concatenate([jnp.where(row == y, x, 0.0) for x in packed], axis=0))
    lhs = jnp.concatenate(chunks, axis=1)
    out = dot3(split(lhs), (p_high[...], p_low[...]))
    for j in range(4):
        proj[j] = out[j * rows : (j + 1) * rows]
    for j in range(7):
        msg[j] = planes[j]
    edge = ids[2]
    misc = jnp.zeros((rows, cols), f32)
    spk = spike_packed[...]
    for side, wet in enumerate((west_sea, east_sea)):
        wet = jnp.where(lane < half, wet[2], 0.0)
        for p in range(2):
            value = out[(2 * side + p) * rows : (2 * side + p + 1) * rows]
            for i in range(2):
                column = jnp.sum(jnp.where(lane == edge + i * half, value, 0.0), axis=1, keepdims=True)
                misc = jnp.where(lane == side * 8 + 2 * p + i, column, misc)
            if p == 1:
                column = jnp.sum(wet * value, axis=1, keepdims=True)
                misc = jnp.where(lane == side * 8 + 4, column, misc)
        column = jnp.sum(wet * spk, axis=1, keepdims=True)
        misc = jnp.where(lane == side * 8 + 5, column, misc)
    msg[7] = jnp.where(lane == CORNER_LANE, corner[...], misc)


def stencil_kernel(dims, step, final, ids, coup, proj, spike, spike_packed, mine, theirs, side_proj,
                   west_const, east_const, coef, *rest):
    levels, rows, cols, half, pair = dims
    count = 1 if pair else 2
    row_new, row_const, row_late, row_far = (rest[i * count : (i + 1) * count] for i in range(4))
    rest = rest[4 * count :]
    if final:
        outs, rest = rest[:4], rest[4:]
    else:
        late_out, rest = rest[0], rest[1:]
        outs, (to_east, to_west), rest = rest[:4], rest[4:6], rest[6:]
        lat_msgs, rest = rest[:count], rest[count:]
    north_w, south_w, north_sea, south_next, line, sides = rest
    lat, depth, edge, parts = ids[0], ids[1], ids[2], ids[3]
    lane = iota((rows, cols), 1)
    row = iota((rows, cols), 0)
    has_north = jnp.where(lat < parts - 1, 1.0, 0.0)
    has_south = jnp.where(lat > 0, 1.0, 0.0)

    row_sums = []
    for h in range(count):
        block = split(row_const[h][6][:, :levels])
        eye = (iota((levels, levels), 0) == iota((levels, levels), 1)).astype(bf16)
        turned = tuple(dot(eye, piece, ((1,), (1,))).astype(bf16) for piece in block)
        pick = (iota((levels, cols), 0) == edge).astype(bf16)
        thin = dot(turned[0], pick) + dot(turned[1], pick)
        line[4] = thin
        for f in range(4):
            line[f] = dot3(turned, split(row_new[h][f]))
        at_edge = pl.ds(edge, 1)
        far = row_far[h]
        c = far[7:8, :]
        other_corner = far[6:7, :]
        own_corner = line[4, at_edge, :]
        scaled = c / (1.0 - c * c * own_corner * other_corner)
        wet = row_const[h][4]
        if pair:
            masks = ((north_w, has_north), (south_w, has_south))
        else:
            masks = ((north_w, has_north),) if h == 0 else ((south_w, has_south),)
        for f in range(4):
            carried = scaled * (far[f : f + 1, :] + c * other_corner * line[f, at_edge, :])
            value = wet * (line[f] + thin * carried)
            for target, mask in masks:
                target[f] = value * mask
        if pair or h == 0:
            north_sea[...] = wet * has_north
        if pair or h == 1:
            late = row_const[h][5] if step else row_late[h][4]
            south_next[...] = late * has_south
        theirs_v = scaled * (line[3, at_edge, :] + c * own_corner * far[3:4, :])
        row_sums.append(far[4:5, :] + far[5:6, :] * theirs_v)
    row_sum_north, row_sum_south = row_sums[0], row_sums[-1]

    c = jnp.zeros((rows, cols), f32)
    for y in range(rows):
        c = jnp.where(row == y, coup[y], c)
    own_corner = lane_of(mine[7], CORNER_LANE)
    other_corner = lane_of(theirs[7], CORNER_LANE)
    scaled = c / (1.0 - c * c * own_corner * other_corner)
    co, cm = c * other_corner, c * own_corner
    carried = [scaled * (theirs[f] + co * mine[f]) for f in range(4)]
    misc = theirs[7]
    carried_side = scaled * (misc + co * mine[7])
    theirs_side = scaled * (mine[7] + cm * misc)

    spk = spike_packed[...]
    for side, const in enumerate((west_const, east_const)):
        wet = jnp.where(lane < half, const[2], pltpu.roll(const[2], half, 1))
        for p in range(2):
            joined = jnp.where(
                lane < half,
                lane_of(carried_side, side * 8 + 2 * p),
                lane_of(carried_side, side * 8 + 2 * p + 1),
            )
            sides[2 * side + p] = wet * (side_proj[2 * side + p] + spk * joined)

    sum_u = theirs[4] + theirs[6] * (scaled * (mine[2] + cm * theirs[2]))
    sum_v = theirs[5] + theirs[6] * (scaled * (mine[3] + cm * theirs[3]))
    side_u = [lane_of(misc, q * 8 + 4) + lane_of(misc, q * 8 + 5) * lane_of(theirs_side, q * 8 + 2) for q in (0, 1)]

    def shifted(value, west_in, east_in, south_in, north_in):
        return (
            jnp.where(lane == 0, west_in, pltpu.roll(value, 1, 1)),
            jnp.where(lane == cols - 1, east_in, pltpu.roll(value, cols - 1, 1)),
            jnp.where(row == 0, south_in, pltpu.roll(value, 1, 0)),
            jnp.where(row == rows - 1, north_in, pltpu.roll(value, rows - 1, 0)),
        )

    west_u = jnp.where(lane == 0, side_u[0], pltpu.roll(sum_u, 1, 1))
    east_u = jnp.where(lane == cols - 1, side_u[1], pltpu.roll(sum_u, cols - 1, 1))
    south_v = jnp.where(row == 0, row_sum_south * has_south, pltpu.roll(sum_v, 1, 0))
    north_v = jnp.where(row == rows - 1, row_sum_north * has_north, pltpu.roll(sum_v, rows - 1, 0))
    upper = jnp.where(depth == 0, 1.0, 0.0)
    deeper = (west_u - east_u + south_v - north_v) * upper

    north_index = (lat * rows + row).astype(f32)
    coriolis = 0.2 + 0.6 * (north_index + 0.5) / (rows * parts).astype(f32)

    west_sides = (sides[0], sides[1])
    east_sides = (sides[2], sides[3])
    push = -0.5 * pressure_scale * gravity
    top, bottom = row == rows - 1, row == 0

    def one(j, carry):
        below, *accs = carry
        k = levels - 1 - j
        here = level_at(k, rows)
        one = pl.ds(k, 1)
        east_own, west_own = coef[step, 0, here, :], coef[step, 1, here, :]
        north_own = coef[step, 2, here, :] * jnp.where(top, north_sea[one, :], 1.0)
        south_own = coef[step, 3, here, :] * jnp.where(bottom, south_next[one, :], 1.0)
        spk_k = spike[here, :]
        solved, around = [], []
        for f in range(4):
            w = proj[f, here, :] + spk_k * carried[f]
            shift = (f % 2) * half
            solved.append(w)
            around.append(
                shifted(
                    w,
                    turn(west_sides[f // 2], 2 * cols - shift - k),
                    turn(east_sides[f // 2], 2 * cols - 1 - shift - k),
                    south_w[f, one, :],
                    north_w[f, one, :],
                )
            )
        below = below + ((around[2][0] - around[2][1]) + (around[3][2] - around[3][3]))
        buoyancy = push * below
        new = []
        for f in range(2):
            w, (ww, we, ws, wn) = solved[f], around[f]
            q = w + ((east_own * (we - w) + west_own * (w - ww)) + (north_own * (wn - w) + south_own * (w - ws)))
            new.append(q + buoyancy if f == 0 else q - haline * buoyancy)
        for f in (2, 3):
            w, (ww, we, ws, wn) = solved[f], around[f]
            spin = coriolis * solved[5 - f]
            centre = (1.0 - 4.0 * viscosity) * w
            centre = centre - spin if f == 2 else centre + spin
            new.append(centre + viscosity * ((we + ww) + (wn + ws)))
        for f in range(4):
            outs[f][here, :] = new[f]
        if not final:
            for f in range(4):
                place = k + (f % 2) * half
                there = lane == place
                accs[f // 2] = jnp.where(there, turn(new[f], place + 1), accs[f // 2])
                accs[2 + f // 2] = jnp.where(there, turn(new[f], place), accs[2 + f // 2])
        return (below, *accs)

    zero = jnp.zeros((rows, cols), f32)
    extra = () if final else (zero,) * 4
    _, *accs = each_level(levels, one, (deeper, *extra))
    if not final:
        for p in range(2):
            to_east[p] = accs[p]
            to_west[p] = accs[2 + p]
        for which, at in enumerate(row_choices(pair, rows, lat)):
            for f in range(4):
                lat_msgs[which][f] = take_row(outs[f], at, levels, rows)
            lat_msgs[which][4] = late_out[...]


def call(kernel, outs, args, smem=(0,), scratch=(), name=None, hbm=()):
    places = [pltpu.SMEM if i in smem else pltpu.HBM if i in hbm else pltpu.VMEM for i in range(len(args))]
    specs = [pl.BlockSpec(memory_space=place) for place in places]
    return pl.pallas_call(
        kernel,
        out_shape=[jax.ShapeDtypeStruct(shape, kind) for shape, kind in outs],
        in_specs=specs,
        out_specs=[pl.BlockSpec(memory_space=pltpu.VMEM)] * len(outs),
        scratch_shapes=list(scratch),
        compiler_params=pltpu.CompilerParams(vmem_limit_bytes=VMEM_BYTES),
        name=name,
    )(*args)


def on_device(
    adj_temp,
    adj_salt,
    adj_zonal,
    adj_merid,
    east_speed,
    north_speed,
    branch_flags,
    sea_mask,
    block_inverse,
    coupling,
):
    levels, rows, cols = adj_temp.shape
    half = cols // 2
    lons, lats, depths = (lax.axis_size(a) for a in ("lon", "lat", "depth"))
    pair = lats == 2
    dims = (levels, rows, cols, half, pair)
    count = 1 if pair else 2
    n = levels * rows
    lat, depth = lax.axis_index("lat"), lax.axis_index("depth")
    ids = jnp.stack([lat, depth, (levels - 1) * (1 - depth), jnp.int32(lats)]).astype(jnp.int32)
    flat = lambda x: x.reshape(x.shape[:-3] + (n, cols))
    sea, east, north, flags = flat(sea_mask), flat(east_speed), flat(north_speed), flat(branch_flags)
    state = [flat(x) for x in (adj_temp, adj_salt, adj_zonal, adj_merid)]
    plane = (rows, cols)
    grid = (levels, cols)

    ring = [(i, (i + 1) % lons) for i in range(lons)]
    back = [(b, a) for a, b in ring]
    up = [(i, i + 1) for i in range(lats - 1)]
    down = [(b, a) for a, b in up]

    def to_lat(msgs, flip):
        routes = [up + down] if pair else [down, up]
        if not flip:
            return [lax.ppermute(m, "lat", r) for m, r in zip(msgs, routes)]
        both = [
            [(a * depths + d, b * depths + (depths - 1 - d)) for a, b in r for d in range(depths)] for r in routes
        ]
        return [lax.ppermute(m, ("lat", "depth"), r) for m, r in zip(msgs, both)]

    def to_depth(msg):
        return lax.ppermute(msg, "depth", [(d, depths - 1 - d) for d in range(depths)])

    sources = (*state, sea, east, north, flags, block_inverse)
    sources = tuple(pltpu.with_memory_space_constraint(x, pltpu.HBM) for x in sources)
    to_east, to_west, late, *rest = call(
        functools.partial(pack_kernel, dims),
        [((4,) + plane, f32), ((3,) + plane, f32), (grid, f32)]
        + [((7,) + grid, f32)] * count
        + [(x.shape, x.dtype) for x in sources],
        (ids, *sources),
        scratch=(pltpu.SemaphoreType.DMA((9,)),),
        name="pack",
        hbm=range(1, 10),
    )
    lat_msgs, rest = rest[:count], rest[count:]
    state, (sea, east, north, flags, block_inverse) = rest[:4], rest[4:]
    row_const = to_lat(lat_msgs, False)
    west_const = lax.ppermute(to_east, "lon", ring)
    east_const = lax.ppermute(to_west, "lon", back)
    row_new, west, east_in = row_const, west_const, east_const

    for step in reversed(range(STEPS)):
        first = step == STEPS - 1
        outs = [((4, n, cols), f32), ((7,) + plane, f32)] + [(plane, f32)] * count
        if first:
            outs += [((n, cols), f32)] + [((n, n), bf16)] * 2 + [((rows * cols, cols), bf16)] * 2 + [(plane, f32)] * 3
            args = (ids, *state, sea, block_inverse, coupling)
            smem = (0, 7)
            scratch = (pltpu.VMEM((n, levels), f32), pltpu.VMEM((rows, cols, cols), f32))
        else:
            args = (ids, *state, sea, coupling, corner, b_plane, w_high, w_low)
            smem = (0, 6)
            scratch = ()
        proj, planes, *more = call(
            functools.partial(project_kernel, dims, first), outs, args, smem, scratch, name="project"
        )
        far_msgs = more[:count]
        if first:
            spike, w_high, w_low, p_high, p_low, spike_packed, corner, b_plane = more[count:]
        row_far = to_lat(far_msgs, True)
        mine, side_proj = call(
            functools.partial(side_kernel, dims),
            [((8,) + plane, f32), ((4,) + plane, f32)],
            (ids, west, east_in, west_const, east_const, planes, corner, spike_packed, p_high, p_low),
            name="sides",
        )
        theirs = to_depth(mine)
        if first:
            (coef,) = call(
                functools.partial(coef_kernel, dims),
                [((STEPS, 4, n, cols), f32)],
                (sea, east, north, flags, west_const, east_const),
                (),
                name="coef",
            )
        final = step == 0
        state_shape = [((n, cols), f32)] * 4
        if final:
            outs, extra = state_shape, ()
        else:
            outs = state_shape + [((2,) + plane, f32)] * 2 + [((5,) + grid, f32)] * count
            extra = (late,)
        result = call(
            functools.partial(stencil_kernel, dims, step, final),
            outs,
            (
                ids, coupling, proj, spike, spike_packed, mine, theirs, side_proj, west_const, east_const,
                coef, *row_new, *row_const, *row_new, *row_far, *extra,
            ),
            (0, 1),
            (
                pltpu.VMEM((4,) + grid, f32),
                pltpu.VMEM((4,) + grid, f32),
                pltpu.VMEM(grid, f32),
                pltpu.VMEM(grid, f32),
                pltpu.VMEM((5,) + grid, f32),
                pltpu.VMEM((4,) + plane, f32),
            ),
            name="stencil",
        )
        state = result[:4]
        if not final:
            row_new = to_lat(result[6:], False)
            west = lax.ppermute(result[4], "lon", ring)
            east_in = lax.ppermute(result[5], "lon", back)
    return tuple(x.reshape(levels, rows, cols) for x in state)


def solution(mesh):
    in_specs = (
        P("depth", "lat", "lon"),
        P("depth", "lat", "lon"),
        P("depth", "lat", "lon"),
        P("depth", "lat", "lon"),
        P("depth", "lat", "lon"),
        P("depth", "lat", "lon"),
        P(None, "depth", "lat", "lon"),
        P("depth", "lat", "lon"),
        P("lat", "depth", None),
        P("lat"),
    )
    out_specs = (
        P("depth", "lat", "lon"),
        P("depth", "lat", "lon"),
        P("depth", "lat", "lon"),
        P("depth", "lat", "lon"),
    )
    return jax.shard_map(
        on_device, mesh=mesh, in_specs=in_specs, out_specs=out_specs, check_vma=False
    )
```

```python
import functools

import jax
import jax.numpy as jnp
from jax import lax
from jax.experimental import pallas as pl
from jax.experimental.pallas import tpu as pltpu
from jax.sharding import PartitionSpec as P

STEPS = 2

advect_scale = 0.25
diffusion = 0.5
gravity = 0.1
pressure_scale = 1.0
viscosity = 0.1
haline = 0.8

BLOCK = 48
VMEM_BYTES = 16 * 1024 * 1024
f32 = jnp.float32
bf16 = jnp.bfloat16
CORNER_LANE = 16


def split(value):
    high = value.astype(bf16)
    return high, (value - high.astype(f32)).astype(bf16)


def dot(a, b, contract=((1,), (0,))):
    return lax.dot_general(a, b, (contract, ((), ())), preferred_element_type=f32)


def dot3(a, b):
    return dot(a[0], b[0]) + (dot(a[0], b[1]) + dot(a[1], b[0]))


def iota(shape, dim):
    return lax.broadcasted_iota(jnp.int32, shape, dim)


def branches(flags):
    one = jnp.where(flags >= 3, 1, 0) + jnp.where(flags >= 6, 1, 0)
    zonal = (flags - 3 * one).astype(f32) * 0.5
    return zonal, one.astype(f32) * 0.5


def lane_of(value, lane):
    return jnp.broadcast_to(value[:, lane : lane + 1], value.shape)


def level_at(k, rows):
    return pl.ds(k * rows if isinstance(k, int) else pl.multiple_of(k * rows, rows), rows)


def level(ref, k, rows):
    return ref[level_at(k, rows), :]


def turn(value, shift):
    return pltpu.roll(value, shift % value.shape[1], 1)


def each_level(levels, body, carry):
    block = min(BLOCK, levels)

    def some(b, carry):
        for i in range(block):
            carry = body(b * block + i, carry)
        return carry

    if block == levels:
        return some(0, carry)
    return lax.fori_loop(0, levels // block, some, carry)


def take_row(ref, row, levels, rows):
    if isinstance(row, int):
        return ref[pl.ds(row, levels, stride=rows), :]
    low = ref[pl.ds(0, levels, stride=rows), :]
    high = ref[pl.ds(rows - 1, levels, stride=rows), :]
    return jnp.where(row == 0, low, high)


def row_choices(pair, rows, lat):
    return [jnp.where(lat == 0, rows - 1, 0)] if pair else [0, rows - 1]


def pack_kernel(dims, ids, *refs):
    levels, rows, cols, half, pair = dims
    sources, (to_east, to_west, nn_late), rest = refs[:9], refs[9:12], refs[12:]
    count = 1 if pair else 2
    lat_msgs, copies, sems = rest[:count], rest[count : count + 9], rest[-1]
    moves = [pltpu.make_async_copy(a, b, sems.at[i]) for i, (a, b) in enumerate(zip(sources, copies))]
    for move in moves:
        move.start()
    t, s, u, v, sea, east, north, flags, inverse = copies
    lane = iota((rows, cols), 1)
    fields = (t, s, u, v)
    for move in moves:
        move.wait()
    pairs = ((t, s, 2), (u, v, 2), (sea, east, 2), (flags.at[1], flags.at[0], 1))
    packed = [edge_columns(levels, rows, x, y, pieces) for x, y, pieces in pairs]
    for j in range(2):
        to_east[j], to_west[j] = packed[j]
    wet_speed, flag = packed[2][0], packed[3][0]
    wet, speed = wet_speed, turn(wet_speed, half)
    zonal = branches(jnp.round(flag).astype(jnp.int32))[0]
    nexts = [wet * (speed * z - diffusion) for z in (zonal, turn(zonal, half))]
    to_east[2] = jnp.where(lane < half, wet, turn(nexts[0], half))
    to_east[3] = nexts[1]
    to_west[2] = packed[2][1]
    for which, row in enumerate(row_choices(pair, rows, ids[0])):
        msg = lat_msgs[which]
        for j, x in enumerate(fields):
            msg[j] = take_row(x, row, levels, rows)
        wet = take_row(sea, row, levels, rows).astype(f32)
        speed = take_row(north, row, levels, rows)
        msg[4] = wet
        for step in (1, 0):
            _, merid = branches(take_row(flags.at[step], row, levels, rows))
            value = wet * (speed * merid - diffusion)
            if step:
                msg[5] = value
            elif pair or row:
                nn_late[...] = value
        msg[6] = jnp.zeros((levels, cols), f32)
        if pair:
            block = jnp.where(row == 0, inverse[0], inverse[rows - 1])
        else:
            block = inverse[row]
        msg[6, :, pl.ds(0, levels)] = block


def edge_columns(levels, rows, x, y, pieces):
    cols = x.shape[1]
    half = cols // 2
    source, target = iota((2 * cols, 2 * cols), 0), iota((2 * cols, 2 * cols), 1)
    column = jnp.where(target < cols, cols - 1, 0) + jnp.where(target % cols < half, 0, cols)
    spread = (source == column).astype(bf16)
    both = jnp.concatenate([x[...].astype(f32), y[...].astype(f32)], axis=1)
    high, low = split(both)
    wide = dot(high, spread)
    if pieces == 2:
        wide = wide + dot(low, spread)
    place = iota((rows, 2 * cols), 1) % half
    out = jnp.zeros((rows, 2 * cols), f32)
    for k in range(levels):
        out = jnp.where(place == k, wide[k * rows : (k + 1) * rows], out)
    return out[:, :cols], out[:, cols:]


def insert(lane, value, west_in, east_in):
    cols = value.shape[1]
    return (
        jnp.where(lane == 0, west_in, turn(value, 1)),
        jnp.where(lane == cols - 1, east_in, turn(value, cols - 1)),
    )


def inner(row, value):
    rows = value.shape[0]
    return (
        jnp.where(row == 0, 0.0, pltpu.roll(value, 1, 0)),
        jnp.where(row == rows - 1, 0.0, pltpu.roll(value, rows - 1, 0)),
    )


def coef_kernel(dims, sea, east, north, flags, west_const, east_const, spike, spike_packed, out, factor, beside):
    levels, rows, cols, half, pair = dims
    lane, row = iota((rows, cols), 1), iota((rows, cols), 0)
    sea_side = east_const[2]
    sides = (west_const[3], west_const[2])

    spk = spike_packed[...]
    spike_west = jnp.where(lane < half, west_const[2], 0.0) * spk
    spike_east = jnp.where(lane < half, east_const[2], 0.0) * spk

    def one(k, carry):
        wet = level(sea, k, rows).astype(f32)
        part = advect_scale * wet
        speed_e, speed_n = level(east, k, rows), level(north, k, rows)
        sea_east = jnp.where(lane == cols - 1, turn(sea_side, cols - 1 - k), turn(wet, cols - 1))
        sea_north = jnp.where(row == rows - 1, 1.0, pltpu.roll(wet, rows - 1, 0))
        here = level_at(k, rows)
        mid = level(spike, k, rows)
        west, east_ = insert(lane, mid, turn(spike_west, cols - k), turn(spike_east, cols - 1 - k))
        south, north_ = inner(row, mid)
        for j, value in enumerate((east_, west, north_, south)):
            beside[j, here, :] = value
        for step in (1, 0):
            zonal, merid = branches(level(flags.at[step], k, rows))
            speed_z, speed_m = speed_e * zonal, speed_n * merid
            east_own = part * (speed_e - speed_z + diffusion) * sea_east
            next_west = jnp.where(
                lane == 0, turn(sides[step], 2 * cols - step * half - k), turn(wet * (speed_z - diffusion), 1)
            )
            west_own = part * next_west
            north_own = part * (speed_n - speed_m + diffusion) * sea_north
            next_south = jnp.where(row == 0, 1.0, pltpu.roll(wet * (speed_m - diffusion), 1, 0))
            south_own = part * next_south
            for j, value in enumerate((east_own, west_own, north_own, south_own)):
                out[step, j, here, :] = value
            inside_n = jnp.where(row == rows - 1, 0.0, north_own)
            inside_s = jnp.where(row == 0, 0.0, south_own)
            factor[step, 0, here, :] = mid * (1.0 + ((west_own - east_own) + (inside_s - inside_n)))
            factor[step, 1, here, :] = east_own * east_
            factor[step, 2, here, :] = -west_own * west
            factor[step, 3, here, :] = inside_n * north_
            factor[step, 4, here, :] = -inside_s * south
        return carry

    each_level(levels, one, ())


def coriolis_of(dims, ids):
    levels, rows, cols, half, pair = dims
    index = (ids[0] * rows + iota((rows, cols), 0)).astype(f32)
    return 0.2 + 0.6 * (index + 0.5) / (rows * ids[3]).astype(f32)


def base_kernel(dims, step, ids, proj, side_proj, west_const, east_const, coef, out):
    levels, rows, cols, half, pair = dims
    lane, row = iota((rows, cols), 1), iota((rows, cols), 0)
    parts = []
    for p in range(2):
        line = []
        for side, const in enumerate((west_const, east_const)):
            wet = jnp.where(lane < half, const[2], turn(const[2], half))
            line.append(wet * side_proj[2 * side + p])
        parts.append(jnp.concatenate(line, axis=1))
    source, target = iota((2 * cols, 2 * cols), 0), iota((2 * cols, 2 * cols), 1)
    pick = target % cols
    wanted = pick // 2 + jnp.where(target < cols, 0, half) + jnp.where(pick % 2 == 1, 0, cols)
    spread = (source == wanted).astype(bf16)
    high, low = split(jnp.concatenate(parts, axis=0))
    mixed = dot(high, spread) + dot(low, spread)
    halo = [mixed[p * rows : (p + 1) * rows, i * cols : (i + 1) * cols] for p in range(2) for i in range(2)]
    coriolis = coriolis_of(dims, ids)
    push = -0.5 * pressure_scale * gravity
    top, bottom = row == rows - 1, row == 0

    def one(j, below):
        k = levels - 1 - j
        here = level_at(k, rows)
        east_own, west_own = coef[step, 0, here, :], coef[step, 1, here, :]
        north_own = jnp.where(top, 0.0, coef[step, 2, here, :])
        south_own = jnp.where(bottom, 0.0, coef[step, 3, here, :])
        mids, around = [], []
        for f in range(4):
            w = proj[f, here, :]
            mids.append(w)
            side = turn(halo[f], 2 * cols - 2 * k - 1)
            around.append((*insert(lane, w, side, side), *inner(row, w)))
        below = below + ((around[2][0] - around[2][1]) + (around[3][2] - around[3][3]))
        buoyancy = push * below
        for f in range(2):
            w, (ww, we, ws, wn) = mids[f], around[f]
            q = w + ((east_own * (we - w) + west_own * (w - ww)) + (north_own * (wn - w) + south_own * (w - ws)))
            out[f, here, :] = q + buoyancy if f == 0 else q - haline * buoyancy
        for f in (2, 3):
            w, (ww, we, ws, wn) = mids[f], around[f]
            spin = coriolis * mids[5 - f]
            centre = (1.0 - 4.0 * viscosity) * w
            centre = centre - spin if f == 2 else centre + spin
            out[f, here, :] = centre + viscosity * ((we + ww) + (wn + ws))
        return below

    each_level(levels, one, jnp.zeros((rows, cols), f32))


def rows_kernel(dims, ids, *refs):
    levels, rows, cols, half, pair = dims
    count = 1 if pair else 2
    new, const, outs, lines, (scratch,) = (refs[i * count : (i + 1) * count] for i in range(5))
    eye = (iota((levels, levels), 0) == iota((levels, levels), 1)).astype(bf16)
    pick = (iota((levels, cols), 0) == ids[2]).astype(bf16)
    at_edge = pl.ds(ids[2], 1)
    for h in range(count):
        block = split(const[h][6][:, :levels])
        turned = tuple(dot(eye, piece, ((1,), (1,))).astype(bf16) for piece in block)
        scratch[4] = dot(turned[0], pick) + dot(turned[1], pick)
        for p in range(2):
            both = dot3(turned, split(jnp.concatenate([new[h][2 * p], new[h][2 * p + 1]], axis=1)))
            scratch[2 * p] = both[:, :cols]
            scratch[2 * p + 1] = both[:, cols:]
        lines[h][...] = jnp.zeros_like(lines[h])
        wet = const[h][4]
        for j in range(5):
            lines[h][pl.ds(j, 1), :] = scratch[j, at_edge, :]
            outs[h][j] = wet * scratch[j]


def project_kernel(dims, setup, ids, t, s, u, v, sea, *rest):
    levels, rows, cols, half, pair = dims
    if setup:
        inverse, coup, proj, planes, *rest = rest
        lat_out, (spike, w_high, w_low, p_high, p_low, spike_packed, corner, b_plane, cells, wide) = rest[:-10], rest[-10:]
        n = levels * rows
        for y in range(rows):
            cells[pl.ds(y, levels, stride=rows), :] = inverse[y]
        pieces = split(cells[...])
        pick = (iota((n, levels), 0) // rows == iota((n, levels), 1)).astype(bf16)
        same = (iota((n, n), 0) % rows) == (iota((n, n), 1) % rows)
        for piece, out in zip(pieces, (w_high, w_low)):
            full = dot(pick, piece, ((1,), (1,)))
            out[...] = jnp.where(same, full, 0.0).astype(bf16)
        wide[...] = jnp.zeros_like(wide)
        for y in range(rows):
            wide[y, pl.ds(0, levels), pl.ds(0, levels)] = inverse[y]
            wide[y, pl.ds(half, levels), pl.ds(half, levels)] = inverse[y]
        high, low = split(wide[...].reshape(rows * cols, cols))
        p_high[...] = high
        p_low[...] = low
        spike_packed[...] = jnp.zeros_like(spike_packed)
        for y in range(rows):
            line = inverse[y, pl.ds(ids[2], 1), :]
            spike_packed[pl.ds(y, 1), pl.ds(0, levels)] = line
            spike_packed[pl.ds(y, 1), pl.ds(half, levels)] = line
    else:
        coup, corner, b_plane, w_high, w_low, proj, planes, *lat_out = rest
    w = (w_high[...], w_low[...])
    for f, (x, y) in enumerate(((t, s), (u, v))):
        both = dot3(w, split(jnp.concatenate([x[...], y[...]], axis=1)))
        proj[2 * f] = both[:, :cols]
        proj[2 * f + 1] = both[:, cols:]
    edge = pl.ds(pl.multiple_of(ids[2] * rows, rows), rows)
    zero = jnp.zeros((rows, cols), f32)
    if setup:
        n = levels * rows
        pick = (iota((n, cols), 0) // rows == ids[2]).astype(bf16)
        spike[...] = dot(w[0], pick) + dot(w[1], pick)
        corner[...] = spike[edge, :]
    for f in range(4):
        planes[f] = proj[f, edge, :]

    def one(k, sums):
        here = level_at(k, rows)
        wet = sea[here, :].astype(f32)
        values = [wet * proj[f, here, :] for f in range(4)]
        for f in range(4):
            proj[f, here, :] = values[f]
        sums = [sums[0] + values[2], sums[1] + values[3], *sums[2:]]
        if setup:
            value = wet * spike[here, :]
            spike[here, :] = value
            sums[2] = sums[2] + value
        return tuple(sums)

    sums = each_level(levels, one, (zero,) * (3 if setup else 2))
    if setup:
        b_plane[...] = sums[2]
    sums = [sums[0], sums[1], b_plane[...]]
    for j in range(3):
        planes[4 + j] = sums[j]
    lane_row = iota((rows, cols), 0)
    coupled = jnp.zeros((rows, cols), f32)
    for y in range(rows):
        coupled = jnp.where(lane_row == y, coup[y], coupled)
    lines = [planes[f] for f in range(4)] + [sums[1], sums[2], corner[...], coupled]
    for which, row in enumerate(row_choices(pair, rows, ids[0])):
        for j, value in enumerate(lines):
            if pair:
                line = jnp.where(row == 0, value[0:1], value[rows - 1 : rows])
            else:
                line = value[row : row + 1]
            lat_out[which][pl.ds(j, 1), :] = line


def side_kernel(dims, ids, west, east, west_sea, east_sea, planes, corner, spike_packed, p_high, p_low, msg, proj):
    levels, rows, cols, half, pair = dims
    lane = iota((rows, cols), 1)
    row = iota((rows, cols), 0)
    packed = (west[0], west[1], east[0], east[1])
    chunks = []
    for y in range(rows):
        chunks.append(jnp.concatenate([jnp.where(row == y, x, 0.0) for x in packed], axis=0))
    lhs = jnp.concatenate(chunks, axis=1)
    out = dot3(split(lhs), (p_high[...], p_low[...]))
    for j in range(4):
        proj[j] = out[j * rows : (j + 1) * rows]
    for j in range(7):
        msg[j] = planes[j]
    edge = ids[2]
    misc = jnp.zeros((rows, cols), f32)
    spk = spike_packed[...]
    for side, wet in enumerate((west_sea, east_sea)):
        wet = jnp.where(lane < half, wet[2], 0.0)
        for p in range(2):
            value = out[(2 * side + p) * rows : (2 * side + p + 1) * rows]
            for i in range(2):
                column = jnp.sum(jnp.where(lane == edge + i * half, value, 0.0), axis=1, keepdims=True)
                misc = jnp.where(lane == side * 8 + 2 * p + i, column, misc)
            if p == 1:
                column = jnp.sum(wet * value, axis=1, keepdims=True)
                misc = jnp.where(lane == side * 8 + 4, column, misc)
        column = jnp.sum(wet * spk, axis=1, keepdims=True)
        misc = jnp.where(lane == side * 8 + 5, column, misc)
    msg[7] = jnp.where(lane == CORNER_LANE, corner[...], misc)


def apply_kernel(dims, step, final, ids, coup, proj, spike, mine, theirs, base, coef, factor, beside, *rest):
    levels, rows, cols, half, pair = dims
    count = 1 if pair else 2
    row_proj, row_line, row_const, row_late, row_far = (rest[i * count : (i + 1) * count] for i in range(5))
    rest = rest[5 * count :]
    if final:
        outs = rest
    else:
        late_out, outs, (to_east, to_west), lat_msgs = rest[0], rest[1:5], rest[5:7], rest[7:]
    lat, depth, parts = ids[0], ids[1], ids[3]
    lane = iota((rows, cols), 1)
    row = iota((rows, cols), 0)
    has_north = jnp.where(lat < parts - 1, 1.0, 0.0)
    has_south = jnp.where(lat > 0, 1.0, 0.0)

    c = jnp.zeros((rows, cols), f32)
    for y in range(rows):
        c = jnp.where(row == y, coup[y], c)
    own_corner = lane_of(mine[7], CORNER_LANE)
    other_corner = lane_of(theirs[7], CORNER_LANE)
    scaled = c / (1.0 - c * c * own_corner * other_corner)
    co, cm = c * other_corner, c * own_corner
    carried = [scaled * (theirs[f] + co * mine[f]) for f in range(4)]
    misc = theirs[7]
    carried_side = scaled * (misc + co * mine[7])
    theirs_side = scaled * (mine[7] + cm * misc)

    row_solved, row_sums = [], []
    for h in range(count):
        far, line = row_far[h], row_line[h]
        c_row, other, own = far[7:8, :], far[6:7, :], line[4:5, :]
        scaled_row = c_row / (1.0 - c_row * c_row * own * other)
        joined = [scaled_row * (far[f : f + 1, :] + c_row * other * line[f : f + 1, :]) for f in range(4)]
        row_solved.append([row_proj[h][f] + row_proj[h][4] * joined[f] for f in range(4)])
        theirs_v = scaled_row * (line[3:4, :] + c_row * own * far[3:4, :])
        row_sums.append(far[4:5, :] + far[5:6, :] * theirs_v)

    sum_u = theirs[4] + theirs[6] * (scaled * (mine[2] + cm * theirs[2]))
    sum_v = theirs[5] + theirs[6] * (scaled * (mine[3] + cm * theirs[3]))
    side_u = [lane_of(misc, q * 8 + 4) + lane_of(misc, q * 8 + 5) * lane_of(theirs_side, q * 8 + 2) for q in (0, 1)]
    west_u, east_u = insert(lane, sum_u, *side_u)
    south_v = jnp.where(row == 0, row_sums[-1] * has_south, pltpu.roll(sum_v, 1, 0))
    north_v = jnp.where(row == rows - 1, row_sums[0] * has_north, pltpu.roll(sum_v, rows - 1, 0))
    upper = jnp.where(depth == 0, 1.0, 0.0)
    deeper = (west_u - east_u + south_v - north_v) * upper

    coriolis = coriolis_of(dims, ids)
    push = -0.5 * pressure_scale * gravity
    around = []
    for f in range(4):
        west, east = insert(lane, carried[f], lane_of(carried_side, f), lane_of(carried_side, 8 + f))
        south, north = inner(row, carried[f])
        around.append((east, west, north, south))
    plain = 1.0 - 4.0 * viscosity
    mids = (plain * carried[2] - coriolis * carried[3], plain * carried[3] + coriolis * carried[2])

    def one(j, below):
        k = levels - 1 - j
        here = level_at(k, rows)
        sides = [beside[j, here, :] for j in range(4)]
        moved = [[side * plane for side, plane in zip(sides, around[f])] for f in (2, 3)]
        below = below + ((moved[0][1] - moved[0][0]) + (moved[1][3] - moved[1][2]))
        buoyancy = push * below
        factors = [factor[step, j, here, :] for j in range(5)]
        for f in range(2):
            q = base[f, here, :] + factors[0] * carried[f]
            q = q + (
                (factors[1] * around[f][0] + factors[2] * around[f][1])
                + (factors[3] * around[f][2] + factors[4] * around[f][3])
            )
            outs[f][here, :] = q + buoyancy if f == 0 else q - haline * buoyancy
        spk = spike[here, :]
        for i in range(2):
            total = (moved[i][0] + moved[i][1]) + (moved[i][2] + moved[i][3])
            outs[2 + i][here, :] = base[2 + i, here, :] + (spk * mids[i] + viscosity * total)
        return below

    each_level(levels, one, deeper)

    later = (iota((levels, levels), 1) >= iota((levels, levels), 0)).astype(bf16)
    for h in range(count):
        if pair:
            at, sign = jnp.where(lat == 0, rows - 1, 0), jnp.where(lat == 0, -1.0, 1.0)
        else:
            at, sign = ((rows - 1, -1.0), (0, 1.0))[h]
        take = lambda ref: take_row(ref, at, levels, rows)
        beyond = row_solved[h]
        if pair:
            own = jnp.where(lat == 0, coef[step, 2, pl.ds(rows - 1, levels, stride=rows), :],
                            coef[step, 3, pl.ds(0, levels, stride=rows), :])
        else:
            own = coef[step, 2 + h, pl.ds(at, levels, stride=rows), :]
        late = row_const[h][5] if step else row_late[h][4]
        here_north = row_const[h][4]
        if pair:
            other = jnp.where(lat == 0, here_north, -late)
        else:
            other = here_north if h == 0 else -late
        gate = own * other
        above = push * sign * beyond[3]
        high, low = split(above)
        rise = dot(later, high) + dot(later, low)
        spk = take(spike)
        pick = lambda plane: (
            jnp.where(lat == 0, plane[rows - 1 : rows], plane[0:1]) if pair else plane[at : at + 1]
        )
        extra = []
        for f in range(2):
            mid = take(proj.at[f]) + spk * pick(carried[f])
            flow = gate * (beyond[f] - mid)
            extra.append(flow + rise if f == 0 else flow - haline * rise)
        for f in (2, 3):
            extra.append(viscosity * beyond[f])
        for f in range(4):
            if pair:
                for place, mask in ((rows - 1, has_north), (0, has_south)):
                    there = pl.ds(place, levels, stride=rows)
                    outs[f][there, :] = outs[f][there, :] + mask * extra[f]
            else:
                there = pl.ds(at, levels, stride=rows)
                outs[f][there, :] = outs[f][there, :] + (has_north if h == 0 else has_south) * extra[f]

    if not final:
        for which, at in enumerate(row_choices(pair, rows, lat)):
            for f in range(4):
                lat_msgs[which][f] = take_row(outs[f], at, levels, rows)
            lat_msgs[which][4] = late_out[...]
        for p in range(2):
            to_east[p], to_west[p] = edge_columns(levels, rows, outs[2 * p], outs[2 * p + 1], 2)


def call(kernel, outs, args, smem=(0,), scratch=(), name=None, hbm=()):
    places = [pltpu.SMEM if i in smem else pltpu.HBM if i in hbm else pltpu.VMEM for i in range(len(args))]
    specs = [pl.BlockSpec(memory_space=place) for place in places]
    return pl.pallas_call(
        kernel,
        out_shape=[jax.ShapeDtypeStruct(shape, kind) for shape, kind in outs],
        in_specs=specs,
        out_specs=[pl.BlockSpec(memory_space=pltpu.VMEM)] * len(outs),
        scratch_shapes=list(scratch),
        compiler_params=pltpu.CompilerParams(vmem_limit_bytes=VMEM_BYTES),
        name=name,
    )(*args)


def on_device(
    adj_temp,
    adj_salt,
    adj_zonal,
    adj_merid,
    east_speed,
    north_speed,
    branch_flags,
    sea_mask,
    block_inverse,
    coupling,
):
    levels, rows, cols = adj_temp.shape
    half = cols // 2
    lons, lats, depths = (lax.axis_size(a) for a in ("lon", "lat", "depth"))
    pair = lats == 2
    dims = (levels, rows, cols, half, pair)
    count = 1 if pair else 2
    n = levels * rows
    lat, depth = lax.axis_index("lat"), lax.axis_index("depth")
    ids = jnp.stack([lat, depth, (levels - 1) * (1 - depth), jnp.int32(lats)]).astype(jnp.int32)
    flat = lambda x: x.reshape(x.shape[:-3] + (n, cols))
    sea, east, north, flags = flat(sea_mask), flat(east_speed), flat(north_speed), flat(branch_flags)
    state = [flat(x) for x in (adj_temp, adj_salt, adj_zonal, adj_merid)]
    plane = (rows, cols)
    grid = (levels, cols)

    ring = [(i, (i + 1) % lons) for i in range(lons)]
    back = [(b, a) for a, b in ring]
    up = [(i, i + 1) for i in range(lats - 1)]
    down = [(b, a) for a, b in up]

    def to_lat(msgs, flip):
        routes = [up + down] if pair else [down, up]
        if not flip:
            return [lax.ppermute(m, "lat", r) for m, r in zip(msgs, routes)]
        both = [
            [(a * depths + d, b * depths + (depths - 1 - d)) for a, b in r for d in range(depths)] for r in routes
        ]
        return [lax.ppermute(m, ("lat", "depth"), r) for m, r in zip(msgs, both)]

    def to_depth(msg):
        return lax.ppermute(msg, "depth", [(d, depths - 1 - d) for d in range(depths)])

    sources = (*state, sea, east, north, flags, block_inverse)
    sources = tuple(pltpu.with_memory_space_constraint(x, pltpu.HBM) for x in sources)
    to_east, to_west, late, *rest = call(
        functools.partial(pack_kernel, dims),
        [((4,) + plane, f32), ((3,) + plane, f32), (grid, f32)]
        + [((7,) + grid, f32)] * count
        + [(x.shape, x.dtype) for x in sources],
        (ids, *sources),
        scratch=(pltpu.SemaphoreType.DMA((9,)),),
        name="pack",
        hbm=range(1, 10),
    )
    lat_msgs, rest = rest[:count], rest[count:]
    state, (sea, east, north, flags, block_inverse) = rest[:4], rest[4:]
    row_const = to_lat(lat_msgs, False)
    west_const = lax.ppermute(to_east, "lon", ring)
    east_const = lax.ppermute(to_west, "lon", back)
    row_new, west, east_in = row_const, west_const, east_const

    for step in reversed(range(STEPS)):
        first = step == STEPS - 1
        outs = [((4, n, cols), f32), ((7,) + plane, f32)] + [(plane, f32)] * count
        if first:
            outs += [((n, cols), f32)] + [((n, n), bf16)] * 2 + [((rows * cols, cols), bf16)] * 2 + [(plane, f32)] * 3
            args = (ids, *state, sea, block_inverse, coupling)
            smem = (0, 7)
            scratch = (pltpu.VMEM((n, levels), f32), pltpu.VMEM((rows, cols, cols), f32))
        else:
            args = (ids, *state, sea, coupling, corner, b_plane, w_high, w_low)
            smem = (0, 6)
            scratch = ()
        proj, planes, *more = call(
            functools.partial(project_kernel, dims, first), outs, args, smem, scratch, name="project"
        )
        far_msgs = more[:count]
        if first:
            spike, w_high, w_low, p_high, p_low, spike_packed, corner, b_plane = more[count:]
        row_far = to_lat(far_msgs, True)
        mine, side_proj = call(
            functools.partial(side_kernel, dims),
            [((8,) + plane, f32), ((4,) + plane, f32)],
            (ids, west, east_in, west_const, east_const, planes, corner, spike_packed, p_high, p_low),
            name="sides",
        )
        theirs = to_depth(mine)
        if first:
            coef, factor, beside = call(
                functools.partial(coef_kernel, dims),
                [((STEPS, 4, n, cols), f32), ((STEPS, 5, n, cols), f32), ((4, n, cols), f32)],
                (sea, east, north, flags, west_const, east_const, spike, spike_packed),
                (),
                name="coef",
            )
        (base,) = call(
            functools.partial(base_kernel, dims, step),
            [((4, n, cols), f32)],
            (ids, proj, side_proj, west_const, east_const, coef),
            name="base",
        )
        rows_out = call(
            functools.partial(rows_kernel, dims),
            [((5,) + grid, f32)] * count + [(plane, f32)] * count,
            (ids, *row_new, *row_const),
            scratch=(pltpu.VMEM((5,) + grid, f32),),
            name="rows",
        )
        final = step == 0
        outs, extra = [((n, cols), f32)] * 4, ()
        if not final:
            outs = outs + [((2,) + plane, f32)] * 2 + [((5,) + grid, f32)] * count
            extra = (late,)
        result = call(
            functools.partial(apply_kernel, dims, step, final),
            outs,
            (
                ids, coupling, proj, spike, mine, theirs, base, coef, factor, beside,
                *rows_out, *row_const, *row_new, *row_far, *extra,
            ),
            (0, 1),
            name="apply",
        )
        state = result[:4]
        if not final:
            row_new = to_lat(result[6:], False)
            west = lax.ppermute(result[4], "lon", ring)
            east_in = lax.ppermute(result[5], "lon", back)
    return tuple(x.reshape(levels, rows, cols) for x in state)


def solution(mesh):
    in_specs = (
        P("depth", "lat", "lon"),
        P("depth", "lat", "lon"),
        P("depth", "lat", "lon"),
        P("depth", "lat", "lon"),
        P("depth", "lat", "lon"),
        P("depth", "lat", "lon"),
        P(None, "depth", "lat", "lon"),
        P("depth", "lat", "lon"),
        P("lat", "depth", None),
        P("lat"),
    )
    out_specs = (
        P("depth", "lat", "lon"),
        P("depth", "lat", "lon"),
        P("depth", "lat", "lon"),
        P("depth", "lat", "lon"),
    )
    return jax.shard_map(
        on_device, mesh=mesh, in_specs=in_specs, out_specs=out_specs, check_vma=False
    )
```

```python
import functools

import jax
import jax.numpy as jnp
from jax import lax
from jax.experimental import pallas as pl
from jax.experimental.pallas import tpu as pltpu
from jax.sharding import PartitionSpec as P

STEPS = 2

advect_scale = 0.25
diffusion = 0.5
gravity = 0.1
pressure_scale = 1.0
viscosity = 0.1
haline = 0.8

BLOCK = 48
VMEM_BYTES = 16 * 1024 * 1024
f32 = jnp.float32
bf16 = jnp.bfloat16
CORNER_LANE = 16


def split(value):
    high = value.astype(bf16)
    return high, (value - high.astype(f32)).astype(bf16)


def dot(a, b, contract=((1,), (0,))):
    return lax.dot_general(a, b, (contract, ((), ())), preferred_element_type=f32)


def dot3(a, b):
    return dot(a[0], b[0]) + (dot(a[0], b[1]) + dot(a[1], b[0]))


def iota(shape, dim):
    return lax.broadcasted_iota(jnp.int32, shape, dim)


def branches(flags):
    one = jnp.where(flags >= 3, 1, 0) + jnp.where(flags >= 6, 1, 0)
    zonal = (flags - 3 * one).astype(f32) * 0.5
    return zonal, one.astype(f32) * 0.5


def lane_of(value, lane):
    return jnp.broadcast_to(value[:, lane : lane + 1], value.shape)


def level_at(k, rows):
    return pl.ds(k * rows if isinstance(k, int) else pl.multiple_of(k * rows, rows), rows)


def level(ref, k, rows):
    return ref[level_at(k, rows), :]


def turn(value, shift):
    return pltpu.roll(value, shift % value.shape[1], 1)


def each_level(levels, body, carry):
    block = min(BLOCK, levels)

    def some(b, carry):
        for i in range(block):
            carry = body(b * block + i, carry)
        return carry

    if block == levels:
        return some(0, carry)
    return lax.fori_loop(0, levels // block, some, carry)


def take_row(ref, row, levels, rows):
    if isinstance(row, int):
        return ref[pl.ds(row, levels, stride=rows), :]
    low = ref[pl.ds(0, levels, stride=rows), :]
    high = ref[pl.ds(rows - 1, levels, stride=rows), :]
    return jnp.where(row == 0, low, high)


def by_side(ids, near, far, j):
    even = ids[4] == 0
    return jnp.where(even, far[j], near[j]), jnp.where(even, near[j], far[j])


def to_pairs(ids, near, far, j, to_east, to_west):
    even = ids[4] == 0
    near[j] = jnp.where(even, to_east, to_west)
    far[j] = jnp.where(even, to_west, to_east)


def row_choices(pair, rows, lat):
    return [jnp.where(lat == 0, rows - 1, 0)] if pair else [0, rows - 1]


def pack_kernel(dims, ids, *refs):
    levels, rows, cols, half, pair = dims
    coup, sources, (near, far, nn_late, coupled), rest = refs[0], refs[1:10], refs[10:14], refs[14:]
    count = 1 if pair else 2
    lat_msgs, copies, sems = rest[:count], rest[count : count + 9], rest[-1]
    moves = [pltpu.make_async_copy(a, b, sems.at[i]) for i, (a, b) in enumerate(zip(sources, copies))]
    for move in moves:
        move.start()
    t, s, u, v, sea, east, north, flags, inverse = copies
    lane = iota((rows, cols), 1)
    fields = (t, s, u, v)
    index = iota((rows, cols), 0)
    value = jnp.zeros((rows, cols), f32)
    for y in range(rows):
        value = jnp.where(index == y, coup[y], value)
    coupled[...] = value
    for move in moves:
        move.wait()
    pairs = ((t, s, 2), (u, v, 2), (sea, east, 2), (flags.at[1], flags.at[0], 1))
    packed = [edge_columns(levels, rows, x, y, pieces) for x, y, pieces in pairs]
    for j in range(2):
        to_pairs(ids, near, far, j, *packed[j])
    wet_speed, flag = packed[2][0], packed[3][0]
    wet, speed = wet_speed, turn(wet_speed, half)
    zonal = branches(jnp.round(flag).astype(jnp.int32))[0]
    nexts = [wet * (speed * z - diffusion) for z in (zonal, turn(zonal, half))]
    to_pairs(ids, near, far, 2, jnp.where(lane < half, wet, turn(nexts[0], half)), packed[2][1])
    to_pairs(ids, near, far, 3, nexts[1], nexts[1])
    for which, row in enumerate(row_choices(pair, rows, ids[0])):
        msg = lat_msgs[which]
        for j, x in enumerate(fields):
            msg[j] = take_row(x, row, levels, rows)
        wet = take_row(sea, row, levels, rows).astype(f32)
        speed = take_row(north, row, levels, rows)
        msg[4] = wet
        for step in (1, 0):
            _, merid = branches(take_row(flags.at[step], row, levels, rows))
            value = wet * (speed * merid - diffusion)
            if step:
                msg[5] = value
            elif pair or row:
                nn_late[...] = value
        msg[6] = jnp.zeros((levels, cols), f32)
        if pair:
            block = jnp.where(row == 0, inverse[0], inverse[rows - 1])
        else:
            block = inverse[row]
        msg[6, :, pl.ds(0, levels)] = block


def edge_columns(levels, rows, x, y, pieces):
    cols = x.shape[1]
    half = cols // 2
    source, target = iota((2 * cols, 2 * cols), 0), iota((2 * cols, 2 * cols), 1)
    column = jnp.where(target < cols, cols - 1, 0) + jnp.where(target % cols < half, 0, cols)
    spread = (source == column).astype(bf16)
    both = jnp.concatenate([x[...].astype(f32), y[...].astype(f32)], axis=1)
    high, low = split(both)
    wide = dot(high, spread)
    if pieces == 2:
        wide = wide + dot(low, spread)
    place = iota((rows, 2 * cols), 1) % half
    out = jnp.zeros((rows, 2 * cols), f32)
    for k in range(levels):
        out = jnp.where(place == k, wide[k * rows : (k + 1) * rows], out)
    return out[:, :cols], out[:, cols:]


def insert(lane, value, west_in, east_in):
    cols = value.shape[1]
    return (
        jnp.where(lane == 0, west_in, turn(value, 1)),
        jnp.where(lane == cols - 1, east_in, turn(value, cols - 1)),
    )


def inner(row, value):
    rows = value.shape[0]
    return (
        jnp.where(row == 0, 0.0, pltpu.roll(value, 1, 0)),
        jnp.where(row == rows - 1, 0.0, pltpu.roll(value, rows - 1, 0)),
    )


def coef_kernel(step, dims, ids, sea, east, north, flags, near, far, spike, spike_packed, out, factor, *beside):
    levels, rows, cols, half, _ = dims
    lane, row = iota((rows, cols), 1), iota((rows, cols), 0)
    west_const, sea_side = by_side(ids, near, far, 2)
    next_side = west_const if step else by_side(ids, near, far, 3)[0]
    spk = spike_packed[...]
    spike_west = jnp.where(lane < half, west_const, 0.0) * spk
    spike_east = jnp.where(lane < half, sea_side, 0.0) * spk

    def one(k, carry):
        wet = level(sea, k, rows).astype(f32)
        part = advect_scale * wet
        speed_e, speed_n = level(east, k, rows), level(north, k, rows)
        sea_east = jnp.where(lane == cols - 1, turn(sea_side, cols - 1 - k), turn(wet, cols - 1))
        sea_north = jnp.where(row == rows - 1, 1.0, pltpu.roll(wet, rows - 1, 0))
        here = level_at(k, rows)
        mid = level(spike, k, rows)
        west, east_ = insert(lane, mid, turn(spike_west, cols - k), turn(spike_east, cols - 1 - k))
        south, north_ = inner(row, mid)
        for ref in beside:
            for j, value in enumerate((east_, west, north_, south)):
                ref[j, here, :] = value
        zonal, merid = branches(level(flags.at[step], k, rows))
        speed_z, speed_m = speed_e * zonal, speed_n * merid
        east_own = part * (speed_e - speed_z + diffusion) * sea_east
        next_west = jnp.where(
            lane == 0, turn(next_side, 2 * cols - step * half - k), turn(wet * (speed_z - diffusion), 1)
        )
        west_own = part * next_west
        north_own = part * (speed_n - speed_m + diffusion) * sea_north
        next_south = jnp.where(row == 0, 1.0, pltpu.roll(wet * (speed_m - diffusion), 1, 0))
        south_own = part * next_south
        for j, value in enumerate((east_own, west_own, north_own, south_own)):
            out[j, here, :] = value
        inside_n = jnp.where(row == rows - 1, 0.0, north_own)
        inside_s = jnp.where(row == 0, 0.0, south_own)
        factor[0, here, :] = mid * (1.0 + ((west_own - east_own) + (inside_s - inside_n)))
        factor[1, here, :] = east_own * east_
        factor[2, here, :] = -west_own * west
        factor[3, here, :] = inside_n * north_
        factor[4, here, :] = -inside_s * south
        return carry

    each_level(levels, one, ())


def coriolis_of(dims, ids):
    _, rows, cols, _, _ = dims
    index = (ids[0] * rows + iota((rows, cols), 0)).astype(f32)
    return 0.2 + 0.6 * (index + 0.5) / (rows * ids[3])


def base_kernel(dims, ids, proj, side_proj, near, far, coef, out):
    levels, rows, cols, half, _ = dims
    lane, row = iota((rows, cols), 1), iota((rows, cols), 0)
    parts = []
    for p in range(2):
        line = []
        for side, const in enumerate(by_side(ids, near, far, 2)):
            wet = jnp.where(lane < half, const, turn(const, half))
            line.append(wet * side_proj[2 * side + p])
        parts.append(jnp.concatenate(line, axis=1))
    source, target = iota((2 * cols, 2 * cols), 0), iota((2 * cols, 2 * cols), 1)
    pick = target % cols
    wanted = pick // 2 + jnp.where(target < cols, 0, half) + jnp.where(pick % 2 == 1, 0, cols)
    spread = (source == wanted).astype(bf16)
    high, low = split(jnp.concatenate(parts, axis=0))
    mixed = dot(high, spread) + dot(low, spread)
    halo = [mixed[p * rows : (p + 1) * rows, i * cols : (i + 1) * cols] for p in range(2) for i in range(2)]
    coriolis = coriolis_of(dims, ids)
    push = -0.5 * pressure_scale * gravity
    top, bottom = row == rows - 1, row == 0

    def one(j, below):
        k = levels - 1 - j
        here = level_at(k, rows)
        east_own, west_own = coef[0, here, :], coef[1, here, :]
        north_own = jnp.where(top, 0.0, coef[2, here, :])
        south_own = jnp.where(bottom, 0.0, coef[3, here, :])
        mids, around = [], []
        for f in range(4):
            w = proj[f, here, :]
            mids.append(w)
            side = turn(halo[f], 2 * cols - 2 * k - 1)
            around.append((*insert(lane, w, side, side), *inner(row, w)))
        below = below + ((around[2][0] - around[2][1]) + (around[3][2] - around[3][3]))
        buoyancy = push * below
        for f in range(2):
            w, (ww, we, ws, wn) = mids[f], around[f]
            q = w + ((east_own * (we - w) + west_own * (w - ww)) + (north_own * (wn - w) + south_own * (w - ws)))
            out[f, here, :] = q + buoyancy if f == 0 else q - haline * buoyancy
        for f in (2, 3):
            w, (ww, we, ws, wn) = mids[f], around[f]
            spin = coriolis * mids[5 - f]
            centre = (1.0 - 4.0 * viscosity) * w
            centre = centre - spin if f == 2 else centre + spin
            out[f, here, :] = centre + viscosity * ((we + ww) + (wn + ws))
        return below

    each_level(levels, one, jnp.zeros((rows, cols), f32))


def rows_kernel(first, dims, ids, *refs):
    levels, _, cols, _, pair = dims
    count = 1 if pair else 2
    new, const, *refs = (refs[i * count : (i + 1) * count] for i in range(len(refs) // count + 1))
    turned_high, turned_low, thin = refs[2:5] if first else refs[:3]
    outs, lines = refs[:2] if first else refs[3:5]
    (scratch,) = refs[5]
    at_edge = pl.ds(ids[2], 1)
    for h in range(count):
        if first:
            eye = (iota((levels, levels), 0) == iota((levels, levels), 1)).astype(bf16)
            pick = (iota((levels, cols), 0) == ids[2]).astype(bf16)
            turned = tuple(dot(eye, piece, ((1,), (1,))).astype(bf16) for piece in split(const[h][6][:, :levels]))
            turned_high[h][...], turned_low[h][...] = turned
            thin[h][...] = dot(turned[0], pick) + dot(turned[1], pick)
        turned = (turned_high[h][...], turned_low[h][...])
        both = dot3(turned, split(jnp.concatenate([new[h][f] for f in range(4)], axis=1)))
        for f in range(4):
            scratch[f] = both[:, f * cols : (f + 1) * cols]
        lines[h][...] = jnp.zeros_like(lines[h])
        wet = const[h][4]
        for j in range(4):
            lines[h][pl.ds(j, 1), :] = scratch[j, at_edge, :]
            outs[h][j] = wet * scratch[j]
        lines[h][pl.ds(4, 1), :] = thin[h][at_edge, :]
        outs[h][4] = wet * thin[h][...]


def project_kernel(setup, dims, ids, t, s, u, v, sea, *rest):
    levels, rows, cols, half, pair = dims
    if setup:
        inverse, coupled, proj, planes, *rest = rest
        lat_out, (spike, w_high, w_low, p_high, p_low, spike_packed, corner, b_plane, cells, wide) = rest[:-10], rest[-10:]
        n = levels * rows
        for y in range(rows):
            cells[pl.ds(y, levels, stride=rows), :] = inverse[y]
        pieces = split(cells[...])
        pick = (iota((n, levels), 0) // rows == iota((n, levels), 1)).astype(bf16)
        same = (iota((n, n), 0) % rows) == (iota((n, n), 1) % rows)
        for piece, out in zip(pieces, (w_high, w_low)):
            full = dot(pick, piece, ((1,), (1,)))
            out[...] = jnp.where(same, full, 0.0).astype(bf16)
        wide[...] = jnp.zeros_like(wide)
        for y in range(rows):
            wide[y, pl.ds(0, levels), pl.ds(0, levels)] = inverse[y]
            wide[y, pl.ds(half, levels), pl.ds(half, levels)] = inverse[y]
        high, low = split(wide[...].reshape(rows * cols, cols))
        p_high[...] = high
        p_low[...] = low
        spike_packed[...] = jnp.zeros_like(spike_packed)
        for y in range(rows):
            line = inverse[y, pl.ds(ids[2], 1), :]
            spike_packed[pl.ds(y, 1), pl.ds(0, levels)] = line
            spike_packed[pl.ds(y, 1), pl.ds(half, levels)] = line
    else:
        coupled, corner, b_plane, w_high, w_low, proj, planes, *lat_out = rest
    w = (w_high[...], w_low[...])
    for f, (x, y) in enumerate(((t, s), (u, v))):
        both = dot3(w, split(jnp.concatenate([x[...], y[...]], axis=1)))
        proj[2 * f] = both[:, :cols]
        proj[2 * f + 1] = both[:, cols:]
    edge = pl.ds(pl.multiple_of(ids[2] * rows, rows), rows)
    zero = jnp.zeros((rows, cols), f32)
    if setup:
        n = levels * rows
        pick = (iota((n, cols), 0) // rows == ids[2]).astype(bf16)
        spike[...] = dot(w[0], pick) + dot(w[1], pick)
        corner[...] = spike[edge, :]
    for f in range(4):
        planes[f] = proj[f, edge, :]

    def one(k, sums):
        here = level_at(k, rows)
        wet = sea[here, :].astype(f32)
        values = [wet * proj[f, here, :] for f in range(4)]
        for f in range(4):
            proj[f, here, :] = values[f]
        sums = [sums[0] + values[2], sums[1] + values[3], *sums[2:]]
        if setup:
            value = wet * spike[here, :]
            spike[here, :] = value
            sums[2] = sums[2] + value
        return tuple(sums)

    sums = each_level(levels, one, (zero,) * (3 if setup else 2))
    if setup:
        b_plane[...] = sums[2]
    sums = [sums[0], sums[1], b_plane[...]]
    for j in range(3):
        planes[4 + j] = sums[j]
    lines = [planes[f] for f in range(4)] + [sums[1], sums[2], corner[...], coupled[...]]
    for which, row in enumerate(row_choices(pair, rows, ids[0])):
        for j, value in enumerate(lines):
            if pair:
                line = jnp.where(row == 0, value[0:1], value[rows - 1 : rows])
            else:
                line = value[row : row + 1]
            lat_out[which][pl.ds(j, 1), :] = line


def side_kernel(dims, ids, near, far, near_const, far_const, planes, corner, spike_packed, p_high, p_low, msg, proj):
    _, rows, cols, half, _ = dims
    lane = iota((rows, cols), 1)
    row = iota((rows, cols), 0)
    (west0, east0), (west1, east1) = (by_side(ids, near, far, j) for j in range(2))
    packed = (west0, west1, east0, east1)
    chunks = []
    for y in range(rows):
        chunks.append(jnp.concatenate([jnp.where(row == y, x, 0.0) for x in packed], axis=0))
    lhs = jnp.concatenate(chunks, axis=1)
    out = dot3(split(lhs), (p_high[...], p_low[...]))
    for j in range(4):
        proj[j] = out[j * rows : (j + 1) * rows]
    for j in range(7):
        msg[j] = planes[j]
    edge = ids[2]
    misc = jnp.zeros((rows, cols), f32)
    spk = spike_packed[...]
    for side, wet in enumerate(by_side(ids, near_const, far_const, 2)):
        wet = jnp.where(lane < half, wet, 0.0)
        for p in range(2):
            value = out[(2 * side + p) * rows : (2 * side + p + 1) * rows]
            for i in range(2):
                column = jnp.sum(jnp.where(lane == edge + i * half, value, 0.0), axis=1, keepdims=True)
                misc = jnp.where(lane == side * 8 + 2 * p + i, column, misc)
            if p == 1:
                column = jnp.sum(wet * value, axis=1, keepdims=True)
                misc = jnp.where(lane == side * 8 + 4, column, misc)
        column = jnp.sum(wet * spk, axis=1, keepdims=True)
        misc = jnp.where(lane == side * 8 + 5, column, misc)
    msg[7] = jnp.where(lane == CORNER_LANE, corner[...], misc)


def apply_kernel(step, final, dims, ids, coupled, proj, spike, mine, theirs, base, coef, factor, beside, *rest):
    levels, rows, cols, _, pair = dims
    count = 1 if pair else 2
    row_proj, row_line, row_const, row_late, row_far = (rest[i * count : (i + 1) * count] for i in range(5))
    rest = rest[5 * count :]
    if final:
        outs = rest
    else:
        late_out, outs, (to_near, to_far), lat_msgs = rest[0], rest[1:5], rest[5:7], rest[7:]
    lat, depth, parts = ids[0], ids[1], ids[3]
    lane = iota((rows, cols), 1)
    row = iota((rows, cols), 0)
    has_north = jnp.where(lat < parts - 1, 1.0, 0.0)
    has_south = jnp.where(lat > 0, 1.0, 0.0)

    c = coupled[...]
    own_corner = lane_of(mine[7], CORNER_LANE)
    other_corner = lane_of(theirs[7], CORNER_LANE)
    scaled = c / (1.0 - c * c * own_corner * other_corner)
    co, cm = c * other_corner, c * own_corner
    carried = [scaled * (theirs[f] + co * mine[f]) for f in range(4)]
    misc = theirs[7]
    carried_side = scaled * (misc + co * mine[7])
    theirs_side = scaled * (mine[7] + cm * misc)

    row_solved, row_sums = [], []
    for h in range(count):
        far, line = row_far[h], row_line[h]
        c_row, other, own = far[7:8, :], far[6:7, :], line[4:5, :]
        scaled_row = c_row / (1.0 - c_row * c_row * own * other)
        joined = [scaled_row * (far[f : f + 1, :] + c_row * other * line[f : f + 1, :]) for f in range(4)]
        row_solved.append([row_proj[h][f] + row_proj[h][4] * joined[f] for f in range(4)])
        theirs_v = scaled_row * (line[3:4, :] + c_row * own * far[3:4, :])
        row_sums.append(far[4:5, :] + far[5:6, :] * theirs_v)

    sum_u = theirs[4] + theirs[6] * (scaled * (mine[2] + cm * theirs[2]))
    sum_v = theirs[5] + theirs[6] * (scaled * (mine[3] + cm * theirs[3]))
    side_u = [lane_of(misc, q * 8 + 4) + lane_of(misc, q * 8 + 5) * lane_of(theirs_side, q * 8 + 2) for q in (0, 1)]
    west_u, east_u = insert(lane, sum_u, *side_u)
    south_v = jnp.where(row == 0, row_sums[-1] * has_south, pltpu.roll(sum_v, 1, 0))
    north_v = jnp.where(row == rows - 1, row_sums[0] * has_north, pltpu.roll(sum_v, rows - 1, 0))
    upper = jnp.where(depth == 0, 1.0, 0.0)
    deeper = (west_u - east_u + south_v - north_v) * upper

    coriolis = coriolis_of(dims, ids)
    push = -0.5 * pressure_scale * gravity
    around = []
    for f in range(4):
        west, east = insert(lane, carried[f], lane_of(carried_side, f), lane_of(carried_side, 8 + f))
        south, north = inner(row, carried[f])
        around.append((east, west, north, south))
    plain = 1.0 - 4.0 * viscosity
    mids = (plain * carried[2] - coriolis * carried[3], plain * carried[3] + coriolis * carried[2])

    def one(j, below):
        k = levels - 1 - j
        here = level_at(k, rows)
        sides = [beside[j, here, :] for j in range(4)]
        moved = [[side * plane for side, plane in zip(sides, around[f])] for f in (2, 3)]
        below = below + ((moved[0][1] - moved[0][0]) + (moved[1][3] - moved[1][2]))
        buoyancy = push * below
        factors = [factor[j, here, :] for j in range(5)]
        for f in range(2):
            q = base[f, here, :] + factors[0] * carried[f]
            q = q + (
                (factors[1] * around[f][0] + factors[2] * around[f][1])
                + (factors[3] * around[f][2] + factors[4] * around[f][3])
            )
            outs[f][here, :] = q + buoyancy if f == 0 else q - haline * buoyancy
        spk = spike[here, :]
        for i in range(2):
            total = (moved[i][0] + moved[i][1]) + (moved[i][2] + moved[i][3])
            outs[2 + i][here, :] = base[2 + i, here, :] + (spk * mids[i] + viscosity * total)
        return below

    each_level(levels, one, deeper)

    later = (iota((levels, levels), 1) >= iota((levels, levels), 0)).astype(bf16)
    for h in range(count):
        if pair:
            at, sign = jnp.where(lat == 0, rows - 1, 0), jnp.where(lat == 0, -1.0, 1.0)
        else:
            at, sign = ((rows - 1, -1.0), (0, 1.0))[h]
        take = lambda ref: take_row(ref, at, levels, rows)
        beyond = row_solved[h]
        if pair:
            own = jnp.where(lat == 0, coef[2, pl.ds(rows - 1, levels, stride=rows), :],
                            coef[3, pl.ds(0, levels, stride=rows), :])
        else:
            own = coef[2 + h, pl.ds(at, levels, stride=rows), :]
        late = row_const[h][5] if step else row_late[h][4]
        here_north = row_const[h][4]
        if pair:
            other = jnp.where(lat == 0, here_north, -late)
        else:
            other = here_north if h == 0 else -late
        gate = own * other
        above = push * sign * beyond[3]
        high, low = split(above)
        rise = dot(later, high) + dot(later, low)
        spk = take(spike)
        pick = lambda plane: (
            jnp.where(lat == 0, plane[rows - 1 : rows], plane[0:1]) if pair else plane[at : at + 1]
        )
        extra = []
        for f in range(2):
            mid = take(proj.at[f]) + spk * pick(carried[f])
            flow = gate * (beyond[f] - mid)
            extra.append(flow + rise if f == 0 else flow - haline * rise)
        for f in (2, 3):
            extra.append(viscosity * beyond[f])
        for f in range(4):
            if pair:
                for place, mask in ((rows - 1, has_north), (0, has_south)):
                    there = pl.ds(place, levels, stride=rows)
                    outs[f][there, :] = outs[f][there, :] + mask * extra[f]
            else:
                there = pl.ds(at, levels, stride=rows)
                outs[f][there, :] = outs[f][there, :] + (has_north if h == 0 else has_south) * extra[f]

    if not final:
        for which, at in enumerate(row_choices(pair, rows, lat)):
            for f in range(4):
                lat_msgs[which][f] = take_row(outs[f], at, levels, rows)
            lat_msgs[which][4] = late_out[...]
        for p in range(2):
            to_pairs(ids, to_near, to_far, p, *edge_columns(levels, rows, outs[2 * p], outs[2 * p + 1], 2))


def places(levels):
    lat, depth, lon = (lax.axis_index(a) for a in ("lat", "depth", "lon"))
    return lat, depth, (levels - 1) * (1 - depth), lax.axis_size("lat"), lax.rem(lon, 2)


def call(kernel, dims, outs, args, smem=(), scratch=(), hbm=()):
    spaces = [pltpu.SMEM if i in smem else pltpu.HBM if i in hbm else pltpu.VMEM for i in range(len(args))]

    def run(*refs):
        kernel(dims, places(dims[0]), *refs)

    return pl.pallas_call(
        run,
        out_shape=[jax.ShapeDtypeStruct(shape, kind) for shape, kind in outs],
        in_specs=[pl.BlockSpec(memory_space=space) for space in spaces],
        out_specs=[pl.BlockSpec(memory_space=pltpu.VMEM)] * len(outs),
        scratch_shapes=list(scratch),
        compiler_params=pltpu.CompilerParams(vmem_limit_bytes=VMEM_BYTES),
    )(*args)


def on_device(
    adj_temp,
    adj_salt,
    adj_zonal,
    adj_merid,
    east_speed,
    north_speed,
    branch_flags,
    sea_mask,
    block_inverse,
    coupling,
):
    levels, rows, cols = adj_temp.shape
    half = cols // 2
    lons, lats, depths = (lax.axis_size(a) for a in ("lon", "lat", "depth"))
    pair = lats == 2
    dims = (levels, rows, cols, half, pair)
    count = 1 if pair else 2
    n = levels * rows
    flat = lambda x: x.reshape(x.shape[:-3] + (n, cols))
    sea, east, north, flags = flat(sea_mask), flat(east_speed), flat(north_speed), flat(branch_flags)
    state = [flat(x) for x in (adj_temp, adj_salt, adj_zonal, adj_merid)]
    plane = (rows, cols)
    grid = (levels, cols)

    assert lons % 2 == 0
    close = [(i, i ^ 1) for i in range(lons)]
    apart = [(i, (i + 1 if i % 2 else i - 1) % lons) for i in range(lons)]
    up = [(i, i + 1) for i in range(lats - 1)]
    down = [(b, a) for a, b in up]

    def to_lat(msgs, flip):
        routes = [up + down] if pair else [down, up]
        if not flip:
            return [lax.ppermute(m, "lat", r) for m, r in zip(msgs, routes)]
        both = [
            [(a * depths + d, b * depths + (depths - 1 - d)) for a, b in r for d in range(depths)] for r in routes
        ]
        return [lax.ppermute(m, ("lat", "depth"), r) for m, r in zip(msgs, both)]

    def to_depth(msg):
        return lax.ppermute(msg, "depth", [(d, depths - 1 - d) for d in range(depths)])

    sources = (*state, sea, east, north, flags, block_inverse)
    sources = tuple(pltpu.with_memory_space_constraint(x, pltpu.HBM) for x in sources)
    near, far, late, coupled, *rest = call(
        pack_kernel,
        dims,
        [((4,) + plane, f32)] * 2
        + [(grid, f32), (plane, f32)]
        + [((7,) + grid, f32)] * count
        + [(x.shape, x.dtype) for x in sources],
        (pltpu.with_memory_space_constraint(coupling, pltpu.HBM), *sources),
        (0,),
        (pltpu.SemaphoreType.DMA((9,)),),
        range(1, 10),
    )
    lat_msgs, rest = rest[:count], rest[count:]
    state, (sea, east, north, flags, block_inverse) = rest[:4], rest[4:]
    row_const = row_new = to_lat(lat_msgs, False)
    near_const = near = lax.ppermute(near, "lon", close)
    far_const = far = lax.ppermute(far, "lon", apart)

    for step in reversed(range(STEPS)):
        first = step == STEPS - 1
        outs = [((4, n, cols), f32), ((7,) + plane, f32)] + [(plane, f32)] * count
        if first:
            outs += [((n, cols), f32)] + [((n, n), bf16)] * 2 + [((rows * cols, cols), bf16)] * 2 + [(plane, f32)] * 3
            args = (*state, sea, block_inverse, coupled)
            scratch = (pltpu.VMEM((n, levels), f32), pltpu.VMEM((rows, cols, cols), f32))
        else:
            args = (*state, sea, coupled, corner, b_plane, w_high, w_low)
            scratch = ()
        proj, planes, *more = call(functools.partial(project_kernel, first), dims, outs, args, (), scratch)
        far_msgs = more[:count]
        if first:
            spike, w_high, w_low, p_high, p_low, spike_packed, corner, b_plane = more[count:]
        row_far = to_lat(far_msgs, True)
        mine, side_proj = call(
            side_kernel,
            dims,
            [((8,) + plane, f32), ((4,) + plane, f32)],
            (near, far, near_const, far_const, planes, corner, spike_packed, p_high, p_low),
        )
        theirs = to_depth(mine)
        coef, factor, *more = call(
            functools.partial(coef_kernel, step),
            dims,
            [((4, n, cols), f32), ((5, n, cols), f32)] + [((4, n, cols), f32)] * first,
            (sea, east, north, flags, near_const, far_const, spike, spike_packed),
        )
        if first:
            (beside,) = more
        (base,) = call(base_kernel, dims, [((4, n, cols), f32)], (proj, side_proj, near_const, far_const, coef))
        block = ((levels, levels), bf16)
        rows_out = call(
            functools.partial(rows_kernel, first),
            dims,
            [((5,) + grid, f32)] * count
            + [(plane, f32)] * count
            + ([block] * (2 * count) + [(grid, f32)] * count) * first,
            (*row_new, *row_const, *(() if first else row_block)),
            scratch=(pltpu.VMEM((4,) + grid, f32),),
        )
        if first:
            row_block = rows_out[2 * count :]
        rows_out = rows_out[: 2 * count]
        final = step == 0
        outs, extra = [((n, cols), f32)] * 4, ()
        if not final:
            outs = outs + [((2,) + plane, f32)] * 2 + [((5,) + grid, f32)] * count
            extra = (late,)
        result = call(
            functools.partial(apply_kernel, step, final),
            dims,
            outs,
            (
                coupled, proj, spike, mine, theirs, base, coef, factor, beside,
                *rows_out, *row_const, *row_new, *row_far, *extra,
            ),
        )
        state = result[:4]
        if not final:
            row_new = to_lat(result[6:], False)
            near = lax.ppermute(result[4], "lon", close)
            far = lax.ppermute(result[5], "lon", apart)
    return tuple(x.reshape(levels, rows, cols) for x in state)


def solution(mesh):
    in_specs = (
        P("depth", "lat", "lon"),
        P("depth", "lat", "lon"),
        P("depth", "lat", "lon"),
        P("depth", "lat", "lon"),
        P("depth", "lat", "lon"),
        P("depth", "lat", "lon"),
        P(None, "depth", "lat", "lon"),
        P("depth", "lat", "lon"),
        P("lat", "depth", None),
        P("lat"),
    )
    out_specs = (
        P("depth", "lat", "lon"),
        P("depth", "lat", "lon"),
        P("depth", "lat", "lon"),
        P("depth", "lat", "lon"),
    )

    return jax.shard_map(on_device, mesh=mesh, in_specs=in_specs, out_specs=out_specs, check_vma=False)
```

```python
import functools

import jax
import jax.numpy as jnp
from jax import lax
from jax.experimental import pallas as pl
from jax.experimental.pallas import tpu as pltpu
from jax.sharding import PartitionSpec as P

STEPS = 2

advect_scale = 0.25
diffusion = 0.5
gravity = 0.1
pressure_scale = 1.0
viscosity = 0.1
haline = 0.8

BLOCK = 48
VMEM_BYTES = 16 * 1024 * 1024
f32 = jnp.float32
CHUNKS = 3
bf16 = jnp.bfloat16
CORNER_LANE = 16


def split(value):
    high = value.astype(bf16)
    return high, (value - high.astype(f32)).astype(bf16)


def dot(a, b, contract=((1,), (0,))):
    return lax.dot_general(a, b, (contract, ((), ())), preferred_element_type=f32)


def dot3(a, b):
    return dot(a[0], b[0]) + (dot(a[0], b[1]) + dot(a[1], b[0]))


def iota(shape, dim):
    return lax.broadcasted_iota(jnp.int32, shape, dim)


def branches(flags):
    one = jnp.where(flags >= 3, 1, 0) + jnp.where(flags >= 6, 1, 0)
    zonal = (flags - 3 * one).astype(f32) * 0.5
    return zonal, one.astype(f32) * 0.5


def lane_of(value, lane):
    return jnp.broadcast_to(value[:, lane : lane + 1], value.shape)


def level_at(k, rows):
    return pl.ds(k * rows if isinstance(k, int) else pl.multiple_of(k * rows, rows), rows)


def level(ref, k, rows):
    return ref[level_at(k, rows), :]


def turn(value, shift):
    return pltpu.roll(value, shift % value.shape[1], 1)


def each_level(levels, body, carry):
    block = min(BLOCK, levels)

    def some(b, carry):
        for i in range(block):
            carry = body(b * block + i, carry)
        return carry

    if block == levels:
        return some(0, carry)
    return lax.fori_loop(0, levels // block, some, carry)


def take_row(ref, row, levels, rows):
    if isinstance(row, int):
        return ref[pl.ds(row, levels, stride=rows), :]
    low = ref[pl.ds(0, levels, stride=rows), :]
    high = ref[pl.ds(rows - 1, levels, stride=rows), :]
    return jnp.where(row == 0, low, high)


def by_side(ids, near, far, j):
    even = ids[4] == 0
    return jnp.where(even, far[j], near[j]), jnp.where(even, near[j], far[j])


def to_pairs(ids, near, far, j, to_east, to_west):
    even = ids[4] == 0
    near[j] = jnp.where(even, to_east, to_west)
    far[j] = jnp.where(even, to_west, to_east)


def row_choices(pair, rows, lat):
    return [jnp.where(lat == 0, rows - 1, 0)] if pair else [0, rows - 1]


def block_shape(levels):
    return levels // 2


def fetch_kernel(dims, ids, *refs):
    levels, rows, cols, half, pair = dims
    coup, sources, (nn_late, coupled), rest = refs[0], refs[1:10], refs[10:12], refs[12:]
    count = 1 if pair else 2
    lat_msgs, copies, (coup_here, sems) = rest[:count], rest[count : count + 9], rest[count + 9 :]
    moves = [pltpu.make_async_copy(a, b, sems.at[i]) for i, (a, b) in enumerate(zip(sources, copies))]
    moves.append(pltpu.make_async_copy(coup, coup_here, sems.at[9]))
    for move in moves:
        move.start()
    t, s, u, v, sea, _, north, flags, inverse = copies
    for move in moves:
        move.wait()
    spot = iota((rows, rows), 0) == iota((rows, rows), 1)
    value = jnp.sum(jnp.where(spot, coup_here[...], 0.0), axis=1, keepdims=True)
    coupled[...] = jnp.broadcast_to(value, (rows, cols))
    for which, row in enumerate(row_choices(pair, rows, ids[0])):
        msg = lat_msgs[which]

        def put(j, value):
            msg[pl.ds(j * levels, levels), :] = value

        for j, x in enumerate((t, s, u, v)):
            put(j, take_row(x, row, levels, rows))
        wet = take_row(sea, row, levels, rows).astype(f32)
        speed = take_row(north, row, levels, rows)
        put(4, wet)
        for step in (1, 0):
            _, merid = branches(take_row(flags.at[step], row, levels, rows))
            value = wet * (speed * merid - diffusion)
            if step:
                put(5, value)
            elif pair or row:
                nn_late[...] = value
        if pair:
            block = jnp.where(row == 0, inverse[0], inverse[rows - 1])
        else:
            block = inverse[row]
        size = block_shape(levels)
        last = pl.ds(6 * levels, size)
        msg[last, :] = jnp.zeros((size, cols), f32)
        msg[last, pl.ds(0, levels)] = block[:size]
        msg[last, pl.ds(half, levels)] = block[size:]


def edges_kernel(first, dims, ids, t, s, u, v, *refs):
    levels, rows, cols, half, _ = dims
    lane = iota((rows, cols), 1)
    sea, east, flags, near, far = refs if first else (None, None, None, *refs)
    to_pairs(ids, near, far, 0, *edge_columns(levels, rows, t, s, 2))
    to_pairs(ids, near, far, 1, *edge_columns(levels, rows, u, v, 2))
    if first:
        wet, first_wet = edge_columns(levels, rows, sea, east, 2)
        flag, _ = edge_columns(levels, rows, flags.at[1], flags.at[0], 1)
        speed = turn(wet, half)
        zonal = branches(jnp.round(flag).astype(jnp.int32))[0]
        nexts = [wet * (speed * z - diffusion) for z in (zonal, turn(zonal, half))]
        to_pairs(ids, near, far, 2, jnp.where(lane < half, wet, turn(nexts[0], half)), first_wet)
        to_pairs(ids, near, far, 3, nexts[1], nexts[1])


def edge_columns(levels, rows, x, y, pieces):
    cols = x.shape[1]
    half = cols // 2
    source, target = iota((2 * cols, 2 * cols), 0), iota((2 * cols, 2 * cols), 1)
    column = jnp.where(target < cols, cols - 1, 0) + jnp.where(target % cols < half, 0, cols)
    spread = (source == column).astype(bf16)
    both = jnp.concatenate([x[...].astype(f32), y[...].astype(f32)], axis=1)
    high, low = split(both)
    wide = dot(high, spread)
    if pieces == 2:
        wide = wide + dot(low, spread)
    place = iota((rows, 2 * cols), 1) % half
    out = jnp.zeros((rows, 2 * cols), f32)
    for k in range(levels):
        out = jnp.where(place == k, wide[k * rows : (k + 1) * rows], out)
    return out[:, :cols], out[:, cols:]


def insert(lane, value, west_in, east_in):
    cols = value.shape[1]
    return (
        jnp.where(lane == 0, west_in, turn(value, 1)),
        jnp.where(lane == cols - 1, east_in, turn(value, cols - 1)),
    )


def inner(row, value):
    rows = value.shape[0]
    return (
        jnp.where(row == 0, 0.0, pltpu.roll(value, 1, 0)),
        jnp.where(row == rows - 1, 0.0, pltpu.roll(value, rows - 1, 0)),
    )


def coef_kernel(step, dims, ids, sea, east, north, flags, near, far, spike, spike_packed, out, factor, *beside):
    levels, rows, cols, half, _ = dims
    lane, row = iota((rows, cols), 1), iota((rows, cols), 0)
    west_const, sea_side = by_side(ids, near, far, 2)
    next_side = west_const if step else by_side(ids, near, far, 3)[0]
    spk = spike_packed[...]
    spike_west = jnp.where(lane < half, west_const, 0.0) * spk
    spike_east = jnp.where(lane < half, sea_side, 0.0) * spk

    def one(k, carry):
        wet = level(sea, k, rows).astype(f32)
        part = advect_scale * wet
        speed_e, speed_n = level(east, k, rows), level(north, k, rows)
        sea_east = jnp.where(lane == cols - 1, turn(sea_side, cols - 1 - k), turn(wet, cols - 1))
        sea_north = jnp.where(row == rows - 1, 1.0, pltpu.roll(wet, rows - 1, 0))
        here = level_at(k, rows)
        mid = level(spike, k, rows)
        west, east_ = insert(lane, mid, turn(spike_west, cols - k), turn(spike_east, cols - 1 - k))
        south, north_ = inner(row, mid)
        for ref in beside:
            for j, value in enumerate((east_, west, north_, south)):
                ref[j, here, :] = value
        zonal, merid = branches(level(flags.at[step], k, rows))
        speed_z, speed_m = speed_e * zonal, speed_n * merid
        east_own = part * (speed_e - speed_z + diffusion) * sea_east
        next_west = jnp.where(
            lane == 0, turn(next_side, 2 * cols - step * half - k), turn(wet * (speed_z - diffusion), 1)
        )
        west_own = part * next_west
        north_own = part * (speed_n - speed_m + diffusion) * sea_north
        next_south = jnp.where(row == 0, 1.0, pltpu.roll(wet * (speed_m - diffusion), 1, 0))
        south_own = part * next_south
        for j, value in enumerate((east_own, west_own, north_own, south_own)):
            out[j, here, :] = value
        inside_n = jnp.where(row == rows - 1, 0.0, north_own)
        inside_s = jnp.where(row == 0, 0.0, south_own)
        factor[0, here, :] = mid * (1.0 + ((west_own - east_own) + (inside_s - inside_n)))
        factor[1, here, :] = east_own * east_
        factor[2, here, :] = -west_own * west
        factor[3, here, :] = inside_n * north_
        factor[4, here, :] = -inside_s * south
        return carry

    each_level(levels, one, ())


def coriolis_of(dims, ids):
    _, rows, cols, _, _ = dims
    index = (ids[0] * rows + iota((rows, cols), 0)).astype(f32)
    return 0.2 + 0.6 * (index + 0.5) / (rows * ids[3])


def base_kernel(dims, ids, proj, side_proj, near, far, coef, out):
    levels, rows, cols, half, _ = dims
    lane, row = iota((rows, cols), 1), iota((rows, cols), 0)
    parts = []
    for p in range(2):
        line = []
        for side, const in enumerate(by_side(ids, near, far, 2)):
            wet = jnp.where(lane < half, const, turn(const, half))
            line.append(wet * side_proj[2 * side + p])
        parts.append(jnp.concatenate(line, axis=1))
    source, target = iota((2 * cols, 2 * cols), 0), iota((2 * cols, 2 * cols), 1)
    pick = target % cols
    wanted = pick // 2 + jnp.where(target < cols, 0, half) + jnp.where(pick % 2 == 1, 0, cols)
    spread = (source == wanted).astype(bf16)
    high, low = split(jnp.concatenate(parts, axis=0))
    mixed = dot(high, spread) + dot(low, spread)
    halo = [mixed[p * rows : (p + 1) * rows, i * cols : (i + 1) * cols] for p in range(2) for i in range(2)]
    coriolis = coriolis_of(dims, ids)
    push = -0.5 * pressure_scale * gravity
    top, bottom = row == rows - 1, row == 0

    def one(j, below):
        k = levels - 1 - j
        here = level_at(k, rows)
        east_own, west_own = coef[0, here, :], coef[1, here, :]
        north_own = jnp.where(top, 0.0, coef[2, here, :])
        south_own = jnp.where(bottom, 0.0, coef[3, here, :])
        mids, around = [], []
        for f in range(4):
            w = proj[f, here, :]
            mids.append(w)
            side = turn(halo[f], 2 * cols - 2 * k - 1)
            around.append((*insert(lane, w, side, side), *inner(row, w)))
        below = below + ((around[2][0] - around[2][1]) + (around[3][2] - around[3][3]))
        buoyancy = push * below
        for f in range(2):
            w, (ww, we, ws, wn) = mids[f], around[f]
            q = w + ((east_own * (we - w) + west_own * (w - ww)) + (north_own * (wn - w) + south_own * (w - ws)))
            out[f, here, :] = q + buoyancy if f == 0 else q - haline * buoyancy
        for f in (2, 3):
            w, (ww, we, ws, wn) = mids[f], around[f]
            spin = coriolis * mids[5 - f]
            centre = (1.0 - 4.0 * viscosity) * w
            centre = centre - spin if f == 2 else centre + spin
            out[f, here, :] = centre + viscosity * ((we + ww) + (wn + ws))
        return below

    each_level(levels, one, jnp.zeros((rows, cols), f32))


def plane_of(ref, j, levels):
    return ref[pl.ds(j * levels, levels), :]


def rows_kernel(first, dims, ids, *refs):
    levels, _, cols, half, pair = dims
    count = 1 if pair else 2
    new, const, *refs = (refs[i * count : (i + 1) * count] for i in range(len(refs) // count + 1))
    turned_high, turned_low, thin = refs[2:5] if first else refs[:3]
    outs, lines = refs[:2] if first else refs[3:5]
    (scratch,) = refs[5]
    at_edge = pl.ds(ids[2], 1)
    for h in range(count):
        if first:
            size = block_shape(levels)
            packed = const[h][pl.ds(6 * levels, size), :]
            square = jnp.concatenate([packed[:, :levels], turn(packed, half)[:, :levels]], axis=0)
            eye = (iota((levels, levels), 0) == iota((levels, levels), 1)).astype(bf16)
            pick = (iota((levels, cols), 0) == ids[2]).astype(bf16)
            turned = tuple(dot(eye, piece, ((1,), (1,))).astype(bf16) for piece in split(square))
            turned_high[h][...], turned_low[h][...] = turned
            thin[h][...] = dot(turned[0], pick) + dot(turned[1], pick)
        turned = (turned_high[h][...], turned_low[h][...])
        both = dot3(turned, split(jnp.concatenate([plane_of(new[h], f, levels) for f in range(4)], axis=1)))
        for f in range(4):
            scratch[f] = both[:, f * cols : (f + 1) * cols]
        lines[h][...] = jnp.zeros_like(lines[h])
        wet = plane_of(const[h], 4, levels)
        for j in range(4):
            lines[h][pl.ds(j, 1), :] = scratch[j, at_edge, :]
            outs[h][j] = wet * scratch[j]
        lines[h][pl.ds(4, 1), :] = thin[h][at_edge, :]
        outs[h][4] = wet * thin[h][...]


def project_kernel(setup, dims, ids, t, s, u, v, sea, *rest):
    levels, rows, cols, half, pair = dims
    if setup:
        inverse, coupled, proj, planes, *rest = rest
        lat_out, (spike, w_high, w_low, p_high, p_low, spike_packed, corner, b_plane, cells, wide) = rest[:-10], rest[-10:]
        n = levels * rows
        for y in range(rows):
            cells[pl.ds(y, levels, stride=rows), :] = inverse[y]
        pieces = split(cells[...])
        pick = (iota((n, levels), 0) // rows == iota((n, levels), 1)).astype(bf16)
        same = (iota((n, n), 0) % rows) == (iota((n, n), 1) % rows)
        for piece, out in zip(pieces, (w_high, w_low)):
            full = dot(pick, piece, ((1,), (1,)))
            out[...] = jnp.where(same, full, 0.0).astype(bf16)
        wide[...] = jnp.zeros_like(wide)
        for y in range(rows):
            wide[y, pl.ds(0, levels), pl.ds(0, levels)] = inverse[y]
            wide[y, pl.ds(half, levels), pl.ds(half, levels)] = inverse[y]
        high, low = split(wide[...].reshape(rows * cols, cols))
        p_high[...] = high
        p_low[...] = low
        spike_packed[...] = jnp.zeros_like(spike_packed)
        for y in range(rows):
            line = inverse[y, pl.ds(ids[2], 1), :]
            spike_packed[pl.ds(y, 1), pl.ds(0, levels)] = line
            spike_packed[pl.ds(y, 1), pl.ds(half, levels)] = line
    else:
        coupled, corner, b_plane, w_high, w_low, proj, planes, *lat_out = rest
    w = (w_high[...], w_low[...])
    for f, (x, y) in enumerate(((t, s), (u, v))):
        both = dot3(w, split(jnp.concatenate([x[...], y[...]], axis=1)))
        proj[2 * f] = both[:, :cols]
        proj[2 * f + 1] = both[:, cols:]
    edge = pl.ds(pl.multiple_of(ids[2] * rows, rows), rows)
    zero = jnp.zeros((rows, cols), f32)
    if setup:
        n = levels * rows
        pick = (iota((n, cols), 0) // rows == ids[2]).astype(bf16)
        spike[...] = dot(w[0], pick) + dot(w[1], pick)
        corner[...] = spike[edge, :]
    for f in range(4):
        planes[f] = proj[f, edge, :]

    def one(k, sums):
        here = level_at(k, rows)
        wet = sea[here, :].astype(f32)
        values = [wet * proj[f, here, :] for f in range(4)]
        for f in range(4):
            proj[f, here, :] = values[f]
        sums = [sums[0] + values[2], sums[1] + values[3], *sums[2:]]
        if setup:
            value = wet * spike[here, :]
            spike[here, :] = value
            sums[2] = sums[2] + value
        return tuple(sums)

    sums = each_level(levels, one, (zero,) * (3 if setup else 2))
    if setup:
        b_plane[...] = sums[2]
    sums = [sums[0], sums[1], b_plane[...]]
    for j in range(3):
        planes[4 + j] = sums[j]
    lines = [planes[f] for f in range(4)] + [sums[1], sums[2], corner[...], coupled[...]]
    for which, row in enumerate(row_choices(pair, rows, ids[0])):
        for j, value in enumerate(lines):
            if pair:
                line = jnp.where(row == 0, value[0:1], value[rows - 1 : rows])
            else:
                line = value[row : row + 1]
            lat_out[which][pl.ds(j, 1), :] = line


def side_kernel(dims, ids, near, far, near_const, far_const, planes, corner, spike_packed, p_high, p_low, msg, proj):
    _, rows, cols, half, _ = dims
    lane = iota((rows, cols), 1)
    row = iota((rows, cols), 0)
    (west0, east0), (west1, east1) = (by_side(ids, near, far, j) for j in range(2))
    packed = (west0, west1, east0, east1)
    chunks = []
    for y in range(rows):
        chunks.append(jnp.concatenate([jnp.where(row == y, x, 0.0) for x in packed], axis=0))
    lhs = jnp.concatenate(chunks, axis=1)
    out = dot3(split(lhs), (p_high[...], p_low[...]))
    for j in range(4):
        proj[j] = out[j * rows : (j + 1) * rows]
    for j in range(7):
        msg[j] = planes[j]
    edge = ids[2]
    misc = jnp.zeros((rows, cols), f32)
    spk = spike_packed[...]
    for side, wet in enumerate(by_side(ids, near_const, far_const, 2)):
        wet = jnp.where(lane < half, wet, 0.0)
        for p in range(2):
            value = out[(2 * side + p) * rows : (2 * side + p + 1) * rows]
            for i in range(2):
                column = jnp.sum(jnp.where(lane == edge + i * half, value, 0.0), axis=1, keepdims=True)
                misc = jnp.where(lane == side * 8 + 2 * p + i, column, misc)
            if p == 1:
                column = jnp.sum(wet * value, axis=1, keepdims=True)
                misc = jnp.where(lane == side * 8 + 4, column, misc)
        column = jnp.sum(wet * spk, axis=1, keepdims=True)
        misc = jnp.where(lane == side * 8 + 5, column, misc)
    msg[7] = jnp.where(lane == CORNER_LANE, corner[...], misc)


def apply_kernel(step, final, dims, ids, coupled, proj, spike, mine, theirs, base, coef, factor, beside, *rest):
    levels, rows, cols, _, pair = dims
    count = 1 if pair else 2
    row_proj, row_line, row_const, row_late, row_far = (rest[i * count : (i + 1) * count] for i in range(5))
    rest = rest[5 * count :]
    if final:
        outs, (extras, work, sems) = rest[:4], rest[4:]
    else:
        late_out, outs, lat_msgs, extras = rest[0], rest[1:5], rest[5:-1], rest[-1]
        work = outs
    lat, depth, parts = ids[0], ids[1], ids[3]
    lane = iota((rows, cols), 1)
    row = iota((rows, cols), 0)
    has_north = jnp.where(lat < parts - 1, 1.0, 0.0)
    has_south = jnp.where(lat > 0, 1.0, 0.0)

    c = coupled[...]
    own_corner = lane_of(mine[7], CORNER_LANE)
    other_corner = lane_of(theirs[7], CORNER_LANE)
    scaled = c / (1.0 - c * c * own_corner * other_corner)
    co, cm = c * other_corner, c * own_corner
    carried = [scaled * (theirs[f] + co * mine[f]) for f in range(4)]
    misc = theirs[7]
    carried_side = scaled * (misc + co * mine[7])
    theirs_side = scaled * (mine[7] + cm * misc)

    row_solved, row_sums = [], []
    for h in range(count):
        far, line = row_far[h], row_line[h]
        c_row, other, own = far[7:8, :], far[6:7, :], line[4:5, :]
        scaled_row = c_row / (1.0 - c_row * c_row * own * other)
        joined = [scaled_row * (far[f : f + 1, :] + c_row * other * line[f : f + 1, :]) for f in range(4)]
        row_solved.append([row_proj[h][f] + row_proj[h][4] * joined[f] for f in range(4)])
        theirs_v = scaled_row * (line[3:4, :] + c_row * own * far[3:4, :])
        row_sums.append(far[4:5, :] + far[5:6, :] * theirs_v)

    sum_u = theirs[4] + theirs[6] * (scaled * (mine[2] + cm * theirs[2]))
    sum_v = theirs[5] + theirs[6] * (scaled * (mine[3] + cm * theirs[3]))
    side_u = [lane_of(misc, q * 8 + 4) + lane_of(misc, q * 8 + 5) * lane_of(theirs_side, q * 8 + 2) for q in (0, 1)]
    west_u, east_u = insert(lane, sum_u, *side_u)
    south_v = jnp.where(row == 0, row_sums[-1] * has_south, pltpu.roll(sum_v, 1, 0))
    north_v = jnp.where(row == rows - 1, row_sums[0] * has_north, pltpu.roll(sum_v, rows - 1, 0))
    upper = jnp.where(depth == 0, 1.0, 0.0)
    deeper = (west_u - east_u + south_v - north_v) * upper

    coriolis = coriolis_of(dims, ids)
    push = -0.5 * pressure_scale * gravity
    around = []
    for f in range(4):
        west, east = insert(lane, carried[f], lane_of(carried_side, f), lane_of(carried_side, 8 + f))
        south, north = inner(row, carried[f])
        around.append((east, west, north, south))
    plain = 1.0 - 4.0 * viscosity
    mids = (plain * carried[2] - coriolis * carried[3], plain * carried[3] + coriolis * carried[2])

    later = (iota((levels, levels), 1) >= iota((levels, levels), 0)).astype(bf16)
    for h in range(count):
        if pair:
            at, sign = jnp.where(lat == 0, rows - 1, 0), jnp.where(lat == 0, -1.0, 1.0)
        else:
            at, sign = ((rows - 1, -1.0), (0, 1.0))[h]
        take = lambda ref: take_row(ref, at, levels, rows)
        pick = lambda plane: (
            jnp.where(lat == 0, plane[rows - 1 : rows], plane[0:1]) if pair else plane[at : at + 1]
        )
        beyond = row_solved[h]
        wet = plane_of(row_const[h], 4, levels)
        late = plane_of(row_const[h], 5, levels) if step else plane_of(row_late[h], 4, levels)
        if pair:
            own = jnp.where(
                lat == 0,
                coef[2, pl.ds(rows - 1, levels, stride=rows), :],
                coef[3, pl.ds(0, levels, stride=rows), :],
            )
            gate = own * jnp.where(lat == 0, wet, -late)
        else:
            gate = coef[2 + h, pl.ds(at, levels, stride=rows), :] * (-late if h else wet)
        high, low = split(push * sign * beyond[3])
        rise = dot(later, high) + dot(later, low)
        spk = take(spike)
        for f in range(2):
            mid = take(proj.at[f]) + spk * pick(carried[f])
            flow = gate * (beyond[f] - mid)
            extras[h, f] = flow + rise if f == 0 else flow - haline * rise
        for f in (2, 3):
            extras[h, f] = viscosity * beyond[f]

    def one(k, below):
        here = level_at(k, rows)
        sides = [beside[j, here, :] for j in range(4)]
        moved = [[side * plane for side, plane in zip(sides, around[f])] for f in (2, 3)]
        below = below + ((moved[0][1] - moved[0][0]) + (moved[1][3] - moved[1][2]))
        buoyancy = push * below
        factors = [factor[j, here, :] for j in range(5)]
        for f in range(2):
            q = base[f, here, :] + factors[0] * carried[f]
            q = q + (
                (factors[1] * around[f][0] + factors[2] * around[f][1])
                + (factors[3] * around[f][2] + factors[4] * around[f][3])
            )
            place(f)[here, :] = q + buoyancy if f == 0 else q - haline * buoyancy
        spk = spike[here, :]
        for i in range(2):
            total = (moved[i][0] + moved[i][1]) + (moved[i][2] + moved[i][3])
            place(2 + i)[here, :] = base[2 + i, here, :] + (spk * mids[i] + viscosity * total)
        return below

    place = (lambda f: work.at[f]) if final else (lambda f: outs[f])
    below, moves = deeper, []
    parts_of = CHUNKS if final else 1
    size = levels // parts_of
    for part in reversed(range(parts_of)):
        for k in reversed(range(part * size, (part + 1) * size)):
            below = one(k, below)
        for h in range(count):
            ends = ((rows - 1, has_north), (0, has_south))
            for spot, mask in ends if pair else ends[h : h + 1]:
                there = pl.ds(part * size * rows + spot, size, stride=rows)
                for f in range(4):
                    target = place(f)
                    target[there, :] = target[there, :] + mask * extras[h, f, pl.ds(part * size, size), :]
        if final:
            there = pl.ds(part * size * rows, size * rows)
            for f in range(4):
                move = pltpu.make_async_copy(work.at[f, there], outs[f].at[there], sems.at[4 * part + f])
                move.start()
                moves.append(move)
    for move in moves:
        move.wait()

    if not final:
        for which, at in enumerate(row_choices(pair, rows, lat)):
            for f in range(4):
                lat_msgs[which][pl.ds(f * levels, levels), :] = take_row(outs[f], at, levels, rows)
            lat_msgs[which][pl.ds(4 * levels, levels), :] = late_out[...]


def places(levels):
    lat, depth, lon = (lax.axis_index(a) for a in ("lat", "depth", "lon"))
    return lat, depth, (levels - 1) * (1 - depth), lax.axis_size("lat"), lax.rem(lon, 2)


def call(kernel, dims, outs, args, smem=(), scratch=(), hbm=(), out_space=pltpu.VMEM):
    spaces = [pltpu.SMEM if i in smem else pltpu.HBM if i in hbm else pltpu.VMEM for i in range(len(args))]

    def run(*refs):
        kernel(dims, places(dims[0]), *refs)

    return pl.pallas_call(
        run,
        out_shape=[jax.ShapeDtypeStruct(shape, kind) for shape, kind in outs],
        in_specs=[pl.BlockSpec(memory_space=space) for space in spaces],
        out_specs=[pl.BlockSpec(memory_space=out_space)] * len(outs),
        scratch_shapes=list(scratch),
        compiler_params=pltpu.CompilerParams(vmem_limit_bytes=VMEM_BYTES),
    )(*args)


def on_device(
    adj_temp,
    adj_salt,
    adj_zonal,
    adj_merid,
    east_speed,
    north_speed,
    branch_flags,
    sea_mask,
    block_inverse,
    coupling,
):
    levels, rows, cols = adj_temp.shape
    half = cols // 2
    lons, lats, depths = (lax.axis_size(a) for a in ("lon", "lat", "depth"))
    pair = lats == 2
    dims = (levels, rows, cols, half, pair)
    count = 1 if pair else 2
    n = levels * rows
    flat = lambda x: x.reshape(x.shape[:-3] + (n, cols))
    sea, east, north, flags = flat(sea_mask), flat(east_speed), flat(north_speed), flat(branch_flags)
    state = [flat(x) for x in (adj_temp, adj_salt, adj_zonal, adj_merid)]
    plane = (rows, cols)
    grid = (levels, cols)

    assert lons % 2 == 0
    close = [(i, i ^ 1) for i in range(lons)]
    apart = [(i, (i + 1 if i % 2 else i - 1) % lons) for i in range(lons)]
    up = [(i, i + 1) for i in range(lats - 1)]
    down = [(b, a) for a, b in up]

    def to_lat(msgs, flip):
        routes = [up + down] if pair else [down, up]
        if not flip:
            return [lax.ppermute(m, "lat", r) for m, r in zip(msgs, routes)]
        both = [
            [(a * depths + d, b * depths + (depths - 1 - d)) for a, b in r for d in range(depths)] for r in routes
        ]
        return [lax.ppermute(m, ("lat", "depth"), r) for m, r in zip(msgs, both)]

    def to_depth(msg):
        return lax.ppermute(msg, "depth", [(d, depths - 1 - d) for d in range(depths)])

    sources = (*state, sea, east, north, flags, block_inverse)
    sources = tuple(pltpu.with_memory_space_constraint(x, pltpu.HBM) for x in sources)
    full = 6 * levels + block_shape(levels)
    late, coupled, *rest = call(
        fetch_kernel,
        dims,
        [(grid, f32), (plane, f32)]
        + [((full, cols), f32)] * count
        + [(x.shape, x.dtype) for x in sources],
        (pltpu.with_memory_space_constraint(coupling.reshape(1, rows), pltpu.HBM), *sources),
        (),
        (pltpu.VMEM((1, rows), f32), pltpu.SemaphoreType.DMA((10,))),
        range(10),
    )
    lat_msgs, rest = rest[:count], rest[count:]
    state, (sea, east, north, flags, block_inverse) = rest[:4], rest[4:]

    def to_lon(step, state, *more):
        near, far = call(
            functools.partial(edges_kernel, step == STEPS - 1),
            dims,
            [((4 if more else 2,) + plane, f32)] * 2,
            (*state, *more),
        )
        near = lax.ppermute(near, "lon", close)
        far = lax.ppermute(far, "lon", apart)
        return near, far

    row_const = row_new = to_lat(lat_msgs, False)
    near_const, far_const = near, far = to_lon(STEPS - 1, state, sea, east, flags)

    for step in reversed(range(STEPS)):
        first = step == STEPS - 1
        outs = [((4, n, cols), f32), ((7,) + plane, f32)] + [(plane, f32)] * count
        if first:
            outs += [((n, cols), f32)] + [((n, n), bf16)] * 2 + [((rows * cols, cols), bf16)] * 2 + [(plane, f32)] * 3
            args = (*state, sea, block_inverse, coupled)
            scratch = (pltpu.VMEM((n, levels), f32), pltpu.VMEM((rows, cols, cols), f32))
        else:
            args = (*state, sea, coupled, corner, b_plane, w_high, w_low)
            scratch = ()
        proj, planes, *more = call(functools.partial(project_kernel, first), dims, outs, args, (), scratch)
        far_msgs = more[:count]
        if first:
            spike, w_high, w_low, p_high, p_low, spike_packed, corner, b_plane = more[count:]
        row_far = to_lat(far_msgs, True)
        mine, side_proj = call(
            side_kernel,
            dims,
            [((8,) + plane, f32), ((4,) + plane, f32)],
            (near, far, near_const, far_const, planes, corner, spike_packed, p_high, p_low),
        )
        theirs = to_depth(mine)
        coef, factor, *more = call(
            functools.partial(coef_kernel, step),
            dims,
            [((4, n, cols), f32), ((5, n, cols), f32)] + [((4, n, cols), f32)] * first,
            (sea, east, north, flags, near_const, far_const, spike, spike_packed),
        )
        if first:
            (beside,) = more
        (base,) = call(base_kernel, dims, [((4, n, cols), f32)], (proj, side_proj, near_const, far_const, coef))
        block = ((levels, levels), bf16)
        rows_out = call(
            functools.partial(rows_kernel, first),
            dims,
            [((5,) + grid, f32)] * count
            + [(plane, f32)] * count
            + ([block] * (2 * count) + [(grid, f32)] * count) * first,
            (*row_new, *row_const, *(() if first else row_block)),
            scratch=(pltpu.VMEM((4,) + grid, f32),),
        )
        if first:
            row_block = rows_out[2 * count :]
        rows_out = rows_out[: 2 * count]
        final = step == 0
        outs, extra = [((n, cols), f32)] * 4, ()
        if not final:
            outs = outs + [((5 * levels, cols), f32)] * count
            extra = (late,)
        result = call(
            functools.partial(apply_kernel, step, final),
            dims,
            outs,
            (
                coupled, proj, spike, mine, theirs, base, coef, factor, beside,
                *rows_out, *row_const, *row_new, *row_far, *extra,
            ),
            scratch=(pltpu.VMEM((count, 4) + grid, f32),)
            + ((pltpu.VMEM((4, n, cols), f32), pltpu.SemaphoreType.DMA((4 * CHUNKS,))) if final else ()),
            out_space=pltpu.HBM if final else pltpu.VMEM,
        )
        state = result[:4]
        if not final:
            row_new = to_lat(result[4:], False)
            near, far = to_lon(0, state)
    return tuple(x.reshape(levels, rows, cols) for x in state)


def solution(mesh):
    in_specs = (
        P("depth", "lat", "lon"),
        P("depth", "lat", "lon"),
        P("depth", "lat", "lon"),
        P("depth", "lat", "lon"),
        P("depth", "lat", "lon"),
        P("depth", "lat", "lon"),
        P(None, "depth", "lat", "lon"),
        P("depth", "lat", "lon"),
        P("lat", "depth", None),
        P("lat"),
    )
    out_specs = (
        P("depth", "lat", "lon"),
        P("depth", "lat", "lon"),
        P("depth", "lat", "lon"),
        P("depth", "lat", "lon"),
    )

    return jax.shard_map(on_device, mesh=mesh, in_specs=in_specs, out_specs=out_specs, check_vma=False)
```

```python
import functools

import jax
import jax.numpy as jnp
from jax import lax
from jax.experimental import pallas as pl
from jax.experimental.pallas import tpu as pltpu
from jax.sharding import PartitionSpec as P

STEPS = 2

advect_scale = 0.25
diffusion = 0.5
gravity = 0.1
pressure_scale = 1.0
viscosity = 0.1
haline = 0.8

BLOCK = 48
VMEM_BYTES = 16 * 1024 * 1024
f32 = jnp.float32
CHUNKS = 3
bf16 = jnp.bfloat16
CORNER_LANE = 16


def split(value):
    high = value.astype(bf16)
    return high, (value - high.astype(f32)).astype(bf16)


def dot(a, b, contract=((1,), (0,))):
    return lax.dot_general(a, b, (contract, ((), ())), preferred_element_type=f32)


def dot3(a, b):
    return dot(a[0], b[0]) + (dot(a[0], b[1]) + dot(a[1], b[0]))


def iota(shape, dim):
    return lax.broadcasted_iota(jnp.int32, shape, dim)


def branches(flags):
    one = jnp.where(flags >= 3, 1, 0) + jnp.where(flags >= 6, 1, 0)
    zonal = (flags - 3 * one).astype(f32) * 0.5
    return zonal, one.astype(f32) * 0.5


def lane_of(value, lane):
    return jnp.broadcast_to(value[:, lane : lane + 1], value.shape)


def level_at(k, rows):
    return pl.ds(k * rows if isinstance(k, int) else pl.multiple_of(k * rows, rows), rows)


def level(ref, k, rows):
    return ref[level_at(k, rows), :]


def turn(value, shift):
    return pltpu.roll(value, shift % value.shape[1], 1)


def each_level(levels, body, carry):
    block = min(BLOCK, levels)

    def some(b, carry):
        for i in range(block):
            carry = body(b * block + i, carry)
        return carry

    if block == levels:
        return some(0, carry)
    return lax.fori_loop(0, levels // block, some, carry)


def take_row(ref, row, levels, rows):
    if isinstance(row, int):
        return ref[pl.ds(row, levels, stride=rows), :]
    low = ref[pl.ds(0, levels, stride=rows), :]
    high = ref[pl.ds(rows - 1, levels, stride=rows), :]
    return jnp.where(row == 0, low, high)


def by_side(ids, near, far, j):
    even = ids[4] == 0
    return jnp.where(even, far[j], near[j]), jnp.where(even, near[j], far[j])


def to_pairs(ids, near, far, j, to_east, to_west):
    even = ids[4] == 0
    near[j] = jnp.where(even, to_east, to_west)
    far[j] = jnp.where(even, to_west, to_east)


def row_choices(pair, rows, lat):
    return [jnp.where(lat == 0, rows - 1, 0)] if pair else [0, rows - 1]


def block_shape(levels):
    return levels // 2


def fetch_kernel(dims, ids, *refs):
    levels, rows, cols, half, pair = dims
    coup, sources, (nn_late, coupled), rest = refs[0], refs[1:10], refs[10:12], refs[12:]
    count = 1 if pair else 2
    lat_msgs, copies, (coup_here, sems) = rest[:count], rest[count : count + 9], rest[count + 9 :]
    moves = [pltpu.make_async_copy(a, b, sems.at[i]) for i, (a, b) in enumerate(zip(sources, copies))]
    moves.append(pltpu.make_async_copy(coup, coup_here, sems.at[9]))
    for move in moves:
        move.start()
    t, s, u, v, sea, _, north, flags, inverse = copies
    for move in moves:
        move.wait()
    spot = iota((rows, rows), 0) == iota((rows, rows), 1)
    value = jnp.sum(jnp.where(spot, coup_here[...], 0.0), axis=1, keepdims=True)
    coupled[...] = jnp.broadcast_to(value, (rows, cols))
    for which, row in enumerate(row_choices(pair, rows, ids[0])):
        msg = lat_msgs[which]

        def put(j, value):
            msg[pl.ds(j * levels, levels), :] = value

        for j, x in enumerate((t, s, u, v)):
            put(j, take_row(x, row, levels, rows))
        wet = take_row(sea, row, levels, rows).astype(f32)
        speed = take_row(north, row, levels, rows)
        put(4, wet)
        for step in (1, 0):
            _, merid = branches(take_row(flags.at[step], row, levels, rows))
            value = wet * (speed * merid - diffusion)
            if step:
                put(5, value)
            elif pair or row:
                nn_late[...] = value
        if pair:
            block = jnp.where(row == 0, inverse[0], inverse[rows - 1])
        else:
            block = inverse[row]
        size = block_shape(levels)
        last = pl.ds(6 * levels, size)
        msg[last, :] = jnp.zeros((size, cols), f32)
        msg[last, pl.ds(0, levels)] = block[:size]
        msg[last, pl.ds(half, levels)] = block[size:]


def edges_kernel(first, dims, ids, t, s, u, v, *refs):
    levels, rows, cols, half, _ = dims
    lane = iota((rows, cols), 1)
    sea, east, flags, near, far = refs if first else (None, None, None, *refs)
    to_pairs(ids, near, far, 0, *edge_columns(levels, rows, t, s, 2))
    to_pairs(ids, near, far, 1, *edge_columns(levels, rows, u, v, 2))
    if first:
        wet, first_wet = edge_columns(levels, rows, sea, east, 2)
        flag, _ = edge_columns(levels, rows, flags.at[1], flags.at[0], 1)
        speed = turn(wet, half)
        zonal = branches(jnp.round(flag).astype(jnp.int32))[0]
        nexts = [wet * (speed * z - diffusion) for z in (zonal, turn(zonal, half))]
        to_pairs(ids, near, far, 2, jnp.where(lane < half, wet, turn(nexts[0], half)), first_wet)
        to_pairs(ids, near, far, 3, nexts[1], nexts[1])


def edge_columns(levels, rows, x, y, pieces):
    cols = x.shape[1]
    half = cols // 2
    source, target = iota((2 * cols, 2 * cols), 0), iota((2 * cols, 2 * cols), 1)
    column = jnp.where(target < cols, cols - 1, 0) + jnp.where(target % cols < half, 0, cols)
    spread = (source == column).astype(bf16)
    both = jnp.concatenate([x[...].astype(f32), y[...].astype(f32)], axis=1)
    high, low = split(both)
    wide = dot(high, spread)
    if pieces == 2:
        wide = wide + dot(low, spread)
    place = iota((rows, 2 * cols), 1) % half
    out = jnp.zeros((rows, 2 * cols), f32)
    for k in range(levels):
        out = jnp.where(place == k, wide[k * rows : (k + 1) * rows], out)
    return out[:, :cols], out[:, cols:]


def insert(lane, value, west_in, east_in):
    cols = value.shape[1]
    return (
        jnp.where(lane == 0, west_in, turn(value, 1)),
        jnp.where(lane == cols - 1, east_in, turn(value, cols - 1)),
    )


def inner(row, value):
    rows = value.shape[0]
    return (
        jnp.where(row == 0, 0.0, pltpu.roll(value, 1, 0)),
        jnp.where(row == rows - 1, 0.0, pltpu.roll(value, rows - 1, 0)),
    )


def coef_kernel(step, dims, ids, sea, east, north, flags, near, far, spike, spike_packed, out, factor, *beside):
    levels, rows, cols, half, _ = dims
    lane, row = iota((rows, cols), 1), iota((rows, cols), 0)
    west_const, sea_side = by_side(ids, near, far, 2)
    next_side = west_const if step else by_side(ids, near, far, 3)[0]
    spk = spike_packed[...]
    spike_west = jnp.where(lane < half, west_const, 0.0) * spk
    spike_east = jnp.where(lane < half, sea_side, 0.0) * spk

    def one(k, carry):
        wet = level(sea, k, rows).astype(f32)
        part = advect_scale * wet
        speed_e, speed_n = level(east, k, rows), level(north, k, rows)
        sea_east = jnp.where(lane == cols - 1, turn(sea_side, cols - 1 - k), turn(wet, cols - 1))
        sea_north = jnp.where(row == rows - 1, 1.0, pltpu.roll(wet, rows - 1, 0))
        here = level_at(k, rows)
        mid = level(spike, k, rows)
        west, east_ = insert(lane, mid, turn(spike_west, cols - k), turn(spike_east, cols - 1 - k))
        south, north_ = inner(row, mid)
        for ref in beside:
            for j, value in enumerate((east_, west, north_, south)):
                ref[j, here, :] = value
        zonal, merid = branches(level(flags.at[step], k, rows))
        speed_z, speed_m = speed_e * zonal, speed_n * merid
        east_own = part * (speed_e - speed_z + diffusion) * sea_east
        next_west = jnp.where(
            lane == 0, turn(next_side, 2 * cols - step * half - k), turn(wet * (speed_z - diffusion), 1)
        )
        west_own = part * next_west
        north_own = part * (speed_n - speed_m + diffusion) * sea_north
        next_south = jnp.where(row == 0, 1.0, pltpu.roll(wet * (speed_m - diffusion), 1, 0))
        south_own = part * next_south
        for j, value in enumerate((east_own, west_own, north_own, south_own)):
            out[j, here, :] = value
        inside_n = jnp.where(row == rows - 1, 0.0, north_own)
        inside_s = jnp.where(row == 0, 0.0, south_own)
        factor[0, here, :] = mid * (1.0 + ((west_own - east_own) + (inside_s - inside_n)))
        factor[1, here, :] = east_own * east_
        factor[2, here, :] = -west_own * west
        factor[3, here, :] = inside_n * north_
        factor[4, here, :] = -inside_s * south
        return carry

    each_level(levels, one, ())


def coriolis_of(dims, ids):
    _, rows, cols, _, _ = dims
    index = (ids[0] * rows + iota((rows, cols), 0)).astype(f32)
    return 0.2 + 0.6 * (index + 0.5) / (rows * ids[3])


def base_kernel(dims, ids, proj, side_proj, near, far, coef, out):
    levels, rows, cols, half, _ = dims
    lane, row = iota((rows, cols), 1), iota((rows, cols), 0)
    parts = []
    for p in range(2):
        line = []
        for side, const in enumerate(by_side(ids, near, far, 2)):
            wet = jnp.where(lane < half, const, turn(const, half))
            line.append(wet * side_proj[2 * side + p])
        parts.append(jnp.concatenate(line, axis=1))
    source, target = iota((2 * cols, 2 * cols), 0), iota((2 * cols, 2 * cols), 1)
    pick = target % cols
    wanted = pick // 2 + jnp.where(target < cols, 0, half) + jnp.where(pick % 2 == 1, 0, cols)
    spread = (source == wanted).astype(bf16)
    high, low = split(jnp.concatenate(parts, axis=0))
    mixed = dot(high, spread) + dot(low, spread)
    halo = [mixed[p * rows : (p + 1) * rows, i * cols : (i + 1) * cols] for p in range(2) for i in range(2)]
    coriolis = coriolis_of(dims, ids)
    push = -0.5 * pressure_scale * gravity
    top, bottom = row == rows - 1, row == 0

    def one(j, below):
        k = levels - 1 - j
        here = level_at(k, rows)
        east_own, west_own = coef[0, here, :], coef[1, here, :]
        north_own = jnp.where(top, 0.0, coef[2, here, :])
        south_own = jnp.where(bottom, 0.0, coef[3, here, :])
        mids, around = [], []
        for f in range(4):
            w = proj[f, here, :]
            mids.append(w)
            side = turn(halo[f], 2 * cols - 2 * k - 1)
            around.append((*insert(lane, w, side, side), *inner(row, w)))
        below = below + ((around[2][0] - around[2][1]) + (around[3][2] - around[3][3]))
        buoyancy = push * below
        for f in range(2):
            w, (ww, we, ws, wn) = mids[f], around[f]
            q = w + ((east_own * (we - w) + west_own * (w - ww)) + (north_own * (wn - w) + south_own * (w - ws)))
            out[f, here, :] = q + buoyancy if f == 0 else q - haline * buoyancy
        for f in (2, 3):
            w, (ww, we, ws, wn) = mids[f], around[f]
            spin = coriolis * mids[5 - f]
            centre = (1.0 - 4.0 * viscosity) * w
            centre = centre - spin if f == 2 else centre + spin
            out[f, here, :] = centre + viscosity * ((we + ww) + (wn + ws))
        return below

    each_level(levels, one, jnp.zeros((rows, cols), f32))


def plane_of(ref, j, levels):
    return ref[pl.ds(j * levels, levels), :]


def rows_kernel(first, dims, ids, *refs):
    levels, _, cols, half, pair = dims
    count = 1 if pair else 2
    new, const, *refs = (refs[i * count : (i + 1) * count] for i in range(len(refs) // count + 1))
    turned_high, turned_low, thin = refs[2:5] if first else refs[:3]
    outs, lines = refs[:2] if first else refs[3:5]
    (scratch,) = refs[5]
    at_edge = pl.ds(ids[2], 1)
    for h in range(count):
        if first:
            size = block_shape(levels)
            packed = const[h][pl.ds(6 * levels, size), :]
            square = jnp.concatenate([packed[:, :levels], turn(packed, half)[:, :levels]], axis=0)
            pick = (iota((levels, cols), 0) == ids[2]).astype(bf16)
            turned = split(square.T)
            turned_high[h][...], turned_low[h][...] = turned
            thin[h][...] = dot(turned[0], pick) + dot(turned[1], pick)
        turned = (turned_high[h][...], turned_low[h][...])
        both = dot3(turned, split(jnp.concatenate([plane_of(new[h], f, levels) for f in range(4)], axis=1)))
        for f in range(4):
            scratch[f] = both[:, f * cols : (f + 1) * cols]
        lines[h][...] = jnp.zeros_like(lines[h])
        wet = plane_of(const[h], 4, levels)
        for j in range(4):
            lines[h][pl.ds(j, 1), :] = scratch[j, at_edge, :]
            outs[h][j] = wet * scratch[j]
        lines[h][pl.ds(4, 1), :] = thin[h][at_edge, :]
        outs[h][4] = wet * thin[h][...]


def project_kernel(setup, dims, ids, t, s, u, v, sea, *rest):
    levels, rows, cols, half, pair = dims
    if setup:
        inverse, coupled, proj, planes, *rest = rest
        lat_out, (spike, w_high, w_low, p_high, p_low, spike_packed, corner, b_plane, cells, wide) = rest[:-10], rest[-10:]
        n = levels * rows
        for y in range(rows):
            cells[pl.ds(y, levels, stride=rows), :] = inverse[y]
        pieces = split(cells[...])
        pick = (iota((n, levels), 0) // rows == iota((n, levels), 1)).astype(bf16)
        same = (iota((n, n), 0) % rows) == (iota((n, n), 1) % rows)
        for piece, out in zip(pieces, (w_high, w_low)):
            full = dot(pick, piece, ((1,), (1,)))
            out[...] = jnp.where(same, full, 0.0).astype(bf16)
        wide[...] = jnp.zeros_like(wide)
        for y in range(rows):
            wide[y, pl.ds(0, levels), pl.ds(0, levels)] = inverse[y]
            wide[y, pl.ds(half, levels), pl.ds(half, levels)] = inverse[y]
        high, low = split(wide[...].reshape(rows * cols, cols))
        p_high[...] = high
        p_low[...] = low
        spike_packed[...] = jnp.zeros_like(spike_packed)
        for y in range(rows):
            line = inverse[y, pl.ds(ids[2], 1), :]
            spike_packed[pl.ds(y, 1), pl.ds(0, levels)] = line
            spike_packed[pl.ds(y, 1), pl.ds(half, levels)] = line
    else:
        coupled, corner, b_plane, w_high, w_low, proj, planes, *lat_out = rest
    w = (w_high[...], w_low[...])
    for f, (x, y) in enumerate(((t, s), (u, v))):
        both = dot3(w, split(jnp.concatenate([x[...], y[...]], axis=1)))
        proj[2 * f] = both[:, :cols]
        proj[2 * f + 1] = both[:, cols:]
    edge = pl.ds(pl.multiple_of(ids[2] * rows, rows), rows)
    zero = jnp.zeros((rows, cols), f32)
    if setup:
        n = levels * rows
        pick = (iota((n, cols), 0) // rows == ids[2]).astype(bf16)
        spike[...] = dot(w[0], pick) + dot(w[1], pick)
        corner[...] = spike[edge, :]
    for f in range(4):
        planes[f] = proj[f, edge, :]

    def one(k, sums):
        here = level_at(k, rows)
        wet = sea[here, :].astype(f32)
        values = [wet * proj[f, here, :] for f in range(4)]
        for f in range(4):
            proj[f, here, :] = values[f]
        sums = [sums[0] + values[2], sums[1] + values[3], *sums[2:]]
        if setup:
            value = wet * spike[here, :]
            spike[here, :] = value
            sums[2] = sums[2] + value
        return tuple(sums)

    sums = each_level(levels, one, (zero,) * (3 if setup else 2))
    if setup:
        b_plane[...] = sums[2]
    sums = [sums[0], sums[1], b_plane[...]]
    for j in range(3):
        planes[4 + j] = sums[j]
    lines = [planes[f] for f in range(4)] + [sums[1], sums[2], corner[...], coupled[...]]
    for which, row in enumerate(row_choices(pair, rows, ids[0])):
        for j, value in enumerate(lines):
            if pair:
                line = jnp.where(row == 0, value[0:1], value[rows - 1 : rows])
            else:
                line = value[row : row + 1]
            lat_out[which][pl.ds(j, 1), :] = line


def side_kernel(dims, ids, near, far, near_const, far_const, planes, corner, spike_packed, p_high, p_low, msg, proj):
    _, rows, cols, half, _ = dims
    lane = iota((rows, cols), 1)
    row = iota((rows, cols), 0)
    (west0, east0), (west1, east1) = (by_side(ids, near, far, j) for j in range(2))
    packed = (west0, west1, east0, east1)
    chunks = []
    for y in range(rows):
        chunks.append(jnp.concatenate([jnp.where(row == y, x, 0.0) for x in packed], axis=0))
    lhs = jnp.concatenate(chunks, axis=1)
    out = dot3(split(lhs), (p_high[...], p_low[...]))
    for j in range(4):
        proj[j] = out[j * rows : (j + 1) * rows]
    for j in range(7):
        msg[j] = planes[j]
    edge = ids[2]
    misc = jnp.zeros((rows, cols), f32)
    spk = spike_packed[...]
    for side, wet in enumerate(by_side(ids, near_const, far_const, 2)):
        wet = jnp.where(lane < half, wet, 0.0)
        for p in range(2):
            value = out[(2 * side + p) * rows : (2 * side + p + 1) * rows]
            for i in range(2):
                column = jnp.sum(jnp.where(lane == edge + i * half, value, 0.0), axis=1, keepdims=True)
                misc = jnp.where(lane == side * 8 + 2 * p + i, column, misc)
            if p == 1:
                column = jnp.sum(wet * value, axis=1, keepdims=True)
                misc = jnp.where(lane == side * 8 + 4, column, misc)
        column = jnp.sum(wet * spk, axis=1, keepdims=True)
        misc = jnp.where(lane == side * 8 + 5, column, misc)
    msg[7] = jnp.where(lane == CORNER_LANE, corner[...], misc)


def apply_kernel(step, final, dims, ids, coupled, proj, spike, mine, theirs, base, coef, factor, beside, *rest):
    levels, rows, cols, _, pair = dims
    count = 1 if pair else 2
    row_proj, row_line, row_const, row_late, row_far = (rest[i * count : (i + 1) * count] for i in range(5))
    rest = rest[5 * count :]
    if final:
        outs, (extras, work, sems) = rest[:4], rest[4:]
    else:
        late_out, outs, lat_msgs, extras = rest[0], rest[1:5], rest[5:-1], rest[-1]
        work = outs
    lat, depth, parts = ids[0], ids[1], ids[3]
    lane = iota((rows, cols), 1)
    row = iota((rows, cols), 0)
    has_north = jnp.where(lat < parts - 1, 1.0, 0.0)
    has_south = jnp.where(lat > 0, 1.0, 0.0)

    c = coupled[...]
    own_corner = lane_of(mine[7], CORNER_LANE)
    other_corner = lane_of(theirs[7], CORNER_LANE)
    scaled = c / (1.0 - c * c * own_corner * other_corner)
    co, cm = c * other_corner, c * own_corner
    carried = [scaled * (theirs[f] + co * mine[f]) for f in range(4)]
    misc = theirs[7]
    carried_side = scaled * (misc + co * mine[7])
    theirs_side = scaled * (mine[7] + cm * misc)

    row_solved, row_sums = [], []
    for h in range(count):
        far, line = row_far[h], row_line[h]
        c_row, other, own = far[7:8, :], far[6:7, :], line[4:5, :]
        scaled_row = c_row / (1.0 - c_row * c_row * own * other)
        joined = [scaled_row * (far[f : f + 1, :] + c_row * other * line[f : f + 1, :]) for f in range(4)]
        row_solved.append([row_proj[h][f] + row_proj[h][4] * joined[f] for f in range(4)])
        theirs_v = scaled_row * (line[3:4, :] + c_row * own * far[3:4, :])
        row_sums.append(far[4:5, :] + far[5:6, :] * theirs_v)

    sum_u = theirs[4] + theirs[6] * (scaled * (mine[2] + cm * theirs[2]))
    sum_v = theirs[5] + theirs[6] * (scaled * (mine[3] + cm * theirs[3]))
    side_u = [lane_of(misc, q * 8 + 4) + lane_of(misc, q * 8 + 5) * lane_of(theirs_side, q * 8 + 2) for q in (0, 1)]
    west_u, east_u = insert(lane, sum_u, *side_u)
    south_v = jnp.where(row == 0, row_sums[-1] * has_south, pltpu.roll(sum_v, 1, 0))
    north_v = jnp.where(row == rows - 1, row_sums[0] * has_north, pltpu.roll(sum_v, rows - 1, 0))
    upper = jnp.where(depth == 0, 1.0, 0.0)
    deeper = (west_u - east_u + south_v - north_v) * upper

    coriolis = coriolis_of(dims, ids)
    push = -0.5 * pressure_scale * gravity
    around = []
    for f in range(4):
        west, east = insert(lane, carried[f], lane_of(carried_side, f), lane_of(carried_side, 8 + f))
        south, north = inner(row, carried[f])
        around.append((east, west, north, south))
    plain = 1.0 - 4.0 * viscosity
    mids = (plain * carried[2] - coriolis * carried[3], plain * carried[3] + coriolis * carried[2])

    later = (iota((levels, levels), 1) >= iota((levels, levels), 0)).astype(bf16)
    for h in range(count):
        if pair:
            at, sign = jnp.where(lat == 0, rows - 1, 0), jnp.where(lat == 0, -1.0, 1.0)
        else:
            at, sign = ((rows - 1, -1.0), (0, 1.0))[h]
        take = lambda ref: take_row(ref, at, levels, rows)
        pick = lambda plane: (
            jnp.where(lat == 0, plane[rows - 1 : rows], plane[0:1]) if pair else plane[at : at + 1]
        )
        beyond = row_solved[h]
        wet = plane_of(row_const[h], 4, levels)
        late = plane_of(row_const[h], 5, levels) if step else plane_of(row_late[h], 4, levels)
        if pair:
            own = jnp.where(
                lat == 0,
                coef[2, pl.ds(rows - 1, levels, stride=rows), :],
                coef[3, pl.ds(0, levels, stride=rows), :],
            )
            gate = own * jnp.where(lat == 0, wet, -late)
        else:
            gate = coef[2 + h, pl.ds(at, levels, stride=rows), :] * (-late if h else wet)
        high, low = split(push * sign * beyond[3])
        rise = dot(later, high) + dot(later, low)
        spk = take(spike)
        for f in range(2):
            mid = take(proj.at[f]) + spk * pick(carried[f])
            flow = gate * (beyond[f] - mid)
            extras[h, f] = flow + rise if f == 0 else flow - haline * rise
        for f in (2, 3):
            extras[h, f] = viscosity * beyond[f]

    def one(k, below):
        here = level_at(k, rows)
        sides = [beside[j, here, :] for j in range(4)]
        moved = [[side * plane for side, plane in zip(sides, around[f])] for f in (2, 3)]
        below = below + ((moved[0][1] - moved[0][0]) + (moved[1][3] - moved[1][2]))
        buoyancy = push * below
        factors = [factor[j, here, :] for j in range(5)]
        for f in range(2):
            q = base[f, here, :] + factors[0] * carried[f]
            q = q + (
                (factors[1] * around[f][0] + factors[2] * around[f][1])
                + (factors[3] * around[f][2] + factors[4] * around[f][3])
            )
            place(f)[here, :] = q + buoyancy if f == 0 else q - haline * buoyancy
        spk = spike[here, :]
        for i in range(2):
            total = (moved[i][0] + moved[i][1]) + (moved[i][2] + moved[i][3])
            place(2 + i)[here, :] = base[2 + i, here, :] + (spk * mids[i] + viscosity * total)
        return below

    place = (lambda f: work.at[f]) if final else (lambda f: outs[f])
    below, moves = deeper, []
    parts_of = CHUNKS if final else 1
    size = levels // parts_of
    for part in reversed(range(parts_of)):
        for k in reversed(range(part * size, (part + 1) * size)):
            below = one(k, below)
        for h in range(count):
            ends = ((rows - 1, has_north), (0, has_south))
            for spot, mask in ends if pair else ends[h : h + 1]:
                there = pl.ds(part * size * rows + spot, size, stride=rows)
                for f in range(4):
                    target = place(f)
                    target[there, :] = target[there, :] + mask * extras[h, f, pl.ds(part * size, size), :]
        if final:
            there = pl.ds(part * size * rows, size * rows)
            for f in range(4):
                move = pltpu.make_async_copy(work.at[f, there], outs[f].at[there], sems.at[4 * part + f])
                move.start()
                moves.append(move)
    for move in moves:
        move.wait()

    if not final:
        for which, at in enumerate(row_choices(pair, rows, lat)):
            for f in range(4):
                lat_msgs[which][pl.ds(f * levels, levels), :] = take_row(outs[f], at, levels, rows)
            lat_msgs[which][pl.ds(4 * levels, levels), :] = late_out[...]


def places(levels):
    lat, depth, lon = (lax.axis_index(a) for a in ("lat", "depth", "lon"))
    return lat, depth, (levels - 1) * (1 - depth), lax.axis_size("lat"), lax.rem(lon, 2)


def call(kernel, dims, outs, args, smem=(), scratch=(), hbm=(), out_space=pltpu.VMEM):
    spaces = [pltpu.SMEM if i in smem else pltpu.HBM if i in hbm else pltpu.VMEM for i in range(len(args))]

    def run(*refs):
        kernel(dims, places(dims[0]), *refs)

    return pl.pallas_call(
        run,
        out_shape=[jax.ShapeDtypeStruct(shape, kind) for shape, kind in outs],
        in_specs=[pl.BlockSpec(memory_space=space) for space in spaces],
        out_specs=[pl.BlockSpec(memory_space=out_space)] * len(outs),
        scratch_shapes=list(scratch),
        compiler_params=pltpu.CompilerParams(vmem_limit_bytes=VMEM_BYTES),
    )(*args)


def on_device(
    adj_temp,
    adj_salt,
    adj_zonal,
    adj_merid,
    east_speed,
    north_speed,
    branch_flags,
    sea_mask,
    block_inverse,
    coupling,
):
    levels, rows, cols = adj_temp.shape
    half = cols // 2
    lons, lats, depths = (lax.axis_size(a) for a in ("lon", "lat", "depth"))
    pair = lats == 2
    dims = (levels, rows, cols, half, pair)
    count = 1 if pair else 2
    n = levels * rows
    flat = lambda x: x.reshape(x.shape[:-3] + (n, cols))
    sea, east, north, flags = flat(sea_mask), flat(east_speed), flat(north_speed), flat(branch_flags)
    state = [flat(x) for x in (adj_temp, adj_salt, adj_zonal, adj_merid)]
    plane = (rows, cols)
    grid = (levels, cols)

    assert lons % 2 == 0
    close = [(i, i ^ 1) for i in range(lons)]
    apart = [(i, (i + 1 if i % 2 else i - 1) % lons) for i in range(lons)]
    up = [(i, i + 1) for i in range(lats - 1)]
    down = [(b, a) for a, b in up]

    def to_lat(msgs, flip):
        routes = [up + down] if pair else [down, up]
        if not flip:
            return [lax.ppermute(m, "lat", r) for m, r in zip(msgs, routes)]
        both = [
            [(a * depths + d, b * depths + (depths - 1 - d)) for a, b in r for d in range(depths)] for r in routes
        ]
        return [lax.ppermute(m, ("lat", "depth"), r) for m, r in zip(msgs, both)]

    def to_depth(msg):
        return lax.ppermute(msg, "depth", [(d, depths - 1 - d) for d in range(depths)])

    sources = (*state, sea, east, north, flags, block_inverse)
    sources = tuple(pltpu.with_memory_space_constraint(x, pltpu.HBM) for x in sources)
    full = 6 * levels + block_shape(levels)
    late, coupled, *rest = call(
        fetch_kernel,
        dims,
        [(grid, f32), (plane, f32)]
        + [((full, cols), f32)] * count
        + [(x.shape, x.dtype) for x in sources],
        (pltpu.with_memory_space_constraint(coupling.reshape(1, rows), pltpu.HBM), *sources),
        (),
        (pltpu.VMEM((1, rows), f32), pltpu.SemaphoreType.DMA((10,))),
        range(10),
    )
    lat_msgs, rest = rest[:count], rest[count:]
    state, (sea, east, north, flags, block_inverse) = rest[:4], rest[4:]

    def to_lon(step, state, *more):
        near, far = call(
            functools.partial(edges_kernel, step == STEPS - 1),
            dims,
            [((4 if more else 2,) + plane, f32)] * 2,
            (*state, *more),
        )
        near = lax.ppermute(near, "lon", close)
        far = lax.ppermute(far, "lon", apart)
        return near, far

    row_const = row_new = to_lat(lat_msgs, False)
    near_const, far_const = near, far = to_lon(STEPS - 1, state, sea, east, flags)

    for step in reversed(range(STEPS)):
        first = step == STEPS - 1
        outs = [((4, n, cols), f32), ((7,) + plane, f32)] + [(plane, f32)] * count
        if first:
            outs += [((n, cols), f32)] + [((n, n), bf16)] * 2 + [((rows * cols, cols), bf16)] * 2 + [(plane, f32)] * 3
            args = (*state, sea, block_inverse, coupled)
            scratch = (pltpu.VMEM((n, levels), f32), pltpu.VMEM((rows, cols, cols), f32))
        else:
            args = (*state, sea, coupled, corner, b_plane, w_high, w_low)
            scratch = ()
        proj, planes, *more = call(functools.partial(project_kernel, first), dims, outs, args, (), scratch)
        far_msgs = more[:count]
        if first:
            spike, w_high, w_low, p_high, p_low, spike_packed, corner, b_plane = more[count:]
        row_far = to_lat(far_msgs, True)
        mine, side_proj = call(
            side_kernel,
            dims,
            [((8,) + plane, f32), ((4,) + plane, f32)],
            (near, far, near_const, far_const, planes, corner, spike_packed, p_high, p_low),
        )
        theirs = to_depth(mine)
        if first:
            faces = {}
            for later in reversed(range(STEPS)):
                *faces[later], = call(
                    functools.partial(coef_kernel, later),
                    dims,
                    [((4, n, cols), f32), ((5, n, cols), f32)] + [((4, n, cols), f32)] * (later == step),
                    (sea, east, north, flags, near_const, far_const, spike, spike_packed),
                )
            beside = faces[step][2]
        coef, factor = faces[step][:2]
        (base,) = call(base_kernel, dims, [((4, n, cols), f32)], (proj, side_proj, near_const, far_const, coef))
        block = ((levels, levels), bf16)
        rows_out = call(
            functools.partial(rows_kernel, first),
            dims,
            [((5,) + grid, f32)] * count
            + [(plane, f32)] * count
            + ([block] * (2 * count) + [(grid, f32)] * count) * first,
            (*row_new, *row_const, *(() if first else row_block)),
            scratch=(pltpu.VMEM((4,) + grid, f32),),
        )
        if first:
            row_block = rows_out[2 * count :]
        rows_out = rows_out[: 2 * count]
        final = step == 0
        outs, extra = [((n, cols), f32)] * 4, ()
        if not final:
            outs = outs + [((5 * levels, cols), f32)] * count
            extra = (late,)
        result = call(
            functools.partial(apply_kernel, step, final),
            dims,
            outs,
            (
                coupled, proj, spike, mine, theirs, base, coef, factor, beside,
                *rows_out, *row_const, *row_new, *row_far, *extra,
            ),
            scratch=(pltpu.VMEM((count, 4) + grid, f32),)
            + ((pltpu.VMEM((4, n, cols), f32), pltpu.SemaphoreType.DMA((4 * CHUNKS,))) if final else ()),
            out_space=pltpu.HBM if final else pltpu.VMEM,
        )
        state = result[:4]
        if not final:
            row_new = to_lat(result[4:], False)
            near, far = to_lon(0, state)
    return tuple(x.reshape(levels, rows, cols) for x in state)


def solution(mesh):
    in_specs = (
        P("depth", "lat", "lon"),
        P("depth", "lat", "lon"),
        P("depth", "lat", "lon"),
        P("depth", "lat", "lon"),
        P("depth", "lat", "lon"),
        P("depth", "lat", "lon"),
        P(None, "depth", "lat", "lon"),
        P("depth", "lat", "lon"),
        P("lat", "depth", None),
        P("lat"),
    )
    out_specs = (
        P("depth", "lat", "lon"),
        P("depth", "lat", "lon"),
        P("depth", "lat", "lon"),
        P("depth", "lat", "lon"),
    )

    return jax.shard_map(on_device, mesh=mesh, in_specs=in_specs, out_specs=out_specs, check_vma=False)
```

```python
import functools

import jax
import jax.numpy as jnp
from jax import lax
from jax.experimental import pallas as pl
from jax.experimental.pallas import tpu as pltpu
from jax.sharding import PartitionSpec as P

STEPS = 2

advect_scale = 0.25
diffusion = 0.5
gravity = 0.1
pressure_scale = 1.0
viscosity = 0.1
haline = 0.8

BLOCK = 48
VMEM_BYTES = 16 * 1024 * 1024
f32 = jnp.float32
CHUNKS = 3
bf16 = jnp.bfloat16
CORNER_LANE = 16


def split(value):
    high = value.astype(bf16)
    return high, (value - high.astype(f32)).astype(bf16)


def dot(a, b, contract=((1,), (0,))):
    return lax.dot_general(a, b, (contract, ((), ())), preferred_element_type=f32)


def dot3(a, b):
    return dot(a[0], b[0]) + (dot(a[0], b[1]) + dot(a[1], b[0]))


def iota(shape, dim):
    return lax.broadcasted_iota(jnp.int32, shape, dim)


def branches(flags):
    one = jnp.where(flags >= 3, 1, 0) + jnp.where(flags >= 6, 1, 0)
    zonal = (flags - 3 * one).astype(f32) * 0.5
    return zonal, one.astype(f32) * 0.5


def lane_of(value, lane):
    return jnp.broadcast_to(value[:, lane : lane + 1], value.shape)


def level_at(k, rows):
    return pl.ds(k * rows if isinstance(k, int) else pl.multiple_of(k * rows, rows), rows)


def level(ref, k, rows):
    return ref[level_at(k, rows), :]


def turn(value, shift):
    return pltpu.roll(value, shift % value.shape[1], 1)


def each_level(levels, body, carry):
    block = min(BLOCK, levels)

    def some(b, carry):
        for i in range(block):
            carry = body(b * block + i, carry)
        return carry

    if block == levels:
        return some(0, carry)
    return lax.fori_loop(0, levels // block, some, carry)


def take_row(ref, row, levels, rows):
    if isinstance(row, int):
        return ref[pl.ds(row, levels, stride=rows), :]
    low = ref[pl.ds(0, levels, stride=rows), :]
    high = ref[pl.ds(rows - 1, levels, stride=rows), :]
    return jnp.where(row == 0, low, high)


def by_side(ids, near, far, j):
    even = ids[4] == 0
    return jnp.where(even, far[j], near[j]), jnp.where(even, near[j], far[j])


def to_pairs(ids, near, far, j, to_east, to_west):
    even = ids[4] == 0
    near[j] = jnp.where(even, to_east, to_west)
    far[j] = jnp.where(even, to_west, to_east)


def row_choices(pair, rows, lat):
    return [jnp.where(lat == 0, rows - 1, 0)] if pair else [0, rows - 1]


def block_shape(levels):
    return levels // 2


def fetch_kernel(dims, ids, *refs):
    levels, rows, cols, half, pair = dims
    coup, inverse, sources, (nn_late, coupled), rest = refs[0], refs[1], refs[2:9], refs[9:11], refs[11:]
    count = 1 if pair else 2
    lat_msgs, copies, (coup_here, blocks, sems) = rest[:count], rest[count : count + 7], rest[count + 7 :]
    moves = [pltpu.make_async_copy(a, b, sems.at[i]) for i, (a, b) in enumerate(zip(sources, copies))]
    moves.append(pltpu.make_async_copy(coup, coup_here, sems.at[7]))
    choices = row_choices(pair, rows, ids[0])
    for which, row in enumerate(choices):
        moves.append(pltpu.make_async_copy(inverse.at[row], blocks.at[which], sems.at[8 + which]))
    for move in moves:
        move.start()
    t, s, u, v, sea, north, flags = copies
    for move in moves:
        move.wait()
    spot = iota((rows, rows), 0) == iota((rows, rows), 1)
    value = jnp.sum(jnp.where(spot, coup_here[...], 0.0), axis=1, keepdims=True)
    coupled[...] = jnp.broadcast_to(value, (rows, cols))
    for which, row in enumerate(choices):
        msg = lat_msgs[which]

        def put(j, value):
            msg[pl.ds(j * levels, levels), :] = value

        for j, x in enumerate((t, s, u, v)):
            put(j, take_row(x, row, levels, rows))
        wet = take_row(sea, row, levels, rows).astype(f32)
        speed = take_row(north, row, levels, rows)
        put(4, wet)
        for step in (1, 0):
            _, merid = branches(take_row(flags.at[step], row, levels, rows))
            value = wet * (speed * merid - diffusion)
            if step:
                put(5, value)
            elif pair or row:
                nn_late[...] = value
        block = blocks[which]
        size = block_shape(levels)
        last = pl.ds(6 * levels, size)
        msg[last, :] = jnp.zeros((size, cols), f32)
        msg[last, pl.ds(0, levels)] = block[:size]
        msg[last, pl.ds(half, levels)] = block[size:]


def edges_kernel(first, dims, ids, t, s, u, v, *refs):
    levels, rows, cols, half, _ = dims
    lane = iota((rows, cols), 1)
    sea, east, flags, near, far = refs if first else (None, None, None, *refs)
    to_pairs(ids, near, far, 0, *edge_columns(levels, rows, t, s, 2))
    to_pairs(ids, near, far, 1, *edge_columns(levels, rows, u, v, 2))
    if first:
        wet, first_wet = edge_columns(levels, rows, sea, east, 2)
        flag, _ = edge_columns(levels, rows, flags.at[1], flags.at[0], 1)
        speed = turn(wet, half)
        zonal = branches(jnp.round(flag).astype(jnp.int32))[0]
        nexts = [wet * (speed * z - diffusion) for z in (zonal, turn(zonal, half))]
        to_pairs(ids, near, far, 2, jnp.where(lane < half, wet, turn(nexts[0], half)), first_wet)
        to_pairs(ids, near, far, 3, nexts[1], nexts[1])


def edge_columns(levels, rows, x, y, pieces):
    cols = x.shape[1]
    half = cols // 2
    source, target = iota((2 * cols, 2 * cols), 0), iota((2 * cols, 2 * cols), 1)
    column = jnp.where(target < cols, cols - 1, 0) + jnp.where(target % cols < half, 0, cols)
    spread = (source == column).astype(bf16)
    both = jnp.concatenate([x[...].astype(f32), y[...].astype(f32)], axis=1)
    high, low = split(both)
    wide = dot(high, spread)
    if pieces == 2:
        wide = wide + dot(low, spread)
    place = iota((rows, 2 * cols), 1) % half
    out = jnp.zeros((rows, 2 * cols), f32)
    for k in range(levels):
        out = jnp.where(place == k, wide[k * rows : (k + 1) * rows], out)
    return out[:, :cols], out[:, cols:]


def insert(lane, value, west_in, east_in):
    cols = value.shape[1]
    return (
        jnp.where(lane == 0, west_in, turn(value, 1)),
        jnp.where(lane == cols - 1, east_in, turn(value, cols - 1)),
    )


def inner(row, value):
    rows = value.shape[0]
    return (
        jnp.where(row == 0, 0.0, pltpu.roll(value, 1, 0)),
        jnp.where(row == rows - 1, 0.0, pltpu.roll(value, rows - 1, 0)),
    )


def coef_kernel(step, dims, ids, sea, east, north, flags, near, far, spike, spike_packed, out, factor, *beside):
    levels, rows, cols, half, _ = dims
    lane, row = iota((rows, cols), 1), iota((rows, cols), 0)
    west_const, sea_side = by_side(ids, near, far, 2)
    next_side = west_const if step else by_side(ids, near, far, 3)[0]
    spk = spike_packed[...]
    spike_west = jnp.where(lane < half, west_const, 0.0) * spk
    spike_east = jnp.where(lane < half, sea_side, 0.0) * spk

    def one(k, carry):
        wet = level(sea, k, rows).astype(f32)
        part = advect_scale * wet
        speed_e, speed_n = level(east, k, rows), level(north, k, rows)
        sea_east = jnp.where(lane == cols - 1, turn(sea_side, cols - 1 - k), turn(wet, cols - 1))
        sea_north = jnp.where(row == rows - 1, 1.0, pltpu.roll(wet, rows - 1, 0))
        here = level_at(k, rows)
        mid = level(spike, k, rows)
        west, east_ = insert(lane, mid, turn(spike_west, cols - k), turn(spike_east, cols - 1 - k))
        south, north_ = inner(row, mid)
        for ref in beside:
            for j, value in enumerate((east_, west, north_, south)):
                ref[j, here, :] = value
        zonal, merid = branches(level(flags.at[step], k, rows))
        speed_z, speed_m = speed_e * zonal, speed_n * merid
        east_own = part * (speed_e - speed_z + diffusion) * sea_east
        next_west = jnp.where(
            lane == 0, turn(next_side, 2 * cols - step * half - k), turn(wet * (speed_z - diffusion), 1)
        )
        west_own = part * next_west
        north_own = part * (speed_n - speed_m + diffusion) * sea_north
        next_south = jnp.where(row == 0, 1.0, pltpu.roll(wet * (speed_m - diffusion), 1, 0))
        south_own = part * next_south
        for j, value in enumerate((east_own, west_own, north_own, south_own)):
            out[j, here, :] = value
        inside_n = jnp.where(row == rows - 1, 0.0, north_own)
        inside_s = jnp.where(row == 0, 0.0, south_own)
        factor[0, here, :] = mid * (1.0 + ((west_own - east_own) + (inside_s - inside_n)))
        factor[1, here, :] = east_own * east_
        factor[2, here, :] = -west_own * west
        factor[3, here, :] = inside_n * north_
        factor[4, here, :] = -inside_s * south
        return carry

    each_level(levels, one, ())


def coriolis_of(dims, ids):
    _, rows, cols, _, _ = dims
    index = (ids[0] * rows + iota((rows, cols), 0)).astype(f32)
    return 0.2 + 0.6 * (index + 0.5) / (rows * ids[3])


def base_kernel(dims, ids, proj, side_proj, near, far, coef, out):
    levels, rows, cols, half, _ = dims
    lane, row = iota((rows, cols), 1), iota((rows, cols), 0)
    parts = []
    for p in range(2):
        line = []
        for side, const in enumerate(by_side(ids, near, far, 2)):
            wet = jnp.where(lane < half, const, turn(const, half))
            line.append(wet * side_proj[2 * side + p])
        parts.append(jnp.concatenate(line, axis=1))
    source, target = iota((2 * cols, 2 * cols), 0), iota((2 * cols, 2 * cols), 1)
    pick = target % cols
    wanted = pick // 2 + jnp.where(target < cols, 0, half) + jnp.where(pick % 2 == 1, 0, cols)
    spread = (source == wanted).astype(bf16)
    high, low = split(jnp.concatenate(parts, axis=0))
    mixed = dot(high, spread) + dot(low, spread)
    halo = [mixed[p * rows : (p + 1) * rows, i * cols : (i + 1) * cols] for p in range(2) for i in range(2)]
    coriolis = coriolis_of(dims, ids)
    push = -0.5 * pressure_scale * gravity
    top, bottom = row == rows - 1, row == 0

    def one(j, below):
        k = levels - 1 - j
        here = level_at(k, rows)
        east_own, west_own = coef[0, here, :], coef[1, here, :]
        north_own = jnp.where(top, 0.0, coef[2, here, :])
        south_own = jnp.where(bottom, 0.0, coef[3, here, :])
        mids, around = [], []
        for f in range(4):
            w = proj[f, here, :]
            mids.append(w)
            side = turn(halo[f], 2 * cols - 2 * k - 1)
            around.append((*insert(lane, w, side, side), *inner(row, w)))
        below = below + ((around[2][0] - around[2][1]) + (around[3][2] - around[3][3]))
        buoyancy = push * below
        for f in range(2):
            w, (ww, we, ws, wn) = mids[f], around[f]
            q = w + ((east_own * (we - w) + west_own * (w - ww)) + (north_own * (wn - w) + south_own * (w - ws)))
            out[f, here, :] = q + buoyancy if f == 0 else q - haline * buoyancy
        for f in (2, 3):
            w, (ww, we, ws, wn) = mids[f], around[f]
            spin = coriolis * mids[5 - f]
            centre = (1.0 - 4.0 * viscosity) * w
            centre = centre - spin if f == 2 else centre + spin
            out[f, here, :] = centre + viscosity * ((we + ww) + (wn + ws))
        return below

    each_level(levels, one, jnp.zeros((rows, cols), f32))


def plane_of(ref, j, levels):
    return ref[pl.ds(j * levels, levels), :]


def rows_kernel(first, dims, ids, *refs):
    levels, _, cols, half, pair = dims
    count = 1 if pair else 2
    new, const, *refs = (refs[i * count : (i + 1) * count] for i in range(len(refs) // count + 1))
    turned_high, turned_low, thin = refs[2:5] if first else refs[:3]
    outs, lines = refs[:2] if first else refs[3:5]
    (scratch,) = refs[5]
    at_edge = pl.ds(ids[2], 1)
    for h in range(count):
        if first:
            size = block_shape(levels)
            packed = const[h][pl.ds(6 * levels, size), :]
            square = jnp.concatenate([packed[:, :levels], turn(packed, half)[:, :levels]], axis=0)
            pick = (iota((levels, cols), 0) == ids[2]).astype(bf16)
            turned = split(square.T)
            turned_high[h][...], turned_low[h][...] = turned
            thin[h][...] = dot(turned[0], pick) + dot(turned[1], pick)
        turned = (turned_high[h][...], turned_low[h][...])
        both = dot3(turned, split(jnp.concatenate([plane_of(new[h], f, levels) for f in range(4)], axis=1)))
        for f in range(4):
            scratch[f] = both[:, f * cols : (f + 1) * cols]
        lines[h][...] = jnp.zeros_like(lines[h])
        wet = plane_of(const[h], 4, levels)
        for j in range(4):
            lines[h][pl.ds(j, 1), :] = scratch[j, at_edge, :]
            outs[h][j] = wet * scratch[j]
        lines[h][pl.ds(4, 1), :] = thin[h][at_edge, :]
        outs[h][4] = wet * thin[h][...]


def project_kernel(setup, dims, ids, t, s, u, v, sea, *rest):
    levels, rows, cols, half, pair = dims
    if setup:
        inverse, coupled, proj, planes, *rest = rest
        lat_out, (spike, w_high, w_low, p_high, p_low, spike_packed, corner, b_plane, cells, wide) = rest[:-10], rest[-10:]
        n = levels * rows
        for y in range(rows):
            cells[pl.ds(y, levels, stride=rows), :] = inverse[y]
        pieces = split(cells[...])
        pick = (iota((n, levels), 0) // rows == iota((n, levels), 1)).astype(bf16)
        same = (iota((n, n), 0) % rows) == (iota((n, n), 1) % rows)
        for piece, out in zip(pieces, (w_high, w_low)):
            full = dot(pick, piece, ((1,), (1,)))
            out[...] = jnp.where(same, full, 0.0).astype(bf16)
        wide[...] = jnp.zeros_like(wide)
        for y in range(rows):
            wide[y, pl.ds(0, levels), pl.ds(0, levels)] = inverse[y]
            wide[y, pl.ds(half, levels), pl.ds(half, levels)] = inverse[y]
        high, low = split(wide[...].reshape(rows * cols, cols))
        p_high[...] = high
        p_low[...] = low
        spike_packed[...] = jnp.zeros_like(spike_packed)
        for y in range(rows):
            line = inverse[y, pl.ds(ids[2], 1), :]
            spike_packed[pl.ds(y, 1), pl.ds(0, levels)] = line
            spike_packed[pl.ds(y, 1), pl.ds(half, levels)] = line
    else:
        coupled, corner, b_plane, w_high, w_low, proj, planes, *lat_out = rest
    w = (w_high[...], w_low[...])
    for f, (x, y) in enumerate(((t, s), (u, v))):
        both = dot3(w, split(jnp.concatenate([x[...], y[...]], axis=1)))
        proj[2 * f] = both[:, :cols]
        proj[2 * f + 1] = both[:, cols:]
    edge = pl.ds(pl.multiple_of(ids[2] * rows, rows), rows)
    zero = jnp.zeros((rows, cols), f32)
    if setup:
        n = levels * rows
        pick = (iota((n, cols), 0) // rows == ids[2]).astype(bf16)
        spike[...] = dot(w[0], pick) + dot(w[1], pick)
        corner[...] = spike[edge, :]
    for f in range(4):
        planes[f] = proj[f, edge, :]

    def one(k, sums):
        here = level_at(k, rows)
        wet = sea[here, :].astype(f32)
        values = [wet * proj[f, here, :] for f in range(4)]
        for f in range(4):
            proj[f, here, :] = values[f]
        sums = [sums[0] + values[2], sums[1] + values[3], *sums[2:]]
        if setup:
            value = wet * spike[here, :]
            spike[here, :] = value
            sums[2] = sums[2] + value
        return tuple(sums)

    sums = each_level(levels, one, (zero,) * (3 if setup else 2))
    if setup:
        b_plane[...] = sums[2]
    sums = [sums[0], sums[1], b_plane[...]]
    for j in range(3):
        planes[4 + j] = sums[j]
    lines = [planes[f] for f in range(4)] + [sums[1], sums[2], corner[...], coupled[...]]
    for which, row in enumerate(row_choices(pair, rows, ids[0])):
        for j, value in enumerate(lines):
            if pair:
                line = jnp.where(row == 0, value[0:1], value[rows - 1 : rows])
            else:
                line = value[row : row + 1]
            lat_out[which][pl.ds(j, 1), :] = line


def side_kernel(dims, ids, near, far, near_const, far_const, planes, corner, spike_packed, p_high, p_low, msg, proj):
    _, rows, cols, half, _ = dims
    lane = iota((rows, cols), 1)
    row = iota((rows, cols), 0)
    (west0, east0), (west1, east1) = (by_side(ids, near, far, j) for j in range(2))
    packed = (west0, west1, east0, east1)
    chunks = []
    for y in range(rows):
        chunks.append(jnp.concatenate([jnp.where(row == y, x, 0.0) for x in packed], axis=0))
    lhs = jnp.concatenate(chunks, axis=1)
    out = dot3(split(lhs), (p_high[...], p_low[...]))
    for j in range(4):
        proj[j] = out[j * rows : (j + 1) * rows]
    for j in range(7):
        msg[j] = planes[j]
    edge = ids[2]
    misc = jnp.zeros((rows, cols), f32)
    spk = spike_packed[...]
    for side, wet in enumerate(by_side(ids, near_const, far_const, 2)):
        wet = jnp.where(lane < half, wet, 0.0)
        for p in range(2):
            value = out[(2 * side + p) * rows : (2 * side + p + 1) * rows]
            for i in range(2):
                column = jnp.sum(jnp.where(lane == edge + i * half, value, 0.0), axis=1, keepdims=True)
                misc = jnp.where(lane == side * 8 + 2 * p + i, column, misc)
            if p == 1:
                column = jnp.sum(wet * value, axis=1, keepdims=True)
                misc = jnp.where(lane == side * 8 + 4, column, misc)
        column = jnp.sum(wet * spk, axis=1, keepdims=True)
        misc = jnp.where(lane == side * 8 + 5, column, misc)
    msg[7] = jnp.where(lane == CORNER_LANE, corner[...], misc)


def apply_kernel(step, final, dims, ids, coupled, proj, spike, mine, theirs, base, coef, factor, beside, *rest):
    levels, rows, cols, _, pair = dims
    count = 1 if pair else 2
    row_proj, row_line, row_const, row_late, row_far = (rest[i * count : (i + 1) * count] for i in range(5))
    rest = rest[5 * count :]
    if final:
        outs, (extras, work, sems) = rest[:4], rest[4:]
    else:
        late_out, outs, lat_msgs, extras = rest[0], rest[1:5], rest[5:-1], rest[-1]
        work = outs
    lat, depth, parts = ids[0], ids[1], ids[3]
    lane = iota((rows, cols), 1)
    row = iota((rows, cols), 0)
    has_north = jnp.where(lat < parts - 1, 1.0, 0.0)
    has_south = jnp.where(lat > 0, 1.0, 0.0)

    c = coupled[...]
    own_corner = lane_of(mine[7], CORNER_LANE)
    other_corner = lane_of(theirs[7], CORNER_LANE)
    scaled = c / (1.0 - c * c * own_corner * other_corner)
    co, cm = c * other_corner, c * own_corner
    carried = [scaled * (theirs[f] + co * mine[f]) for f in range(4)]
    misc = theirs[7]
    carried_side = scaled * (misc + co * mine[7])
    theirs_side = scaled * (mine[7] + cm * misc)

    row_solved, row_sums = [], []
    for h in range(count):
        far, line = row_far[h], row_line[h]
        c_row, other, own = far[7:8, :], far[6:7, :], line[4:5, :]
        scaled_row = c_row / (1.0 - c_row * c_row * own * other)
        joined = [scaled_row * (far[f : f + 1, :] + c_row * other * line[f : f + 1, :]) for f in range(4)]
        row_solved.append([row_proj[h][f] + row_proj[h][4] * joined[f] for f in range(4)])
        theirs_v = scaled_row * (line[3:4, :] + c_row * own * far[3:4, :])
        row_sums.append(far[4:5, :] + far[5:6, :] * theirs_v)

    sum_u = theirs[4] + theirs[6] * (scaled * (mine[2] + cm * theirs[2]))
    sum_v = theirs[5] + theirs[6] * (scaled * (mine[3] + cm * theirs[3]))
    side_u = [lane_of(misc, q * 8 + 4) + lane_of(misc, q * 8 + 5) * lane_of(theirs_side, q * 8 + 2) for q in (0, 1)]
    west_u, east_u = insert(lane, sum_u, *side_u)
    south_v = jnp.where(row == 0, row_sums[-1] * has_south, pltpu.roll(sum_v, 1, 0))
    north_v = jnp.where(row == rows - 1, row_sums[0] * has_north, pltpu.roll(sum_v, rows - 1, 0))
    upper = jnp.where(depth == 0, 1.0, 0.0)
    deeper = (west_u - east_u + south_v - north_v) * upper

    coriolis = coriolis_of(dims, ids)
    push = -0.5 * pressure_scale * gravity
    around = []
    for f in range(4):
        west, east = insert(lane, carried[f], lane_of(carried_side, f), lane_of(carried_side, 8 + f))
        south, north = inner(row, carried[f])
        around.append((east, west, north, south))
    plain = 1.0 - 4.0 * viscosity
    mids = (plain * carried[2] - coriolis * carried[3], plain * carried[3] + coriolis * carried[2])

    later = (iota((levels, levels), 1) >= iota((levels, levels), 0)).astype(bf16)
    for h in range(count):
        if pair:
            at, sign = jnp.where(lat == 0, rows - 1, 0), jnp.where(lat == 0, -1.0, 1.0)
        else:
            at, sign = ((rows - 1, -1.0), (0, 1.0))[h]
        take = lambda ref: take_row(ref, at, levels, rows)
        pick = lambda plane: (
            jnp.where(lat == 0, plane[rows - 1 : rows], plane[0:1]) if pair else plane[at : at + 1]
        )
        beyond = row_solved[h]
        wet = plane_of(row_const[h], 4, levels)
        late = plane_of(row_const[h], 5, levels) if step else plane_of(row_late[h], 4, levels)
        if pair:
            own = jnp.where(
                lat == 0,
                coef[2, pl.ds(rows - 1, levels, stride=rows), :],
                coef[3, pl.ds(0, levels, stride=rows), :],
            )
            gate = own * jnp.where(lat == 0, wet, -late)
        else:
            gate = coef[2 + h, pl.ds(at, levels, stride=rows), :] * (-late if h else wet)
        high, low = split(push * sign * beyond[3])
        rise = dot(later, high) + dot(later, low)
        spk = take(spike)
        for f in range(2):
            mid = take(proj.at[f]) + spk * pick(carried[f])
            flow = gate * (beyond[f] - mid)
            extras[h, f] = flow + rise if f == 0 else flow - haline * rise
        for f in (2, 3):
            extras[h, f] = viscosity * beyond[f]

    def one(k, below):
        here = level_at(k, rows)
        sides = [beside[j, here, :] for j in range(4)]
        moved = [[side * plane for side, plane in zip(sides, around[f])] for f in (2, 3)]
        below = below + ((moved[0][1] - moved[0][0]) + (moved[1][3] - moved[1][2]))
        buoyancy = push * below
        factors = [factor[j, here, :] for j in range(5)]
        for f in range(2):
            q = base[f, here, :] + factors[0] * carried[f]
            q = q + (
                (factors[1] * around[f][0] + factors[2] * around[f][1])
                + (factors[3] * around[f][2] + factors[4] * around[f][3])
            )
            place(f)[here, :] = q + buoyancy if f == 0 else q - haline * buoyancy
        spk = spike[here, :]
        for i in range(2):
            total = (moved[i][0] + moved[i][1]) + (moved[i][2] + moved[i][3])
            place(2 + i)[here, :] = base[2 + i, here, :] + (spk * mids[i] + viscosity * total)
        return below

    place = (lambda f: work.at[f]) if final else (lambda f: outs[f])
    below, moves = deeper, []
    parts_of = CHUNKS if final else 1
    size = levels // parts_of
    for part in reversed(range(parts_of)):
        for k in reversed(range(part * size, (part + 1) * size)):
            below = one(k, below)
        for h in range(count):
            ends = ((rows - 1, has_north), (0, has_south))
            for spot, mask in ends if pair else ends[h : h + 1]:
                there = pl.ds(part * size * rows + spot, size, stride=rows)
                for f in range(4):
                    target = place(f)
                    target[there, :] = target[there, :] + mask * extras[h, f, pl.ds(part * size, size), :]
        if final:
            there = pl.ds(part * size * rows, size * rows)
            for f in range(4):
                move = pltpu.make_async_copy(work.at[f, there], outs[f].at[there], sems.at[4 * part + f])
                move.start(priority=f % 2)
                moves.append(move)
    for move in moves:
        move.wait()

    if not final:
        for which, at in enumerate(row_choices(pair, rows, lat)):
            for f in range(4):
                lat_msgs[which][pl.ds(f * levels, levels), :] = take_row(outs[f], at, levels, rows)
            lat_msgs[which][pl.ds(4 * levels, levels), :] = late_out[...]


def places(levels):
    lat, depth, lon = (lax.axis_index(a) for a in ("lat", "depth", "lon"))
    return lat, depth, (levels - 1) * (1 - depth), lax.axis_size("lat"), lax.rem(lon, 2)


def call(kernel, dims, outs, args, smem=(), scratch=(), hbm=(), out_space=pltpu.VMEM):
    spaces = [pltpu.SMEM if i in smem else pltpu.HBM if i in hbm else pltpu.VMEM for i in range(len(args))]

    def run(*refs):
        kernel(dims, places(dims[0]), *refs)

    return pl.pallas_call(
        run,
        out_shape=[jax.ShapeDtypeStruct(shape, kind) for shape, kind in outs],
        in_specs=[pl.BlockSpec(memory_space=space) for space in spaces],
        out_specs=[pl.BlockSpec(memory_space=out_space)] * len(outs),
        scratch_shapes=list(scratch),
        compiler_params=pltpu.CompilerParams(vmem_limit_bytes=VMEM_BYTES),
    )(*args)


def on_device(
    adj_temp,
    adj_salt,
    adj_zonal,
    adj_merid,
    east_speed,
    north_speed,
    branch_flags,
    sea_mask,
    block_inverse,
    coupling,
):
    levels, rows, cols = adj_temp.shape
    half = cols // 2
    lons, lats, depths = (lax.axis_size(a) for a in ("lon", "lat", "depth"))
    pair = lats == 2
    dims = (levels, rows, cols, half, pair)
    count = 1 if pair else 2
    n = levels * rows
    flat = lambda x: x.reshape(x.shape[:-3] + (n, cols))
    sea, east, north, flags = flat(sea_mask), flat(east_speed), flat(north_speed), flat(branch_flags)
    state = [flat(x) for x in (adj_temp, adj_salt, adj_zonal, adj_merid)]
    plane = (rows, cols)
    grid = (levels, cols)

    assert lons % 2 == 0
    close = [(i, i ^ 1) for i in range(lons)]
    apart = [(i, (i + 1 if i % 2 else i - 1) % lons) for i in range(lons)]
    up = [(i, i + 1) for i in range(lats - 1)]
    down = [(b, a) for a, b in up]

    def to_lat(msgs, flip):
        routes = [up + down] if pair else [down, up]
        if not flip:
            return [lax.ppermute(m, "lat", r) for m, r in zip(msgs, routes)]
        both = [
            [(a * depths + d, b * depths + (depths - 1 - d)) for a, b in r for d in range(depths)] for r in routes
        ]
        return [lax.ppermute(m, ("lat", "depth"), r) for m, r in zip(msgs, both)]

    def to_depth(msg):
        return lax.ppermute(msg, "depth", [(d, depths - 1 - d) for d in range(depths)])

    in_place = lambda x: pltpu.with_memory_space_constraint(x, pltpu.HBM)
    sources = tuple(in_place(x) for x in (*state, sea, north, flags))
    full = 6 * levels + block_shape(levels)
    late, coupled, *rest = call(
        fetch_kernel,
        dims,
        [(grid, f32), (plane, f32)]
        + [((full, cols), f32)] * count
        + [(x.shape, x.dtype) for x in sources],
        (in_place(coupling.reshape(1, rows)), in_place(block_inverse), *sources),
        (),
        (
            pltpu.VMEM((1, rows), f32),
            pltpu.VMEM((count, levels, levels), f32),
            pltpu.SemaphoreType.DMA((8 + count,)),
        ),
        range(9),
    )
    lat_msgs, rest = rest[:count], rest[count:]
    state, (sea, north, flags) = rest[:4], rest[4:]

    def to_lon(step, state, *more):
        near, far = call(
            functools.partial(edges_kernel, step == STEPS - 1),
            dims,
            [((4 if more else 2,) + plane, f32)] * 2,
            (*state, *more),
        )
        near = lax.ppermute(near, "lon", close)
        far = lax.ppermute(far, "lon", apart)
        return near, far

    row_const = row_new = to_lat(lat_msgs, False)
    near_const, far_const = near, far = to_lon(STEPS - 1, state, sea, east, flags)

    for step in reversed(range(STEPS)):
        first = step == STEPS - 1
        outs = [((4, n, cols), f32), ((7,) + plane, f32)] + [(plane, f32)] * count
        if first:
            outs += [((n, cols), f32)] + [((n, n), bf16)] * 2 + [((rows * cols, cols), bf16)] * 2 + [(plane, f32)] * 3
            args = (*state, sea, block_inverse, coupled)
            scratch = (pltpu.VMEM((n, levels), f32), pltpu.VMEM((rows, cols, cols), f32))
        else:
            args = (*state, sea, coupled, corner, b_plane, w_high, w_low)
            scratch = ()
        proj, planes, *more = call(functools.partial(project_kernel, first), dims, outs, args, (), scratch)
        far_msgs = more[:count]
        if first:
            spike, w_high, w_low, p_high, p_low, spike_packed, corner, b_plane = more[count:]
        row_far = to_lat(far_msgs, True)
        mine, side_proj = call(
            side_kernel,
            dims,
            [((8,) + plane, f32), ((4,) + plane, f32)],
            (near, far, near_const, far_const, planes, corner, spike_packed, p_high, p_low),
        )
        theirs = to_depth(mine)
        if first:
            faces = {}
            for later in reversed(range(STEPS)):
                *faces[later], = call(
                    functools.partial(coef_kernel, later),
                    dims,
                    [((4, n, cols), f32), ((5, n, cols), f32)] + [((4, n, cols), f32)] * (later == step),
                    (sea, east, north, flags, near_const, far_const, spike, spike_packed),
                )
            beside = faces[step][2]
        coef, factor = faces[step][:2]
        (base,) = call(base_kernel, dims, [((4, n, cols), f32)], (proj, side_proj, near_const, far_const, coef))
        block = ((levels, levels), bf16)
        rows_out = call(
            functools.partial(rows_kernel, first),
            dims,
            [((5,) + grid, f32)] * count
            + [(plane, f32)] * count
            + ([block] * (2 * count) + [(grid, f32)] * count) * first,
            (*row_new, *row_const, *(() if first else row_block)),
            scratch=(pltpu.VMEM((4,) + grid, f32),),
        )
        if first:
            row_block = rows_out[2 * count :]
        rows_out = rows_out[: 2 * count]
        final = step == 0
        outs, extra = [((n, cols), f32)] * 4, ()
        if not final:
            outs = outs + [((5 * levels, cols), f32)] * count
            extra = (late,)
        result = call(
            functools.partial(apply_kernel, step, final),
            dims,
            outs,
            (
                coupled, proj, spike, mine, theirs, base, coef, factor, beside,
                *rows_out, *row_const, *row_new, *row_far, *extra,
            ),
            scratch=(pltpu.VMEM((count, 4) + grid, f32),)
            + ((pltpu.VMEM((4, n, cols), f32), pltpu.SemaphoreType.DMA((4 * CHUNKS,))) if final else ()),
            out_space=pltpu.HBM if final else pltpu.VMEM,
        )
        state = result[:4]
        if not final:
            row_new = to_lat(result[4:], False)
            near, far = to_lon(0, state)
    return tuple(x.reshape(levels, rows, cols) for x in state)


def solution(mesh):
    in_specs = (
        P("depth", "lat", "lon"),
        P("depth", "lat", "lon"),
        P("depth", "lat", "lon"),
        P("depth", "lat", "lon"),
        P("depth", "lat", "lon"),
        P("depth", "lat", "lon"),
        P(None, "depth", "lat", "lon"),
        P("depth", "lat", "lon"),
        P("lat", "depth", None),
        P("lat"),
    )
    out_specs = (
        P("depth", "lat", "lon"),
        P("depth", "lat", "lon"),
        P("depth", "lat", "lon"),
        P("depth", "lat", "lon"),
    )

    return jax.shard_map(on_device, mesh=mesh, in_specs=in_specs, out_specs=out_specs, check_vma=False)
```
